32 devices in a mesh: gx: 4 (over x, core), gy: 8 (over z, y).
Axes of the slice: x: 2, y: 2, z: 4, core: 2. Of those that a mesh axis runs over, the one named last changes fastest.
Arguments:
- increment: float32 [8, 2048, 1024], P(None, 'gx', 'gy'), may hold values from -6 to 6
- deviation: float32 [8, 2048, 1024], P(None, 'gx', 'gy'), may hold values from 0.5 to 2
- land_sea: int32 [8, 2048, 1024], P(None, 'gx', 'gy'), may hold values 0 or 1
- filter_steps: int32 [8], replicated, may hold values from 1 to 2, as said below
- zonal_rate: float32 [8], replicated, may hold values from 0.0009765625 to 0.03
- meridional_rate: float32 [8], replicated, may hold values from 0.001953125 to 0.03
Outputs:
- covaried: float32 [8, 2048, 1024], P(None, 'gx', 'gy')
The draws below stay inside these ranges and needn't reach their ends.
Inputs may be any that keep to these rules, and one draw needn't show every extreme that they name: `filter_steps`: some level has 2 repetitions and some level has 1.
All inputs are finite; a program needn't handle non-finite values. No bound on the sum of `land_sea` on one device may be relied on, other than what follows from the above.
Results may differ from the reference program's by a relative error of at most 0.0003.
Values sent between devices are 32-bit elements; how exact they have to be, the bound alone decides.
A program may use at most 128 MiB of HBM per device.

```python
import math
import jax
import jax.numpy as jnp
from jax import lax

L = 8
MAXSTEPS = 2
NX = 2048
NY = 1024


def draw_filter_steps(key, part):
    values = jax.random.randint(jax.random.fold_in(key, 11), (L,), 1, MAXSTEPS + 1)
    shuffled = jax.random.permutation(jax.random.fold_in(key, 12), L)
    values = values.at[shuffled[0]].set(MAXSTEPS)
    values = values.at[shuffled[1]].set(1)
    return values.astype(jnp.int32)


def place_ends(drawn, own_key, least, largest):
    longest = drawn.shape.index(max(drawn.shape))
    spots = []
    for shift in (0, 1):
        where = [jax.random.randint(jax.random.fold_in(own_key, axis), (), 0, length) for axis, length in enumerate(drawn.shape)]
        where[longest] = (where[longest] + shift) % drawn.shape[longest]
        spots.append(tuple(where))
    return drawn.at[spots[0]].set(least).at[spots[1]].set(largest)


def level_of(key, extent, shards, low, largest):
    factor_of, own = 1.0, jax.random.fold_in(key, 6)
    for axis_at, blocks in shards:
        steps = jnp.exp(jax.random.uniform(jax.random.fold_in(own, axis_at), (blocks,), jnp.float32, low / len(shards), largest / len(shards)))
        factor_of = factor_of * jnp.repeat(steps, extent[axis_at] // blocks).reshape([-1 if axis == axis_at else 1 for axis in range(len(extent))])
    return factor_of


def gaussian(key, dims, spread, limit, cuts=(), dtype=jnp.bfloat16):
    array = jax.random.normal(key, dims, jnp.float32) * spread
    if len(cuts) > 0:
        array = level_of(key, dims, cuts, -0.22, 0.18) * array
    return jnp.clip(array, min=-limit, max=limit).astype(dtype)


def setup_inputs(seed: int = 0) -> dict:
    streams_of = jax.random.split(jax.random.key(seed), 7)
    increment = gaussian(streams_of[0], (L, NX, NY), 1.0, 6.0, ((1, 4), (2, 8)), jnp.float32)
    deviation = jnp.clip(jnp.exp(math.log(2.0) - 1.3862944 * jax.random.uniform(streams_of[1], (L, NX, NY), jnp.float32) ** level_of(streams_of[1], (L, NX, NY), ((1, 4), (2, 8)), -0.2, 0.2)), 0.5, 2.0)
    land_sea = place_ends((jax.random.randint(streams_of[2], (L, NX, NY), 0, 4) < 3).astype(jnp.int32), jax.random.fold_in(streams_of[2], 1), 0, 1)
    filter_steps = draw_filter_steps(jax.random.fold_in(streams_of[6], 71), 0)
    zonal_rate = jnp.clip(jnp.exp(jax.random.uniform(streams_of[4], (L,), jnp.float32, math.log(0.0009765625), math.log(0.03))), 0.0009765625, 0.03)
    meridional_rate = jnp.clip(jnp.exp(jax.random.uniform(streams_of[5], (L,), jnp.float32, math.log(0.001953125), math.log(0.03))), 0.001953125, 0.03)
    return dict(increment=increment, deviation=deviation, land_sea=land_sea, filter_steps=filter_steps, zonal_rate=zonal_rate, meridional_rate=meridional_rate)


gain_base = 3.0 ** 0.125


def section_gain(decay_rate, filter_steps):
    fading = -jnp.expm1(-decay_rate)
    return gain_base * fading ** (1.0 - 1.0 / (16.0 * filter_steps.astype(jnp.float32)))


def recursive_pass(field, decay_rate, section_weight, direction, backward):
    ordered = jnp.moveaxis(field, direction, 0)
    if backward:
        ordered = ordered[::-1]
    factor = jnp.exp(-decay_rate)[:, None]
    weight = section_weight[:, None]

    def advance(carried, column):
        section_one = factor * carried[0] + weight * column
        section_two = factor * carried[1] + weight * section_one
        section_three = factor * carried[2] + weight * section_two
        section_four = factor * carried[3] + weight * section_three
        return (section_one, section_two, section_three, section_four), section_four

    empty_state = jnp.zeros(ordered.shape[1:], jnp.float32)
    _, result = lax.scan(advance, (empty_state, empty_state, empty_state, empty_state), ordered)
    if backward:
        result = result[::-1]
    return jnp.moveaxis(result, 0, direction)


def reference(increment, deviation, land_sea, filter_steps, zonal_rate, meridional_rate):
    wetness = land_sea.astype(jnp.float32)
    field = deviation * wetness * increment
    for repeat in range(MAXSTEPS):
        active = (filter_steps > repeat)[:, None, None]
        current = field
        for direction, rates in ((1, zonal_rate), (2, meridional_rate)):
            weights = section_gain(rates, filter_steps)
            current = wetness * recursive_pass(current, rates, weights, direction, False)
            current = wetness * recursive_pass(current, rates, weights, direction, True)
        field = jnp.where(active, current, field)
    return deviation * field
```

```python
import functools

import jax
import jax.numpy as jnp
from jax import lax
from jax.experimental import pallas as pl
from jax.experimental.pallas import tpu as pltpu
from jax.sharding import PartitionSpec as P

SIDE = 128
PAIR = 2
MAXSTEPS = 2
gain_base = 3.0**0.125
MESH = pl.DeviceIdType.MESH
f32, bf16 = jnp.float32, jnp.bfloat16


def section_gain(decay_rate, filter_steps):
    fading = -jnp.expm1(-decay_rate)
    return gain_base * fading ** (1.0 - 1.0 / (16.0 * filter_steps.astype(f32)))


def binomials(count):
    return (
        jnp.ones_like(count),
        count,
        count * (count + 1.0) / 2.0,
        count * (count + 1.0) * (count + 2.0) / 6.0,
    )


def split(value):
    high = value.astype(bf16)
    return high, (value - high.astype(f32)).astype(bf16)


def three(state):
    high = state.astype(bf16).astype(f32)
    return jnp.concatenate([high, state - high, high, jnp.zeros_like(high)], 0).astype(bf16)


def dot(a, b, ca=1, cb=0):
    return lax.dot_general(a, b, (((ca,), (cb,)), ((), ())), preferred_element_type=f32)


def kernel(
    nx, ny, levels, rows, cols,
    steps, rate_x, rate_y, gains,
    inc_hbm, dev_hbm, sea_hbm,
    out,
    wx, rx, wy, fy, ry, tx, ty, coef_x, coef_y,
    inside, before, ends_x, block_x, mix_x, mix_y, got_m,
    end_x, got_x, end_y, got_y, back_y, come_y, inc, dev, sea, wet,
    smx, rmx, smy, rmy, sx, rx_sem, sy, ry_sem, sb, rb, in_sem,
):
    gx, gy = lax.axis_index("gx"), lax.axis_index("gy")
    nb = rows // SIDE
    groups = levels // PAIR
    share = rows // ny
    mid = 64
    row = lax.broadcasted_iota(jnp.int32, (8, 128), 0)
    lane = lax.broadcasted_iota(jnp.int32, (8, 128), 1)
    place = jnp.where(row < 4, row, row - 4)
    left = lane < mid

    def turned(state):
        return [state] + [pltpu.roll(state, j, 0) for j in range(1, 4)]

    def advance(turns, coef, g, index):
        total = None
        for j in range(4):
            term = coef[g, 4 * index + j] * turns[j]
            total = term if total is None else total + term
        return total

    def mixed(mix, turns):
        total = mix[0] * turns[0]
        for j in range(1, 4):
            total += mix[j] * jnp.where(place >= j, turns[j], pltpu.roll(turns[0], j + 4, 0))
        return total

    def slide(tile, count):
        count = count % 128
        return pltpu.roll(tile, count, 1) if count else tile

    def x_peer(d):
        return (lax.rem(gx + d, nx), gy)

    def y_peer(d):
        return (gx, lax.rem(gy + d, ny))

    def mx_copy(g, d):
        return pltpu.make_async_remote_copy(
            src_ref=mix_x.at[g, gx], dst_ref=mix_x.at[g, gx],
            send_sem=smx.at[d - 1], recv_sem=rmx.at[g],
            device_id=x_peer(d), device_id_type=MESH,
        )

    def my_copy(g, d):
        return pltpu.make_async_remote_copy(
            src_ref=mix_y.at[g, lax.rem(gy + d, ny)], dst_ref=got_m.at[g, gy],
            send_sem=smy.at[d - 1], recv_sem=rmy.at[g],
            device_id=y_peer(d), device_id_type=MESH,
        )

    def x_copy(g, rep, d):
        return pltpu.make_async_remote_copy(
            src_ref=end_x.at[rep, g], dst_ref=got_x.at[rep, g, gx],
            send_sem=sx.at[rep, d - 1], recv_sem=rx_sem.at[rep, g],
            device_id=x_peer(d), device_id_type=MESH,
        )

    def y_copy(g, rep, d):
        return pltpu.make_async_remote_copy(
            src_ref=end_y.at[rep, g, lax.rem(gy + d, ny)], dst_ref=got_y.at[rep, g, gy],
            send_sem=sy.at[rep, d - 1], recv_sem=ry_sem.at[rep, g],
            device_id=y_peer(d), device_id_type=MESH,
        )

    def b_copy(g, rep, d):
        return pltpu.make_async_remote_copy(
            src_ref=back_y.at[rep, g, lax.rem(gy + d, ny)], dst_ref=come_y.at[rep, g, gy],
            send_sem=sb.at[rep, d - 1], recv_sem=rb.at[rep, g],
            device_id=y_peer(d), device_id_type=MESH,
        )

    def taken(ref, sem):
        pltpu.make_async_copy(ref, ref, sem).wait()

    def blocks(value):
        return jnp.concatenate([value[b * SIDE:(b + 1) * SIDE] for b in range(nb)], 1)

    def unblock(wide):
        return jnp.concatenate([wide[:, b * cols:(b + 1) * cols] for b in range(nb)], 0)

    def stack(value):
        return jnp.concatenate(split(value), 0)

    def halves(both):
        return both[:8] + both[8:16]

    def tiles(wide):
        return [wide[:, t * 128:(t + 1) * 128] for t in range(wide.shape[1] // 128)]

    def plus(total, piece):
        return piece if total is None else total + piece

    def packed(first, second, k):
        t, off = (k * share) // 128, (k * share) % 128
        return jnp.where(left, slide(first[t], -off), slide(second[t], mid - off))

    def x_first(g, values, rep):
        closing = opening = None
        for i, value in enumerate(values):
            l = PAIR * g + i
            both = dot(wx[0, l], stack(blocks(value)))
            held = both[:SIDE] + both[SIDE:2 * SIDE]
            inside[l] = held
            closing = plus(closing, halves(both[2 * SIDE:]))
            masked = stack(held * blocks(wet[l]))
            opening = plus(opening, halves(dot(wx[1, l, pl.ds(2 * SIDE, 16), :], masked)))
        closing, opening = tiles(closing), tiles(opening)
        carry = closing[0]
        chain = [opening[0]]
        ends_x[g, 0] = opening[0]
        for n in range(1, nb):
            turns = turned(carry)
            before[g, n - 1] = carry
            ends_x[g, n] = opening[n]
            chain.append(opening[n] + mixed([block_x[g, j, :, pl.ds(n * 128, 128)] for j in range(4)], turns))
            carry = advance(turns, coef_x, g, 0) + closing[n]
        end = chain[-1]
        for n in range(nb - 2, -1, -1):
            end = advance(turned(end), coef_x, g, 0) + chain[n]
        message = jnp.concatenate([carry, end], 0)
        end_x[rep, g] = message
        got_x[rep, g, gx] = message
        for d in range(1, nx):
            x_copy(g, rep, d).start()

    def x_second(g, rep):
        taken(got_x.at[rep, g, pl.ds(0, nx - 1)], rx_sem.at[rep, g])
        carry = got_x[rep, g, 0, pl.ds(0, 8)]
        zero = jnp.zeros_like(carry)
        come = zero
        ending = [None] * nx
        for j in range(1, nx):
            turns = turned(carry)
            come = jnp.where(gx == j, carry, come)
            ending[j] = got_x[rep, g, j, pl.ds(8, 8)] + mixed(
                [mix_x[g, j, pl.ds(8 * k, 8)] for k in range(4)], turns
            )
            if j < nx - 1:
                carry = advance(turns, coef_x, g, nb - 1) + got_x[rep, g, j, pl.ds(0, 8)]
        carry = ending[nx - 1]
        leave = jnp.where(gx == nx - 2, carry, zero)
        for j in range(nx - 2, 0, -1):
            carry = advance(turned(carry), coef_x, g, nb - 1) + ending[j]
            leave = jnp.where(gx == j - 1, carry, leave)
        turns = turned(come)
        starts = [come] + [advance(turns, coef_x, g, n - 1) + before[g, n - 1] for n in range(1, nb)]
        lasts = [None] * nb
        lasts[nb - 1] = leave
        for n in range(nb - 1, 0, -1):
            ending_n = ends_x[g, n] + mixed(
                [block_x[g, j, :, pl.ds(n * 128, 128)] for j in range(4)], turned(starts[n])
            )
            lasts[n - 1] = advance(turned(lasts[n]), coef_x, g, 0) + ending_n
        ahead, behind = three(jnp.concatenate(starts, 1)), three(jnp.concatenate(lasts, 1))
        values = []
        for i in range(PAIR):
            l = PAIR * g + i
            mask = blocks(wet[l])
            field = (inside[l] + dot(rx[0, l], ahead, 0, 0)) * mask
            both = dot(wx[1, l, pl.ds(0, 2 * SIDE), :], stack(field))
            field = both[:SIDE] + both[SIDE:] + dot(rx[1, l], behind, 0, 0)
            values.append(unblock(field * mask))
        return values

    def y_first(g, values, rep):
        closing = opening = None
        for i, value in enumerate(values):
            l = PAIR * g + i
            pair = jnp.concatenate(split(value), 1)
            closing = plus(closing, halves(dot(fy[0, l], pair, 1, 1)))
            wide = dot(pair, wy[0, l])
            held = wide[:, :cols] + wide[:, cols:]
            inside[l] = blocks(held)
            pair = jnp.concatenate(split(held * wet[l]), 1)
            opening = plus(opening, halves(dot(fy[1, l], pair, 1, 1)))
        closing, opening = tiles(closing), tiles(opening)
        for k in range(ny):
            end_y[rep, g, k] = packed(closing, opening, k)
        got_y[rep, g, gy] = end_y[rep, g, gy]
        for d in range(1, ny):
            y_copy(g, rep, d).start()

    def y_owner(g, rep):
        taken(got_y.at[rep, g, pl.ds(0, ny - 1)], ry_sem.at[rep, g])
        got = [got_y[rep, g, j] for j in range(ny)]
        first = [jnp.where(left, tile, slide(tile, mid)) for tile in got]
        starts, ending = [None] * ny, [None] * ny
        starts[0] = jnp.zeros_like(first[0])
        carry = first[0]
        for j in range(1, ny):
            turns = turned(carry)
            starts[j] = carry
            even, odd = got_m[g, j, pl.ds(0, 8)], got_m[g, j, pl.ds(8, 8)]
            ending[j] = got[j] + mixed([slide(even, mid), even, slide(odd, mid), odd], turns)
            if j < ny - 1:
                carry = advance(turns, coef_y, g, 0) + first[j]
        last = jnp.zeros_like(carry)
        for j in range(ny - 1, -1, -1):
            back_y[rep, g, j] = jnp.where(left, starts[j], last)
            if j:
                last = ending[j] if j == ny - 1 else advance(turned(last), coef_y, g, 0) + ending[j]
        come_y[rep, g, gy] = back_y[rep, g, gy]
        for d in range(1, ny):
            b_copy(g, rep, d).start()

    def y_second(g, rep):
        taken(come_y.at[rep, g, pl.ds(0, ny - 1)], rb.at[rep, g])
        starts, lasts = [None] * (rows // 128), [None] * (rows // 128)
        for k in range(ny):
            t, off = (k * share) // 128, (k * share) % 128
            tile = come_y[rep, g, k]
            start, last = slide(tile, off), slide(tile, off - mid)
            if off == 0:
                starts[t], lasts[t] = start, last
            else:
                starts[t] = jnp.where(lane >= off, start, starts[t])
                lasts[t] = jnp.where(lane >= off, last, lasts[t])
        ahead = dot(three(jnp.concatenate(starts, 1)), ry[0, g], 0, 0)
        behind = dot(three(jnp.concatenate(lasts, 1)), ry[1, g], 0, 0)
        values = []
        for i in range(PAIR):
            l = PAIR * g + i
            own = slice(i * cols, (i + 1) * cols)
            mask = wet[l]
            field = (unblock(inside[l]) + ahead[:, own]) * mask
            wide = dot(jnp.concatenate(split(field), 1), wy[1, l])
            values.append((wide[:, :cols] + wide[:, cols:] + behind[:, own]) * mask)
        return values

    def each(body, unroll=1):
        lax.fori_loop(0, groups, lambda g, c: (body(g), c)[1], 0, unroll=unroll)

    sources = ((sea_hbm, sea), (inc_hbm, inc), (dev_hbm, dev))

    def incoming(l, n):
        src, dst = sources[n]
        return pltpu.make_async_copy(src.at[l], dst.at[l], in_sem.at[n, l])

    for l in range(levels):
        for n in range(3):
            incoming(l, n).start()

    lags = (
        lax.broadcasted_iota(jnp.int32, (SIDE, SIDE), 0) - lax.broadcasted_iota(jnp.int32, (SIDE, SIDE), 1)
    ).astype(f32)

    def shape_of(lag):
        span = jnp.maximum(lag, 0.0)
        return span, jnp.where(lag > -0.5, (span + 1.0) * (span + 2.0) * (span + 3.0) / 6.0, 0.0)

    near = (shape_of(lags), shape_of(-lags))

    def tile(shape, rate, weight):
        weight4 = weight * weight * weight * weight
        return split(weight4 * shape[1] * jnp.exp(-rate * shape[0]))

    def by_row(values, i):
        total = jnp.zeros(row.shape, f32)
        for k, value in enumerate(values):
            total = jnp.where(row == k + 4 * i, value, total)
        return total

    def powers(weight):
        return [jnp.full((8, 128), v) for v in (1.0, weight, weight * weight, weight * weight * weight)]

    def final_of(i, places, rate, weight):
        pw, leave = powers(weight), binomials(places + 1.0)
        return by_row([weight * pw[k] * leave[k] for k in range(4)], i) * jnp.exp(-rate * places)

    def answer_of(i, places, rate, weight):
        pw, ahead = powers(weight), places + 1.0
        come = binomials(ahead)
        return by_row([pw[3 - k] * come[3 - k] for k in range(4)], i) * jnp.exp(-rate * ahead)

    def high_low(value):
        high = value.astype(bf16).astype(f32)
        return high, value - high

    def ends(i, back, rate, weight):
        across = lane.astype(f32)
        mirror = SIDE - 1.0 - across
        high, low = high_low(final_of(i, across if back else mirror, rate, weight))
        finals = jnp.concatenate([high, low], 0).astype(bf16)
        high, low = high_low(answer_of(i, mirror if back else across, rate, weight))
        answers = jnp.concatenate([high, high, low, jnp.zeros_like(high)], 0).astype(bf16)
        return finals, answers

    def products(i, places, rate, weight):
        final = final_of(i, places, rate, weight)
        turns = turned(answer_of(i, places, rate, weight))
        parts = []
        for j in range(4):
            turn = turns[0] if j == 0 else jnp.where(place >= j, turns[j], pltpu.roll(turns[0], j + 4, 0))
            parts += list(high_low(final * turn))
        return jnp.concatenate(parts, 0).astype(bf16)

    def coefs(coef, g, spans, rates, weights):
        low = row < 4
        rate = jnp.where(low, rates[0], rates[1])
        weight = jnp.where(low, weights[0], weights[1])
        power = (jnp.ones_like(weight), weight, weight * weight, weight * weight * weight)
        for n, span in enumerate(spans):
            fall = jnp.exp(-rate * span)
            count = (1.0, span, span * (span + 1.0) / 2.0, span * (span + 1.0) * (span + 2.0) / 6.0)
            for j in range(4):
                coef[g, 4 * n + j] = jnp.where(place >= j, fall * (power[j] * count[j]), 0.0)

    def build(g):
        zero = jnp.zeros((SIDE, SIDE), bf16)
        across = lane.astype(f32)
        lower, upper, rest = pl.ds(0, SIDE), pl.ds(SIDE, SIDE), pl.ds(2 * SIDE, 16)
        for i in range(PAIR):
            l = PAIR * g + i
            rate, weight = rate_x[l], gains[0, l]
            for back in (0, 1):
                high, low = tile(near[back], rate, weight)
                wx[back, l, lower, lower] = high
                wx[back, l, lower, upper] = high
                wx[back, l, upper, lower] = low
                wx[back, l, upper, upper] = zero
                finals, answers = ends(i, back, rate, weight)
                wx[back, l, rest, lower] = finals
                wx[back, l, rest, upper] = finals
                rx[back, l] = answers
            for b in range(nb):
                tx[l, :, pl.ds(b * SIDE, SIDE)] = products(i, across + float(b * SIDE), rate, weight)
            rate, weight = rate_y[l], gains[1, l]
            for back in (0, 1):
                high, low = tile(near[1 - back], rate, weight)
                wy[back, l, lower, lower] = high
                wy[back, l, upper, lower] = high
                wy[back, l, lower, upper] = low
                wy[back, l, upper, upper] = zero
                finals, answers = ends(i, back, rate, weight)
                fy[back, l, :, lower] = finals
                fy[back, l, :, upper] = finals
                ry[back, g, :, pl.ds(i * cols, cols)] = answers
            ty[l] = products(i, across, rate, weight)
        two = [PAIR * g + i for i in range(PAIR)]
        spans = [float(SIDE * n) for n in range(1, nb)] + [float(rows)]
        coefs(coef_x, g, spans, [rate_x[l] for l in two], [gains[0, l] for l in two])
        coefs(coef_y, g, [float(cols)], [rate_y[l] for l in two], [gains[1, l] for l in two])

    barrier = pltpu.get_barrier_semaphore()
    for d in range(1, nx):
        pl.semaphore_signal(barrier, inc=1, device_id=x_peer(d), device_id_type=MESH)
    for d in range(1, ny):
        pl.semaphore_signal(barrier, inc=1, device_id=y_peer(d), device_id_type=MESH)

    each(build)
    pl.semaphore_wait(barrier, nx + ny - 2)

    def four(wide):
        return [halves(wide[16 * j:16 * j + 16]) for j in range(4)]

    def begin(g):
        values = []
        device = block = across = None
        for i in range(PAIR):
            l = PAIR * g + i
            incoming(l, 0).wait()
            mask = sea[l].astype(f32)
            wet[l] = mask
            mask = mask.astype(bf16)
            device = plus(device, dot(tx[l], mask))
            block = plus(block, dot(tx[l, :, pl.ds(0, SIDE)], blocks(mask)))
            across = plus(across, dot(ty[l], mask, 1, 1))
        mix_x[g, gx] = jnp.concatenate(four(device), 0)
        for d in range(1, nx):
            mx_copy(g, d).start()
        for j, part in enumerate(four(block)):
            block_x[g, j] = part
        parts = [tiles(part) for part in four(across)]
        for k in range(ny):
            mix_y[g, k] = jnp.concatenate([packed(parts[0], parts[1], k), packed(parts[2], parts[3], k)], 0)
        got_m[g, gy] = mix_y[g, gy]
        for d in range(1, ny):
            my_copy(g, d).start()
        for i in range(PAIR):
            l = PAIR * g + i
            for n in (1, 2):
                incoming(l, n).wait()
            values.append(dev[l] * wet[l] * inc[l])
        x_first(g, values, 0)

    each(begin)

    def repetition(rep, c):
        @pl.when(rep == 0)
        def _():
            for g in range(groups):
                taken(mix_x.at[g, pl.ds(0, nx - 1)], rmx.at[g])

        each(lambda g: y_first(g, x_second(g, rep), rep))

        @pl.when(rep == 0)
        def _():
            for g in range(groups):
                taken(got_m.at[g, pl.ds(0, ny - 1)], rmy.at[g])

        each(lambda g: y_owner(g, rep))

        @pl.when(rep < MAXSTEPS - 1)
        def _():
            def more(g):
                values = y_second(g, rep)
                for i, value in enumerate(values):
                    out[PAIR * g + i] = dev[PAIR * g + i] * value
                x_first(g, values, rep + 1)

            each(more)

        @pl.when(rep == MAXSTEPS - 1)
        def _():
            def last(g):
                values = y_second(g, rep)
                for i, value in enumerate(values):
                    l = PAIR * g + i
                    out[l] = jnp.where(steps[l] > rep, dev[l] * value, out[l])

            each(last)

        return c

    lax.fori_loop(0, MAXSTEPS, repetition, 0)

    for d in range(1, nx):
        taken(mix_x.at[:, 0], smx.at[d - 1])
        for rep in range(MAXSTEPS):
            taken(end_x.at[rep], sx.at[rep, d - 1])
    for d in range(1, ny):
        taken(mix_y.at[:, 0], smy.at[d - 1])
        for rep in range(MAXSTEPS):
            taken(end_y.at[rep, :, 0], sy.at[rep, d - 1])
            taken(back_y.at[rep, :, 0], sb.at[rep, d - 1])


def on_device(nx, ny, increment, deviation, land_sea, filter_steps, zonal_rate, meridional_rate):
    levels, rows, cols = increment.shape
    nb = rows // SIDE
    groups = levels // PAIR
    gains = section_gain(jnp.stack([zonal_rate, meridional_rate]), filter_steps[None])
    smem = pl.BlockSpec(memory_space=pltpu.SMEM)
    hbm = pl.BlockSpec(memory_space=pltpu.HBM)
    vmem = pl.BlockSpec(memory_space=pltpu.VMEM)
    reps = MAXSTEPS
    dma = pltpu.SemaphoreType.DMA
    return pl.pallas_call(
        functools.partial(kernel, nx, ny, levels, rows, cols),
        out_shape=jax.ShapeDtypeStruct(increment.shape, f32),
        in_specs=[smem] * 4 + [hbm] * 3,
        out_specs=vmem,
        scratch_shapes=[
            pltpu.VMEM((2, levels, 2 * SIDE + 16, 2 * SIDE), bf16),
            pltpu.VMEM((2, levels, 32, SIDE), bf16),
            pltpu.VMEM((2, levels, 2 * cols, 2 * cols), bf16),
            pltpu.VMEM((2, levels, 16, 2 * cols), bf16),
            pltpu.VMEM((2, groups, 32, PAIR * cols), bf16),
            pltpu.VMEM((levels, 64, rows), bf16),
            pltpu.VMEM((levels, 64, cols), bf16),
            pltpu.VMEM((groups, 4 * nb, 8, 128), f32),
            pltpu.VMEM((groups, 4, 8, 128), f32),
            pltpu.VMEM((levels, SIDE, nb * cols), f32),
            pltpu.VMEM((groups, nb - 1, 8, cols), f32),
            pltpu.VMEM((groups, nb, 8, cols), f32),
            pltpu.VMEM((groups, 4, 8, nb * cols), f32),
            pltpu.VMEM((groups, nx, 32, cols), f32),
            pltpu.VMEM((groups, ny, 16, 128), f32),
            pltpu.VMEM((groups, ny, 16, 128), f32),
            pltpu.VMEM((reps, groups, 16, cols), f32),
            pltpu.VMEM((reps, groups, nx, 16, cols), f32),
            pltpu.VMEM((reps, groups, ny, 8, 128), f32),
            pltpu.VMEM((reps, groups, ny, 8, 128), f32),
            pltpu.VMEM((reps, groups, ny, 8, 128), f32),
            pltpu.VMEM((reps, groups, ny, 8, 128), f32),
            pltpu.VMEM((levels, rows, cols), f32),
            pltpu.VMEM((levels, rows, cols), f32),
            pltpu.VMEM((levels, rows, cols), jnp.int32),
            pltpu.VMEM((levels, rows, cols), f32),
            dma((nx - 1,)),
            dma((groups,)),
            dma((ny - 1,)),
            dma((groups,)),
            dma((reps, nx - 1)),
            dma((reps, groups)),
            dma((reps, ny - 1)),
            dma((reps, groups)),
            dma((reps, ny - 1)),
            dma((reps, groups)),
            dma((3, levels)),
        ],
        compiler_params=pltpu.CompilerParams(
            collective_id=0, has_side_effects=True, vmem_limit_bytes=40 * 1024 * 1024
        ),
    )(
        filter_steps, zonal_rate, meridional_rate, gains,
        *(pltpu.with_memory_space_constraint(a, pltpu.HBM) for a in (increment, deviation, land_sea)),
    )


def solution(mesh):
    placed = (P(None, "gx", "gy"), P(None, "gx", "gy"), P(None, "gx", "gy"), P(), P(), P())
    body = functools.partial(on_device, mesh.shape["gx"], mesh.shape["gy"])
    return jax.shard_map(
        body, mesh=mesh, in_specs=placed, out_specs=P(None, "gx", "gy"), check_vma=False
    )
```

```python
import functools

import jax
import jax.numpy as jnp
from jax import lax
from jax.experimental import pallas as pl
from jax.experimental.pallas import tpu as pltpu
from jax.sharding import PartitionSpec as P

SIDE = 128
PAIR = 2
TEAM = 2
MAXSTEPS = 2
gain_base = 3.0**0.125
MESH = pl.DeviceIdType.MESH
f32, bf16 = jnp.float32, jnp.bfloat16


def section_gain(decay_rate, filter_steps):
    rate = jnp.full((8, 128), decay_rate)
    count = jnp.full((8, 128), filter_steps.astype(f32))
    series = jnp.ones_like(rate)
    for n in range(9, 1, -1):
        series = 1.0 - series * rate * (1.0 / n)
    fading = jnp.where(rate < 0.5, rate * series, 1.0 - jnp.exp(-rate))
    return gain_base * jnp.exp((1.0 - 1.0 / (16.0 * count)) * jnp.log(fading))


def binomials(count):
    return (
        jnp.ones_like(count),
        count,
        count * (count + 1.0) / 2.0,
        count * (count + 1.0) * (count + 2.0) / 6.0,
    )


def split(value):
    high = value.astype(bf16)
    return high, (value - high.astype(f32)).astype(bf16)


def three(state):
    high = state.astype(bf16).astype(f32)
    return jnp.concatenate([high, state - high, high, jnp.zeros_like(high)], 0).astype(bf16)


def dot(a, b, ca=1, cb=0):
    return lax.dot_general(a, b, (((ca,), (cb,)), ((), ())), preferred_element_type=f32)


def kernel(
    nx, ny, levels, rows, cols,
    steps_hbm, rate_x_hbm, rate_y_hbm,
    inc_hbm, dev_hbm, sea_hbm,
    out,
    steps, rate_x, rate_y,
    wx, bx, rx, wy, by, ry, tx, ty, coef_x, coef_y,
    inside, before, ends_x, block_x, mix_x, mix_y, got_m,
    end_x, got_x, end_y, got_y, back_y, come_y, inc, dev, sea, wet, wet_t, kept,
    smx, rmx, smy, rmy, sx, rx_sem, sy, ry_sem, sb, rb, in_sem, few_sem,
):
    gx, gy = lax.axis_index("gx"), lax.axis_index("gy")
    nb = rows // SIDE
    groups = levels // PAIR
    share = rows // ny
    mid = 64
    row = lax.broadcasted_iota(jnp.int32, (8, 128), 0)
    lane = lax.broadcasted_iota(jnp.int32, (8, 128), 1)
    place = jnp.where(row < 4, row, row - 4)
    left = lane < mid

    def turned(state):
        return [state] + [pltpu.roll(state, j, 0) for j in range(1, 4)]

    def advance(turns, coef, g, index):
        total = None
        for j in range(4):
            term = coef[g, 4 * index + j] * turns[j]
            total = term if total is None else total + term
        return total

    def mixed(mix, turns):
        total = mix[0] * turns[0]
        for j in range(1, 4):
            total += mix[j] * jnp.where(place >= j, turns[j], pltpu.roll(turns[0], j + 4, 0))
        return total

    def slide(tile, count):
        count = count % 128
        return pltpu.roll(tile, count, 1) if count else tile

    def x_peer(d):
        return (lax.rem(gx + d, nx), gy)

    def y_peer(d):
        return (gx, lax.rem(gy + d, ny))

    def mx_copy(g, d):
        return pltpu.make_async_remote_copy(
            src_ref=mix_x.at[g, gx], dst_ref=mix_x.at[g, gx],
            send_sem=smx.at[d - 1], recv_sem=rmx.at[g],
            device_id=x_peer(d), device_id_type=MESH,
        )

    def my_copy(g, d):
        return pltpu.make_async_remote_copy(
            src_ref=mix_y.at[g, lax.rem(gy + d, ny)], dst_ref=got_m.at[g, gy],
            send_sem=smy.at[d - 1], recv_sem=rmy.at[g],
            device_id=y_peer(d), device_id_type=MESH,
        )

    def x_copy(g, rep, d):
        return pltpu.make_async_remote_copy(
            src_ref=end_x.at[rep, g], dst_ref=got_x.at[rep, g, gx],
            send_sem=sx.at[rep, d - 1], recv_sem=rx_sem.at[rep, g],
            device_id=x_peer(d), device_id_type=MESH,
        )

    def y_copy(g, rep, d):
        return pltpu.make_async_remote_copy(
            src_ref=end_y.at[rep, g, lax.rem(gy + d, ny)], dst_ref=got_y.at[rep, g, gy],
            send_sem=sy.at[rep, d - 1], recv_sem=ry_sem.at[rep, g],
            device_id=y_peer(d), device_id_type=MESH,
        )

    def b_copy(g, rep, d):
        return pltpu.make_async_remote_copy(
            src_ref=back_y.at[rep, g, lax.rem(gy + d, ny)], dst_ref=come_y.at[rep, g, gy],
            send_sem=sb.at[rep, d - 1], recv_sem=rb.at[rep, g],
            device_id=y_peer(d), device_id_type=MESH,
        )

    def taken(ref, sem):
        pltpu.make_async_copy(ref, ref, sem).wait()

    def blocks(value):
        return jnp.concatenate([value[b * SIDE:(b + 1) * SIDE] for b in range(nb)], 1)

    def unblock(wide):
        return jnp.concatenate([wide[:, b * cols:(b + 1) * cols] for b in range(nb)], 0)

    def stack(value):
        return jnp.concatenate(split(value), 0)

    def across(wide):
        high, low = split(wide)
        return jnp.concatenate([unblock(high), unblock(low)], 1)

    def of(gs):
        return [(n, PAIR * g + i) for n, g in enumerate(gs) for i in range(PAIR)]

    def x_mask(l):
        return blocks(wet[l])

    def y_mask(l):
        return wet_t[l]

    def firsts(gs, rhs, dim, weights, mask_of):
        closing, opening = [None] * len(gs), [None] * len(gs)
        masked = []
        for (n, l), side in zip(of(gs), rhs):
            both = dot(weights[l, pl.ds(0, 2 * SIDE + 16), :], side, 1, dim)
            held = both[:SIDE] + both[SIDE:2 * SIDE]
            inside[l] = held
            closing[n] = plus(closing[n], halves(both[2 * SIDE:]))
            masked.append(stack(held * mask_of(l)))
        for (n, l), side in zip(of(gs), masked):
            opening[n] = plus(opening[n], halves(dot(weights[l, pl.ds(2 * SIDE + 16, 16), :], side)))
        return [tiles(value) for value in closing], [tiles(value) for value in opening]

    def seconds(gs, starts, lasts, weights, answers, mask_of):
        ahead = [three(jnp.concatenate(tile, 1)) for tile in starts]
        behind = [three(jnp.concatenate(tile, 1)) for tile in lasts]
        sides = []
        for n, l in of(gs):
            field = (inside[l] + dot(answers[l], ahead[n])) * mask_of(l)
            high, low = split(field)
            sides.append(jnp.concatenate([high, low, high, behind[n]], 0))
        return [dot(weights[l], side) * mask_of(l) for (n, l), side in zip(of(gs), sides)]

    def halves(both):
        return both[:8] + both[8:16]

    def tiles(wide):
        return [wide[:, t * 128:(t + 1) * 128] for t in range(wide.shape[1] // 128)]

    def plus(total, piece):
        return piece if total is None else total + piece

    def packed(first, second, k):
        t, off = (k * share) // 128, (k * share) % 128
        return jnp.where(left, slide(first[t], -off), slide(second[t], mid - off))

    def x_first(gs, rhs, dim, rep):
        closings, openings = firsts(gs, rhs, dim, wx, x_mask)
        for g, closing, opening in zip(gs, closings, openings):
            carry = closing[0]
            chain = [opening[0]]
            ends_x[g, 0] = opening[0]
            for n in range(1, nb):
                turns = turned(carry)
                before[g, n - 1] = carry
                ends_x[g, n] = opening[n]
                chain.append(opening[n] + mixed([block_x[g, j, :, pl.ds(n * 128, 128)] for j in range(4)], turns))
                carry = advance(turns, coef_x, g, 0) + closing[n]
            end = chain[-1]
            for n in range(nb - 2, -1, -1):
                end = advance(turned(end), coef_x, g, 0) + chain[n]
            message = jnp.concatenate([carry, end], 0)
            end_x[rep, g] = message
            got_x[rep, g, gx] = message
        for g in gs:
            for d in range(1, nx):
                x_copy(g, rep, d).start()

    def x_entries(g, rep):
        carry = got_x[rep, g, 0, pl.ds(0, 8)]
        zero = jnp.zeros_like(carry)
        come = zero
        ending = [None] * nx
        for j in range(1, nx):
            turns = turned(carry)
            come = jnp.where(gx == j, carry, come)
            ending[j] = got_x[rep, g, j, pl.ds(8, 8)] + mixed(
                [mix_x[g, j, pl.ds(8 * k, 8)] for k in range(4)], turns
            )
            if j < nx - 1:
                carry = advance(turns, coef_x, g, nb - 1) + got_x[rep, g, j, pl.ds(0, 8)]
        carry = ending[nx - 1]
        leave = jnp.where(gx == nx - 2, carry, zero)
        for j in range(nx - 2, 0, -1):
            carry = advance(turned(carry), coef_x, g, nb - 1) + ending[j]
            leave = jnp.where(gx == j - 1, carry, leave)
        turns = turned(come)
        starts = [come] + [advance(turns, coef_x, g, n - 1) + before[g, n - 1] for n in range(1, nb)]
        lasts = [None] * nb
        lasts[nb - 1] = leave
        for n in range(nb - 1, 0, -1):
            ending_n = ends_x[g, n] + mixed(
                [block_x[g, j, :, pl.ds(n * 128, 128)] for j in range(4)], turned(starts[n])
            )
            lasts[n - 1] = advance(turned(lasts[n]), coef_x, g, 0) + ending_n
        return starts, lasts

    def x_second(gs, rep):
        for g in gs:
            @pl.when(rep == 0)
            def _():
                taken(mix_x.at[g, pl.ds(0, nx - 1)], rmx.at[g])

            taken(got_x.at[rep, g, pl.ds(0, nx - 1)], rx_sem.at[rep, g])
        starts, lasts = zip(*[x_entries(g, rep) for g in gs])
        return seconds(gs, starts, lasts, bx, rx, x_mask)

    def y_first(gs, fields, rep):
        closings, openings = firsts(gs, [across(field) for field in fields], 1, wy, y_mask)
        for g, closing, opening in zip(gs, closings, openings):
            for k in range(ny):
                end_y[rep, g, k] = packed(closing, opening, k)
            got_y[rep, g, gy] = end_y[rep, g, gy]
        for g in gs:
            for d in range(1, ny):
                y_copy(g, rep, d).start()

    def y_owner(gs, rep):
        for g in gs:
            @pl.when(rep == 0)
            def _():
                taken(got_m.at[g, pl.ds(0, ny - 1)], rmy.at[g])

            taken(got_y.at[rep, g, pl.ds(0, ny - 1)], ry_sem.at[rep, g])
        for g in gs:
            got = [got_y[rep, g, j] for j in range(ny)]
            first = [jnp.where(left, tile, slide(tile, mid)) for tile in got]
            starts, ending = [None] * ny, [None] * ny
            starts[0] = jnp.zeros_like(first[0])
            carry = first[0]
            for j in range(1, ny):
                turns = turned(carry)
                starts[j] = carry
                even, odd = got_m[g, j, pl.ds(0, 8)], got_m[g, j, pl.ds(8, 8)]
                ending[j] = got[j] + mixed([slide(even, mid), even, slide(odd, mid), odd], turns)
                if j < ny - 1:
                    carry = advance(turns, coef_y, g, 0) + first[j]
            last = jnp.zeros_like(carry)
            for j in range(ny - 1, -1, -1):
                back_y[rep, g, j] = jnp.where(left, starts[j], last)
                if j:
                    last = ending[j] if j == ny - 1 else advance(turned(last), coef_y, g, 0) + ending[j]
            come_y[rep, g, gy] = back_y[rep, g, gy]
        for g in gs:
            for d in range(1, ny):
                b_copy(g, rep, d).start()

    def y_entries(g, rep):
        starts, lasts = [None] * (rows // 128), [None] * (rows // 128)
        for k in range(ny):
            t, off = (k * share) // 128, (k * share) % 128
            tile = come_y[rep, g, k]
            start, last = slide(tile, off), slide(tile, off - mid)
            if off == 0:
                starts[t], lasts[t] = start, last
            else:
                starts[t] = jnp.where(lane >= off, start, starts[t])
                lasts[t] = jnp.where(lane >= off, last, lasts[t])
        return starts, lasts

    def y_second(gs, rep):
        for g in gs:
            taken(come_y.at[rep, g, pl.ds(0, ny - 1)], rb.at[rep, g])
        starts, lasts = zip(*[y_entries(g, rep) for g in gs])
        return seconds(gs, starts, lasts, by, ry, y_mask)

    def each(body, team=1):
        def step(s, c):
            body([team * s + n for n in range(team)])
            return c

        lax.fori_loop(0, groups // team, step, 0)

    sources = ((sea_hbm, sea), (inc_hbm, inc), (dev_hbm, dev))

    def incoming(l, n):
        src, dst = sources[n]
        return pltpu.make_async_copy(src.at[l], dst.at[l], in_sem.at[n, l])

    few = [
        pltpu.make_async_copy(src, dst, few_sem.at[n])
        for n, (src, dst) in enumerate(((steps_hbm, steps), (rate_x_hbm, rate_x), (rate_y_hbm, rate_y)))
    ]
    for copy in few:
        copy.start()
    for l in range(levels):
        for n in range(3):
            incoming(l, n).start()

    lags = (
        lax.broadcasted_iota(jnp.int32, (SIDE, SIDE), 0) - lax.broadcasted_iota(jnp.int32, (SIDE, SIDE), 1)
    ).astype(f32)

    def shape_of(lag):
        span = jnp.maximum(lag, 0.0)
        return span, jnp.where(lag > -0.5, (span + 1.0) * (span + 2.0) * (span + 3.0) / 6.0, 0.0)

    near = (shape_of(lags), shape_of(-lags))

    def tile(shape, rate, weight):
        weight4 = weight * weight * weight * weight
        weight4 = jnp.concatenate([weight4] * (SIDE // 8), 0)
        return split(weight4 * shape[1] * jnp.exp(-rate * shape[0]))

    def by_row(values, i):
        total = jnp.zeros(row.shape, f32)
        for k, value in enumerate(values):
            total = jnp.where(row == k + 4 * i, value, total)
        return total

    def powers(weight):
        return [jnp.ones_like(weight), weight, weight * weight, weight * weight * weight]

    def final_of(i, places, rate, weight):
        pw, leave = powers(weight), binomials(places + 1.0)
        return by_row([weight * pw[k] * leave[k] for k in range(4)], i) * jnp.exp(-rate * places)

    def answer_of(i, places, rate, weight):
        pw, ahead = powers(weight), places + 1.0
        come = binomials(ahead)
        return by_row([pw[3 - k] * come[3 - k] for k in range(4)], i) * jnp.exp(-rate * ahead)

    def high_low(value):
        high = value.astype(bf16).astype(f32)
        return high, value - high

    def finals(i, back, rate, weight):
        over = lane.astype(f32)
        high, low = high_low(final_of(i, over if back else SIDE - 1.0 - over, rate, weight))
        return jnp.concatenate([high, low], 0).astype(bf16)

    def answers(i, back, rate, weight):
        over = lane.astype(f32)
        high, low = high_low(answer_of(i, SIDE - 1.0 - over if back else over, rate, weight))
        return [high, high, low, jnp.zeros_like(high)]

    def filters(first, second, reply, g, rates, weights):
        zero = jnp.zeros((SIDE, SIDE), bf16)
        lower, upper = pl.ds(0, SIDE), pl.ds(SIDE, SIDE)
        replies = []
        for i in range(PAIR):
            l = PAIR * g + i
            rate, weight = rates[i], weights[i]
            high, low = tile(near[0], rate, weight)
            first[l, lower, lower] = high
            first[l, lower, upper] = high
            first[l, upper, lower] = low
            first[l, upper, upper] = zero
            high, low = tile(near[1], rate, weight)
            second[l, :, lower] = high
            second[l, :, upper] = high
            second[l, :, pl.ds(2 * SIDE, SIDE)] = low
            for back in (0, 1):
                final = finals(i, back, rate, weight)
                first[l, pl.ds(2 * SIDE + 16 * back, 16), lower] = final
                first[l, pl.ds(2 * SIDE + 16 * back, 16), upper] = final
                replies += answers(i, back, rate, weight)
        turn = jnp.concatenate(replies, 0).T
        for i in range(PAIR):
            l = PAIR * g + i
            for back in (0, 1):
                part = slide(turn, -32 * (2 * i + back))[:, :32].astype(bf16)
                if back:
                    second[l, :, pl.ds(3 * SIDE, 32)] = part
                else:
                    reply[l] = part

    def products(i, places, rate, weight):
        final = final_of(i, places, rate, weight)
        turns = turned(answer_of(i, places, rate, weight))
        parts = []
        for j in range(4):
            turn = turns[0] if j == 0 else jnp.where(place >= j, turns[j], pltpu.roll(turns[0], j + 4, 0))
            parts += list(high_low(final * turn))
        return jnp.concatenate(parts, 0).astype(bf16)

    def coefs(coef, g, spans, rates, weights):
        low = row < 4
        rate = jnp.where(low, rates[0], rates[1])
        weight = jnp.where(low, weights[0], weights[1])
        power = (jnp.ones_like(weight), weight, weight * weight, weight * weight * weight)
        for n, span in enumerate(spans):
            fall = jnp.exp(-rate * span)
            count = (1.0, span, span * (span + 1.0) / 2.0, span * (span + 1.0) * (span + 2.0) / 6.0)
            for j in range(4):
                coef[g, 4 * n + j] = jnp.where(place >= j, fall * (power[j] * count[j]), 0.0)

    def build_x(g):
        two = [PAIR * g + i for i in range(PAIR)]
        rates = [rate_x[l] for l in two]
        weights = [section_gain(rate_x[l], steps[l]) for l in two]
        filters(wx, bx, rx, g, rates, weights)
        for i, l in enumerate(two):
            for b in range(nb):
                places = lane.astype(f32) + float(b * SIDE)
                tx[l, :, pl.ds(b * SIDE, SIDE)] = products(i, places, rates[i], weights[i])
        spans = [float(SIDE * n) for n in range(1, nb)] + [float(rows)]
        coefs(coef_x, g, spans, rates, weights)

    def build_y(g):
        two = [PAIR * g + i for i in range(PAIR)]
        rates = [rate_y[l] for l in two]
        weights = [section_gain(rate_y[l], steps[l]) for l in two]
        filters(wy, by, ry, g, rates, weights)
        for i, l in enumerate(two):
            ty[l, pl.ds(0, SIDE)] = jnp.where(lags == 0.0, 1.0, 0.0).astype(bf16)
            ty[l, pl.ds(SIDE, 64)] = products(i, lane.astype(f32), rates[i], weights[i])
        coefs(coef_y, g, [float(cols)], rates, weights)

    barrier = pltpu.get_barrier_semaphore()
    for d in range(1, nx):
        pl.semaphore_signal(barrier, inc=1, device_id=x_peer(d), device_id_type=MESH)
    for d in range(1, ny):
        pl.semaphore_signal(barrier, inc=1, device_id=y_peer(d), device_id_type=MESH)

    for copy in few:
        copy.wait()
    each(lambda gs: build_x(gs[0]))
    pl.semaphore_wait(barrier, nx + ny - 2)

    def four(wide):
        return [halves(wide[16 * j:16 * j + 16]) for j in range(4)]

    def begin_x(gs):
        device, block = [None] * len(gs), [None] * len(gs)
        for n, l in of(gs):
            incoming(l, 0).wait()
        for n, l in of(gs):
            mask = sea[l].astype(f32)
            wet[l] = mask
            mask = mask.astype(bf16)
            device[n] = plus(device[n], dot(tx[l], mask))
            block[n] = plus(block[n], dot(tx[l, :, pl.ds(0, SIDE)], blocks(mask)))
        for n, g in enumerate(gs):
            mix_x[g, gx] = jnp.concatenate(four(device[n]), 0)
            for d in range(1, nx):
                mx_copy(g, d).start()
            for j, part in enumerate(four(block[n])):
                block_x[g, j] = part
        for n, l in of(gs):
            for m in (1, 2):
                incoming(l, m).wait()
        x_first(gs, [stack(blocks(dev[l] * wet[l] * inc[l])) for n, l in of(gs)], 0, 0)

    def begin_y(gs):
        for g in gs:
            build_y(g)
        mixes = [None] * len(gs)
        for n, l in of(gs):
            both = dot(ty[l], wet[l].astype(bf16), 1, 1)
            wet_t[l] = both[:SIDE]
            mixes[n] = plus(mixes[n], both[SIDE:])
        for n, g in enumerate(gs):
            parts = [tiles(part) for part in four(mixes[n])]
            for k in range(ny):
                mix_y[g, k] = jnp.concatenate([packed(parts[0], parts[1], k), packed(parts[2], parts[3], k)], 0)
            got_m[g, gy] = mix_y[g, gy]
            for d in range(1, ny):
                my_copy(g, d).start()

    each(begin_x, TEAM)
    each(begin_y, TEAM)

    def repetition(rep, c):
        each(lambda gs: y_first(gs, x_second(gs, rep), rep), TEAM)
        each(lambda gs: y_owner(gs, rep), TEAM)

        @pl.when(rep < MAXSTEPS - 1)
        def _():
            def more(gs):
                fields = y_second(gs, rep)
                for (n, l), field in zip(of(gs), fields):
                    kept[l] = field
                x_first(gs, [across(field) for field in fields], 1, rep + 1)

            each(more, TEAM)

        @pl.when(rep == MAXSTEPS - 1)
        def _():
            def last(gs):
                fields = y_second(gs, rep)
                for (n, l), field in zip(of(gs), fields):
                    field = jnp.where(steps[l] > rep, field, kept[l])
                    for b in range(nb):
                        own = pl.ds(b * SIDE, SIDE)
                        out[l, own] = dev[l, own] * field[:, b * SIDE:(b + 1) * SIDE].T

            each(last, TEAM)

        return c

    lax.fori_loop(0, MAXSTEPS, repetition, 0)

    for d in range(1, nx):
        taken(mix_x.at[:, 0], smx.at[d - 1])
        for rep in range(MAXSTEPS):
            taken(end_x.at[rep], sx.at[rep, d - 1])
    for d in range(1, ny):
        taken(mix_y.at[:, 0], smy.at[d - 1])
        for rep in range(MAXSTEPS):
            taken(end_y.at[rep, :, 0], sy.at[rep, d - 1])
            taken(back_y.at[rep, :, 0], sb.at[rep, d - 1])


def on_device(nx, ny, increment, deviation, land_sea, filter_steps, zonal_rate, meridional_rate):
    levels, rows, cols = increment.shape
    nb = rows // SIDE
    groups = levels // PAIR
    hbm = pl.BlockSpec(memory_space=pltpu.HBM)
    vmem = pl.BlockSpec(memory_space=pltpu.VMEM)
    reps = MAXSTEPS
    dma = pltpu.SemaphoreType.DMA
    return pl.pallas_call(
        functools.partial(kernel, nx, ny, levels, rows, cols),
        out_shape=jax.ShapeDtypeStruct(increment.shape, f32),
        in_specs=[hbm] * 6,
        out_specs=vmem,
        scratch_shapes=[
            pltpu.SMEM((levels,), jnp.int32),
            pltpu.SMEM((levels,), f32),
            pltpu.SMEM((levels,), f32),
            pltpu.VMEM((levels, 2 * SIDE + 32, 2 * SIDE), bf16),
            pltpu.VMEM((levels, SIDE, 3 * SIDE + 32), bf16),
            pltpu.VMEM((levels, SIDE, 32), bf16),
            pltpu.VMEM((levels, 2 * SIDE + 32, 2 * SIDE), bf16),
            pltpu.VMEM((levels, SIDE, 3 * SIDE + 32), bf16),
            pltpu.VMEM((levels, SIDE, 32), bf16),
            pltpu.VMEM((levels, 64, rows), bf16),
            pltpu.VMEM((levels, SIDE + 64, cols), bf16),
            pltpu.VMEM((groups, 4 * nb, 8, 128), f32),
            pltpu.VMEM((groups, 4, 8, 128), f32),
            pltpu.VMEM((levels, SIDE, nb * cols), f32),
            pltpu.VMEM((groups, nb - 1, 8, cols), f32),
            pltpu.VMEM((groups, nb, 8, cols), f32),
            pltpu.VMEM((groups, 4, 8, nb * cols), f32),
            pltpu.VMEM((groups, nx, 32, cols), f32),
            pltpu.VMEM((groups, ny, 16, 128), f32),
            pltpu.VMEM((groups, ny, 16, 128), f32),
            pltpu.VMEM((reps, groups, 16, cols), f32),
            pltpu.VMEM((reps, groups, nx, 16, cols), f32),
            pltpu.VMEM((reps, groups, ny, 8, 128), f32),
            pltpu.VMEM((reps, groups, ny, 8, 128), f32),
            pltpu.VMEM((reps, groups, ny, 8, 128), f32),
            pltpu.VMEM((reps, groups, ny, 8, 128), f32),
            pltpu.VMEM((levels, rows, cols), f32),
            pltpu.VMEM((levels, rows, cols), f32),
            pltpu.VMEM((levels, rows, cols), jnp.int32),
            pltpu.VMEM((levels, rows, cols), f32),
            pltpu.VMEM((levels, cols, rows), f32),
            pltpu.VMEM((levels, cols, rows), f32),
            dma((nx - 1,)),
            dma((groups,)),
            dma((ny - 1,)),
            dma((groups,)),
            dma((reps, nx - 1)),
            dma((reps, groups)),
            dma((reps, ny - 1)),
            dma((reps, groups)),
            dma((reps, ny - 1)),
            dma((reps, groups)),
            dma((3, levels)),
            dma((3,)),
        ],
        compiler_params=pltpu.CompilerParams(
            collective_id=0, has_side_effects=True, vmem_limit_bytes=40 * 1024 * 1024
        ),
    )(
        *(
            pltpu.with_memory_space_constraint(a, pltpu.HBM)
            for a in (filter_steps, zonal_rate, meridional_rate, increment, deviation, land_sea)
        )
    )


def solution(mesh):
    placed = (P(None, "gx", "gy"), P(None, "gx", "gy"), P(None, "gx", "gy"), P(), P(), P())
    body = functools.partial(on_device, mesh.shape["gx"], mesh.shape["gy"])
    return jax.shard_map(
        body, mesh=mesh, in_specs=placed, out_specs=P(None, "gx", "gy"), check_vma=False
    )
```

```python
import functools

import jax
import jax.numpy as jnp
from jax import lax
from jax.experimental import pallas as pl
from jax.experimental.pallas import tpu as pltpu
from jax.sharding import PartitionSpec as P

SIDE = 128
PAIR = 2
TEAM = 2
MAXSTEPS = 2
gain_base = 3.0**0.125
MESH = pl.DeviceIdType.MESH
f32, bf16 = jnp.float32, jnp.bfloat16


def section_gain(decay_rate, filter_steps):
    rate = jnp.full((8, 128), decay_rate)
    count = jnp.full((8, 128), filter_steps.astype(f32))
    series = jnp.ones_like(rate)
    for n in range(9, 1, -1):
        series = 1.0 - series * rate * (1.0 / n)
    fading = jnp.where(rate < 0.5, rate * series, 1.0 - jnp.exp(-rate))
    return gain_base * jnp.exp((1.0 - 1.0 / (16.0 * count)) * jnp.log(fading))


def binomials(count):
    return (
        jnp.ones_like(count),
        count,
        count * (count + 1.0) / 2.0,
        count * (count + 1.0) * (count + 2.0) / 6.0,
    )


def split(value):
    high = value.astype(bf16)
    return high, (value - high.astype(f32)).astype(bf16)


def three(state):
    high = state.astype(bf16).astype(f32)
    return jnp.concatenate([high, state - high, high, jnp.zeros_like(high)], 0).astype(bf16)


def dot(a, b, ca=1, cb=0):
    return lax.dot_general(a, b, (((ca,), (cb,)), ((), ())), preferred_element_type=f32)


def kernel(
    nx, ny, levels, rows, cols,
    steps_hbm, rate_x_hbm, rate_y_hbm,
    inc_hbm, dev_hbm, sea_hbm,
    out,
    steps, rate_x, rate_y,
    wx, bx, rx, wy, by, ry, tx, ty, coef_x, coef_y,
    inside, before, ends_x, block_x, mix_x, mix_y, got_m,
    end_x, got_x, end_y, got_y, back_y, come_y, inc, dev, sea, wet, wet_t, kept,
    smx, rmx, smy, rmy, sx, rx_sem, sy, ry_sem, sb, rb, in_sem, few_sem,
):
    gx, gy = lax.axis_index("gx"), lax.axis_index("gy")
    nb = rows // SIDE
    groups = levels // PAIR
    owners = ny // 2
    least = ny // 4
    share = rows // owners
    mine = jnp.clip(gy - least, 0, owners - 1)
    is_owner = (gy >= least) & (gy < least + owners)
    row = lax.broadcasted_iota(jnp.int32, (8, 128), 0)
    lane = lax.broadcasted_iota(jnp.int32, (8, 128), 1)
    place = jnp.where(row < 4, row, row - 4)

    def turned(state):
        return [state] + [pltpu.roll(state, j, 0) for j in range(1, 4)]

    def advance(turns, coef, g, index):
        total = None
        for j in range(4):
            term = coef[g, 4 * index + j] * turns[j]
            total = term if total is None else total + term
        return total

    def mixed(mix, turns):
        total = mix[0] * turns[0]
        for j in range(1, 4):
            total += mix[j] * jnp.where(place >= j, turns[j], pltpu.roll(turns[0], j + 4, 0))
        return total

    def slide(tile, count):
        count = count % 128
        return pltpu.roll(tile, count, 1) if count else tile

    def x_peer(d):
        return (lax.rem(gx + d, nx), gy)

    def y_peer(d):
        return (gx, lax.rem(gy + d, ny))

    def mx_copy(g, d):
        return pltpu.make_async_remote_copy(
            src_ref=mix_x.at[g, gx], dst_ref=mix_x.at[g, gx],
            send_sem=smx.at[d - 1], recv_sem=rmx.at[g],
            device_id=x_peer(d), device_id_type=MESH,
        )

    def to_owner(d):
        k = lax.rem(gy + d, owners)
        return k, least + k != gy

    def my_copy(g, k, d):
        return pltpu.make_async_remote_copy(
            src_ref=mix_y.at[g, k], dst_ref=got_m.at[g, gy],
            send_sem=smy.at[d], recv_sem=rmy.at[g],
            device_id=(gx, least + k), device_id_type=MESH,
        )

    def x_copy(g, rep, d):
        return pltpu.make_async_remote_copy(
            src_ref=end_x.at[rep, g], dst_ref=got_x.at[rep, g, gx],
            send_sem=sx.at[rep, d - 1], recv_sem=rx_sem.at[rep, g],
            device_id=x_peer(d), device_id_type=MESH,
        )

    def y_copy(g, rep, k, d):
        return pltpu.make_async_remote_copy(
            src_ref=end_y.at[rep, g, k], dst_ref=got_y.at[rep, g, gy],
            send_sem=sy.at[rep, d], recv_sem=ry_sem.at[rep, g],
            device_id=(gx, least + k), device_id_type=MESH,
        )

    def b_copy(g, rep, d):
        return pltpu.make_async_remote_copy(
            src_ref=back_y.at[rep, g, lax.rem(gy + d, ny)], dst_ref=come_y.at[rep, g, mine],
            send_sem=sb.at[rep, d - 1], recv_sem=rb.at[rep, g],
            device_id=y_peer(d), device_id_type=MESH,
        )

    def taken(ref, sem):
        pltpu.make_async_copy(ref, ref, sem).wait()

    def blocks(value):
        return jnp.concatenate([value[b * SIDE:(b + 1) * SIDE] for b in range(nb)], 1)

    def unblock(wide):
        return jnp.concatenate([wide[:, b * cols:(b + 1) * cols] for b in range(nb)], 0)

    def stack(value):
        return jnp.concatenate(split(value), 0)

    def across(wide):
        high, low = split(wide)
        return jnp.concatenate([unblock(high), unblock(low)], 1)

    def of(gs):
        return [(n, PAIR * g + i) for n, g in enumerate(gs) for i in range(PAIR)]

    def x_mask(l):
        return blocks(wet[l])

    def y_mask(l):
        return wet_t[l]

    def firsts(gs, rhs, dim, weights, mask_of):
        closing, opening = [None] * len(gs), [None] * len(gs)
        masked = []
        for (n, l), side in zip(of(gs), rhs):
            both = dot(weights[l, pl.ds(0, 2 * SIDE + 16), :], side, 1, dim)
            held = both[:SIDE] + both[SIDE:2 * SIDE]
            inside[l] = held
            closing[n] = plus(closing[n], halves(both[2 * SIDE:]))
            masked.append(stack(held * mask_of(l)))
        for (n, l), side in zip(of(gs), masked):
            opening[n] = plus(opening[n], halves(dot(weights[l, pl.ds(2 * SIDE + 16, 16), :], side)))
        return [tiles(value) for value in closing], [tiles(value) for value in opening]

    def seconds(gs, starts, lasts, weights, answers, mask_of):
        ahead = [three(jnp.concatenate(tile, 1)) for tile in starts]
        behind = [three(jnp.concatenate(tile, 1)) for tile in lasts]
        sides = []
        for n, l in of(gs):
            field = (inside[l] + dot(answers[l], ahead[n])) * mask_of(l)
            high, low = split(field)
            sides.append(jnp.concatenate([high, low, high, behind[n]], 0))
        return [dot(weights[l], side) * mask_of(l) for (n, l), side in zip(of(gs), sides)]

    def halves(both):
        return both[:8] + both[8:16]

    def tiles(wide):
        return [wide[:, t * 128:(t + 1) * 128] for t in range(wide.shape[1] // 128)]

    def plus(total, piece):
        return piece if total is None else total + piece

    def packed(parts, k):
        t, off = (k * share) // 128, (k * share) % 128
        return jnp.concatenate([slide(part[t], -off) for part in parts], 0)

    def x_first(gs, rhs, dim, rep):
        closings, openings = firsts(gs, rhs, dim, wx, x_mask)
        for g, closing, opening in zip(gs, closings, openings):
            carry = closing[0]
            chain = [opening[0]]
            ends_x[g, 0] = opening[0]
            for n in range(1, nb):
                turns = turned(carry)
                before[g, n - 1] = carry
                ends_x[g, n] = opening[n]
                chain.append(opening[n] + mixed([block_x[g, j, :, pl.ds(n * 128, 128)] for j in range(4)], turns))
                carry = advance(turns, coef_x, g, 0) + closing[n]
            end = chain[-1]
            for n in range(nb - 2, -1, -1):
                end = advance(turned(end), coef_x, g, 0) + chain[n]
            message = jnp.concatenate([carry, end], 0)
            end_x[rep, g] = message
            got_x[rep, g, gx] = message
        for g in gs:
            for d in range(1, nx):
                x_copy(g, rep, d).start()

    def x_entries(g, rep):
        carry = got_x[rep, g, 0, pl.ds(0, 8)]
        zero = jnp.zeros_like(carry)
        come = zero
        ending = [None] * nx
        for j in range(1, nx):
            turns = turned(carry)
            come = jnp.where(gx == j, carry, come)
            ending[j] = got_x[rep, g, j, pl.ds(8, 8)] + mixed(
                [mix_x[g, j, pl.ds(8 * k, 8)] for k in range(4)], turns
            )
            if j < nx - 1:
                carry = advance(turns, coef_x, g, nb - 1) + got_x[rep, g, j, pl.ds(0, 8)]
        carry = ending[nx - 1]
        leave = jnp.where(gx == nx - 2, carry, zero)
        for j in range(nx - 2, 0, -1):
            carry = advance(turned(carry), coef_x, g, nb - 1) + ending[j]
            leave = jnp.where(gx == j - 1, carry, leave)
        turns = turned(come)
        starts = [come] + [advance(turns, coef_x, g, n - 1) + before[g, n - 1] for n in range(1, nb)]
        lasts = [None] * nb
        lasts[nb - 1] = leave
        for n in range(nb - 1, 0, -1):
            ending_n = ends_x[g, n] + mixed(
                [block_x[g, j, :, pl.ds(n * 128, 128)] for j in range(4)], turned(starts[n])
            )
            lasts[n - 1] = advance(turned(lasts[n]), coef_x, g, 0) + ending_n
        return starts, lasts

    def x_second(gs, rep):
        for g in gs:
            @pl.when(rep == 0)
            def _():
                taken(mix_x.at[g, pl.ds(0, nx - 1)], rmx.at[g])

            taken(got_x.at[rep, g, pl.ds(0, nx - 1)], rx_sem.at[rep, g])
        starts, lasts = zip(*[x_entries(g, rep) for g in gs])
        return seconds(gs, starts, lasts, bx, rx, x_mask)

    def y_first(gs, fields, rep):
        closings, openings = firsts(gs, [across(field) for field in fields], 1, wy, y_mask)
        for g, closing, opening in zip(gs, closings, openings):
            for k in range(owners):
                end_y[rep, g, k] = packed([closing, opening], k)
            got_y[rep, g, gy] = end_y[rep, g, mine]
        for d in range(owners):
            k, other = to_owner(d)

            @pl.when(other)
            def _():
                for g in gs:
                    y_copy(g, rep, k, d).start()

    def y_owner(gs, rep):
        for g in gs:
            @pl.when(rep == 0)
            def _():
                taken(got_m.at[g, pl.ds(0, ny - 1)], rmy.at[g])

            taken(got_y.at[rep, g, pl.ds(0, ny - 1)], ry_sem.at[rep, g])
        for g in gs:
            starts, ending = [None] * ny, [None] * ny
            carry = got_y[rep, g, 0, pl.ds(0, 8)]
            starts[0] = jnp.zeros_like(carry)
            for j in range(1, ny):
                turns = turned(carry)
                starts[j] = carry
                ending[j] = got_y[rep, g, j, pl.ds(8, 8)] + mixed(
                    [got_m[g, j, pl.ds(8 * m, 8)] for m in range(4)], turns
                )
                if j < ny - 1:
                    carry = advance(turns, coef_y, g, 0) + got_y[rep, g, j, pl.ds(0, 8)]
            last = jnp.zeros_like(carry)
            for j in range(ny - 1, -1, -1):
                back_y[rep, g, j] = jnp.concatenate([starts[j], last], 0)
                if j:
                    last = ending[j] if j == ny - 1 else advance(turned(last), coef_y, g, 0) + ending[j]
            come_y[rep, g, mine] = back_y[rep, g, gy]
        for g in gs:
            for d in range(1, ny):
                b_copy(g, rep, d).start()

    def y_entries(g, rep):
        starts, lasts = [None] * (rows // 128), [None] * (rows // 128)
        for k in range(owners):
            t, off = (k * share) // 128, (k * share) % 128
            start = slide(come_y[rep, g, k, pl.ds(0, 8)], off)
            last = slide(come_y[rep, g, k, pl.ds(8, 8)], off)
            if off == 0:
                starts[t], lasts[t] = start, last
            else:
                starts[t] = jnp.where(lane >= off, start, starts[t])
                lasts[t] = jnp.where(lane >= off, last, lasts[t])
        return starts, lasts

    def y_second(gs, rep):
        for count, role in ((owners - 1, is_owner), (owners, jnp.logical_not(is_owner))):
            @pl.when(role)
            def _():
                for g in gs:
                    taken(come_y.at[rep, g, pl.ds(0, count)], rb.at[rep, g])

        starts, lasts = zip(*[y_entries(g, rep) for g in gs])
        return seconds(gs, starts, lasts, by, ry, y_mask)

    def each(body, team=1):
        def step(s, c):
            body([team * s + n for n in range(team)])
            return c

        lax.fori_loop(0, groups // team, step, 0)

    sources = ((sea_hbm, sea), (inc_hbm, inc), (dev_hbm, dev))

    def incoming(l, n):
        src, dst = sources[n]
        return pltpu.make_async_copy(src.at[l], dst.at[l], in_sem.at[n, l])

    few = [
        pltpu.make_async_copy(src, dst, few_sem.at[n])
        for n, (src, dst) in enumerate(((steps_hbm, steps), (rate_x_hbm, rate_x), (rate_y_hbm, rate_y)))
    ]
    for copy in few:
        copy.start()
    for l in range(levels):
        for n in range(3):
            incoming(l, n).start()

    lags = (
        lax.broadcasted_iota(jnp.int32, (SIDE, SIDE), 0) - lax.broadcasted_iota(jnp.int32, (SIDE, SIDE), 1)
    ).astype(f32)

    def shape_of(lag):
        span = jnp.maximum(lag, 0.0)
        return span, jnp.where(lag > -0.5, (span + 1.0) * (span + 2.0) * (span + 3.0) / 6.0, 0.0)

    near = (shape_of(lags), shape_of(-lags))

    def tile(shape, rate, weight):
        weight4 = weight * weight * weight * weight
        weight4 = jnp.concatenate([weight4] * (SIDE // 8), 0)
        return split(weight4 * shape[1] * jnp.exp(-rate * shape[0]))

    def by_row(values, i):
        total = jnp.zeros(row.shape, f32)
        for k, value in enumerate(values):
            total = jnp.where(row == k + 4 * i, value, total)
        return total

    def powers(weight):
        return [jnp.ones_like(weight), weight, weight * weight, weight * weight * weight]

    def final_of(i, places, rate, weight):
        pw, leave = powers(weight), binomials(places + 1.0)
        return by_row([weight * pw[k] * leave[k] for k in range(4)], i) * jnp.exp(-rate * places)

    def answer_of(i, places, rate, weight):
        pw, ahead = powers(weight), places + 1.0
        come = binomials(ahead)
        return by_row([pw[3 - k] * come[3 - k] for k in range(4)], i) * jnp.exp(-rate * ahead)

    def high_low(value):
        high = value.astype(bf16).astype(f32)
        return high, value - high

    def finals(i, back, rate, weight):
        over = lane.astype(f32)
        high, low = high_low(final_of(i, over if back else SIDE - 1.0 - over, rate, weight))
        return jnp.concatenate([high, low], 0).astype(bf16)

    def answers(i, back, rate, weight):
        over = lane.astype(f32)
        high, low = high_low(answer_of(i, SIDE - 1.0 - over if back else over, rate, weight))
        return [high, high, low, jnp.zeros_like(high)]

    def filters(first, second, reply, g, rates, weights):
        zero = jnp.zeros((SIDE, SIDE), bf16)
        lower, upper = pl.ds(0, SIDE), pl.ds(SIDE, SIDE)
        replies = []
        for i in range(PAIR):
            l = PAIR * g + i
            rate, weight = rates[i], weights[i]
            high, low = tile(near[0], rate, weight)
            first[l, lower, lower] = high
            first[l, lower, upper] = high
            first[l, upper, lower] = low
            first[l, upper, upper] = zero
            high, low = tile(near[1], rate, weight)
            second[l, :, lower] = high
            second[l, :, upper] = high
            second[l, :, pl.ds(2 * SIDE, SIDE)] = low
            for back in (0, 1):
                final = finals(i, back, rate, weight)
                first[l, pl.ds(2 * SIDE + 16 * back, 16), lower] = final
                first[l, pl.ds(2 * SIDE + 16 * back, 16), upper] = final
                replies += answers(i, back, rate, weight)
        turn = jnp.concatenate(replies, 0).T
        for i in range(PAIR):
            l = PAIR * g + i
            for back in (0, 1):
                part = slide(turn, -32 * (2 * i + back))[:, :32].astype(bf16)
                if back:
                    second[l, :, pl.ds(3 * SIDE, 32)] = part
                else:
                    reply[l] = part

    def products(i, places, rate, weight):
        final = final_of(i, places, rate, weight)
        turns = turned(answer_of(i, places, rate, weight))
        parts = []
        for j in range(4):
            turn = turns[0] if j == 0 else jnp.where(place >= j, turns[j], pltpu.roll(turns[0], j + 4, 0))
            parts += list(high_low(final * turn))
        return jnp.concatenate(parts, 0).astype(bf16)

    def coefs(coef, g, spans, rates, weights):
        low = row < 4
        rate = jnp.where(low, rates[0], rates[1])
        weight = jnp.where(low, weights[0], weights[1])
        power = (jnp.ones_like(weight), weight, weight * weight, weight * weight * weight)
        for n, span in enumerate(spans):
            fall = jnp.exp(-rate * span)
            count = (1.0, span, span * (span + 1.0) / 2.0, span * (span + 1.0) * (span + 2.0) / 6.0)
            for j in range(4):
                coef[g, 4 * n + j] = jnp.where(place >= j, fall * (power[j] * count[j]), 0.0)

    def build_x(g):
        two = [PAIR * g + i for i in range(PAIR)]
        rates = [rate_x[l] for l in two]
        weights = [section_gain(rate_x[l], steps[l]) for l in two]
        filters(wx, bx, rx, g, rates, weights)
        for i, l in enumerate(two):
            for b in range(nb):
                places = lane.astype(f32) + float(b * SIDE)
                tx[l, :, pl.ds(b * SIDE, SIDE)] = products(i, places, rates[i], weights[i])
        spans = [float(SIDE * n) for n in range(1, nb)] + [float(rows)]
        coefs(coef_x, g, spans, rates, weights)

    def build_y(g):
        two = [PAIR * g + i for i in range(PAIR)]
        rates = [rate_y[l] for l in two]
        weights = [section_gain(rate_y[l], steps[l]) for l in two]
        filters(wy, by, ry, g, rates, weights)
        for i, l in enumerate(two):
            ty[l, pl.ds(0, SIDE)] = jnp.where(lags == 0.0, 1.0, 0.0).astype(bf16)
            ty[l, pl.ds(SIDE, 64)] = products(i, lane.astype(f32), rates[i], weights[i])
        coefs(coef_y, g, [float(cols)], rates, weights)

    barrier = pltpu.get_barrier_semaphore()
    for d in range(1, nx):
        pl.semaphore_signal(barrier, inc=1, device_id=x_peer(d), device_id_type=MESH)
    for d in range(1, ny):
        pl.semaphore_signal(barrier, inc=1, device_id=y_peer(d), device_id_type=MESH)

    for copy in few:
        copy.wait()
    each(lambda gs: build_x(gs[0]))

    def four(wide):
        return [halves(wide[16 * j:16 * j + 16]) for j in range(4)]

    def begin_x(gs):
        device, block = [None] * len(gs), [None] * len(gs)
        for n, l in of(gs):
            incoming(l, 0).wait()
        for n, l in of(gs):
            mask = sea[l].astype(f32)
            wet[l] = mask
            mask = mask.astype(bf16)
            device[n] = plus(device[n], dot(tx[l], mask))
            block[n] = plus(block[n], dot(tx[l, :, pl.ds(0, SIDE)], blocks(mask)))
        for n, g in enumerate(gs):
            mix_x[g, gx] = jnp.concatenate(four(device[n]), 0)
            for j, part in enumerate(four(block[n])):
                block_x[g, j] = part

        @pl.when(gs[0] == 0)
        def _():
            pl.semaphore_wait(barrier, nx + ny - 2)

        for g in gs:
            for d in range(1, nx):
                mx_copy(g, d).start()
        for n, l in of(gs):
            for m in (1, 2):
                incoming(l, m).wait()
        x_first(gs, [stack(blocks(dev[l] * wet[l] * inc[l])) for n, l in of(gs)], 0, 0)

    def begin_y(gs):
        for g in gs:
            build_y(g)
        mixes = [None] * len(gs)
        for n, l in of(gs):
            both = dot(ty[l], wet[l].astype(bf16), 1, 1)
            wet_t[l] = both[:SIDE]
            mixes[n] = plus(mixes[n], both[SIDE:])
        for n, g in enumerate(gs):
            parts = [tiles(part) for part in four(mixes[n])]
            for k in range(owners):
                mix_y[g, k] = packed(parts, k)
            got_m[g, gy] = mix_y[g, mine]
        for d in range(owners):
            k, other = to_owner(d)

            @pl.when(other)
            def _():
                for g in gs:
                    my_copy(g, k, d).start()

    def begin(gs):
        begin_x(gs)
        begin_y(gs)

    each(begin, TEAM)

    def repetition(rep, c):
        each(lambda gs: y_first(gs, x_second(gs, rep), rep), TEAM)
        @pl.when(is_owner)
        def _():
            each(lambda gs: y_owner(gs, rep), TEAM)


        @pl.when(rep < MAXSTEPS - 1)
        def _():
            def more(gs):
                fields = y_second(gs, rep)
                for (n, l), field in zip(of(gs), fields):
                    kept[l] = field
                x_first(gs, [across(field) for field in fields], 1, rep + 1)

            each(more, TEAM)

        @pl.when(rep == MAXSTEPS - 1)
        def _():
            def last(gs):
                fields = y_second(gs, rep)
                for (n, l), field in zip(of(gs), fields):
                    field = jnp.where(steps[l] > rep, field, kept[l])
                    for b in range(nb):
                        own = pl.ds(b * SIDE, SIDE)
                        out[l, own] = dev[l, own] * field[:, b * SIDE:(b + 1) * SIDE].T

            each(last, TEAM)

        return c

    lax.fori_loop(0, MAXSTEPS, repetition, 0)

    for d in range(1, nx):
        taken(mix_x.at[:, 0], smx.at[d - 1])
        for rep in range(MAXSTEPS):
            taken(end_x.at[rep], sx.at[rep, d - 1])
    for d in range(owners):
        k, other = to_owner(d)

        @pl.when(other)
        def _():
            taken(mix_y.at[:, 0], smy.at[d])
            for rep in range(MAXSTEPS):
                taken(end_y.at[rep, :, 0], sy.at[rep, d])

    @pl.when(is_owner)
    def _():
        for d in range(1, ny):
            for rep in range(MAXSTEPS):
                taken(back_y.at[rep, :, 0], sb.at[rep, d - 1])


def on_device(nx, ny, increment, deviation, land_sea, filter_steps, zonal_rate, meridional_rate):
    levels, rows, cols = increment.shape
    nb = rows // SIDE
    groups = levels // PAIR
    hbm = pl.BlockSpec(memory_space=pltpu.HBM)
    vmem = pl.BlockSpec(memory_space=pltpu.VMEM)
    reps = MAXSTEPS
    dma = pltpu.SemaphoreType.DMA
    return pl.pallas_call(
        functools.partial(kernel, nx, ny, levels, rows, cols),
        out_shape=jax.ShapeDtypeStruct(increment.shape, f32),
        in_specs=[hbm] * 6,
        out_specs=vmem,
        scratch_shapes=[
            pltpu.SMEM((levels,), jnp.int32),
            pltpu.SMEM((levels,), f32),
            pltpu.SMEM((levels,), f32),
            pltpu.VMEM((levels, 2 * SIDE + 32, 2 * SIDE), bf16),
            pltpu.VMEM((levels, SIDE, 3 * SIDE + 32), bf16),
            pltpu.VMEM((levels, SIDE, 32), bf16),
            pltpu.VMEM((levels, 2 * SIDE + 32, 2 * SIDE), bf16),
            pltpu.VMEM((levels, SIDE, 3 * SIDE + 32), bf16),
            pltpu.VMEM((levels, SIDE, 32), bf16),
            pltpu.VMEM((levels, 64, rows), bf16),
            pltpu.VMEM((levels, SIDE + 64, cols), bf16),
            pltpu.VMEM((groups, 4 * nb, 8, 128), f32),
            pltpu.VMEM((groups, 4, 8, 128), f32),
            pltpu.VMEM((levels, SIDE, nb * cols), f32),
            pltpu.VMEM((groups, nb - 1, 8, cols), f32),
            pltpu.VMEM((groups, nb, 8, cols), f32),
            pltpu.VMEM((groups, 4, 8, nb * cols), f32),
            pltpu.VMEM((groups, nx, 32, cols), f32),
            pltpu.VMEM((groups, ny // 2, 32, 128), f32),
            pltpu.VMEM((groups, ny, 32, 128), f32),
            pltpu.VMEM((reps, groups, 16, cols), f32),
            pltpu.VMEM((reps, groups, nx, 16, cols), f32),
            pltpu.VMEM((reps, groups, ny // 2, 16, 128), f32),
            pltpu.VMEM((reps, groups, ny, 16, 128), f32),
            pltpu.VMEM((reps, groups, ny, 16, 128), f32),
            pltpu.VMEM((reps, groups, ny // 2, 16, 128), f32),
            pltpu.VMEM((levels, rows, cols), f32),
            pltpu.VMEM((levels, rows, cols), f32),
            pltpu.VMEM((levels, rows, cols), jnp.int32),
            pltpu.VMEM((levels, rows, cols), f32),
            pltpu.VMEM((levels, cols, rows), f32),
            pltpu.VMEM((levels, cols, rows), f32),
            dma((nx - 1,)),
            dma((groups,)),
            dma((ny // 2,)),
            dma((groups,)),
            dma((reps, nx - 1)),
            dma((reps, groups)),
            dma((reps, ny // 2)),
            dma((reps, groups)),
            dma((reps, ny - 1)),
            dma((reps, groups)),
            dma((3, levels)),
            dma((3,)),
        ],
        compiler_params=pltpu.CompilerParams(
            collective_id=0, has_side_effects=True, vmem_limit_bytes=40 * 1024 * 1024
        ),
    )(
        *(
            pltpu.with_memory_space_constraint(a, pltpu.HBM)
            for a in (filter_steps, zonal_rate, meridional_rate, increment, deviation, land_sea)
        )
    )


def solution(mesh):
    placed = (P(None, "gx", "gy"), P(None, "gx", "gy"), P(None, "gx", "gy"), P(), P(), P())
    body = functools.partial(on_device, mesh.shape["gx"], mesh.shape["gy"])
    return jax.shard_map(
        body, mesh=mesh, in_specs=placed, out_specs=P(None, "gx", "gy"), check_vma=False
    )
```

```python
import functools

import jax
import jax.numpy as jnp
from jax import lax
from jax.experimental import pallas as pl
from jax.experimental.pallas import tpu as pltpu
from jax.sharding import PartitionSpec as P

SIDE = 128
PAIR = 2
TEAM = 2
UNIQUE = 20
MAXSTEPS = 2
gain_base = 3.0**0.125
MESH = pl.DeviceIdType.MESH
f32, bf16 = jnp.float32, jnp.bfloat16


def section_gain(decay_rate, filter_steps):
    rate = jnp.full((8, 128), decay_rate)
    count = jnp.full((8, 128), filter_steps.astype(f32))
    series = jnp.ones_like(rate)
    for n in range(9, 1, -1):
        series = 1.0 - series * rate * (1.0 / n)
    fading = jnp.where(rate < 0.5, rate * series, 1.0 - jnp.exp(-rate))
    return gain_base * jnp.exp((1.0 - 1.0 / (16.0 * count)) * jnp.log(fading))


def binomials(count):
    return (
        jnp.ones_like(count),
        count,
        count * (count + 1.0) / 2.0,
        count * (count + 1.0) * (count + 2.0) / 6.0,
    )


def split(value):
    high = value.astype(bf16)
    return high, (value - high.astype(f32)).astype(bf16)


def three(state):
    high = state.astype(bf16).astype(f32)
    return jnp.concatenate([high, state - high, high, jnp.zeros_like(high)], 0).astype(bf16)


def dot(a, b, ca=1, cb=0):
    return lax.dot_general(a, b, (((ca,), (cb,)), ((), ())), preferred_element_type=f32)


def kernel(
    nx, ny, levels, rows, cols,
    steps_hbm, rate_x_hbm, rate_y_hbm,
    inc_hbm, dev_hbm, sea_hbm,
    out,
    steps, rate_x, rate_y,
    wx, bx, rx, wy, by, ry, tx, ty, coef_x, coef_y,
    inside, before, ends_x, block_x, mix_x, mix_y, got_m, full_y,
    end_x, got_x, end_y, got_y, back_y, come_y, inc, dev, sea, wet, wet_t, kept,
    smx, rmx, smy, rmy, sx, rx_sem, sy, ry_sem, sb, rb, in_sem, few_sem,
):
    gx, gy = lax.axis_index("gx"), lax.axis_index("gy")
    nb = rows // SIDE
    groups = levels // PAIR
    owners = ny // 2
    least = ny // 4
    share = rows // owners
    mine = jnp.clip(gy - least, 0, owners - 1)
    is_owner = (gy >= least) & (gy < least + owners)
    row = lax.broadcasted_iota(jnp.int32, (8, 128), 0)
    lane = lax.broadcasted_iota(jnp.int32, (8, 128), 1)
    place = jnp.where(row < 4, row, row - 4)

    def turned(state):
        return [state] + [pltpu.roll(state, j, 0) for j in range(1, 4)]

    def advance(turns, coef, g, index):
        total = None
        for j in range(4):
            term = coef[g, 4 * index + j] * turns[j]
            total = term if total is None else total + term
        return total

    def mixed(mix, turns):
        total = mix[0] * turns[0]
        for j in range(1, 4):
            total += mix[j] * jnp.where(place >= j, turns[j], pltpu.roll(turns[0], j + 4, 0))
        return total

    def slide(tile, count):
        count = count % 128
        return pltpu.roll(tile, count, 1) if count else tile

    def x_peer(d):
        return (lax.rem(gx + d, nx), gy)

    def y_peer(d):
        return (gx, lax.rem(gy + d, ny))

    def mx_copy(g, d):
        return pltpu.make_async_remote_copy(
            src_ref=mix_x.at[g, gx], dst_ref=mix_x.at[g, gx],
            send_sem=smx.at[d - 1], recv_sem=rmx.at[g],
            device_id=x_peer(d), device_id_type=MESH,
        )

    def to_owner(d):
        k = lax.rem(gy + d, owners)
        return k, least + k != gy

    def my_copy(g, k, d):
        return pltpu.make_async_remote_copy(
            src_ref=mix_y.at[g, k, pl.ds(0, UNIQUE)], dst_ref=got_m.at[g, gy, pl.ds(0, UNIQUE)],
            send_sem=smy.at[d], recv_sem=rmy.at[g],
            device_id=(gx, least + k), device_id_type=MESH,
        )

    def x_copy(g, rep, d):
        return pltpu.make_async_remote_copy(
            src_ref=end_x.at[rep, g], dst_ref=got_x.at[rep, g, gx],
            send_sem=sx.at[rep, d - 1], recv_sem=rx_sem.at[rep, g],
            device_id=x_peer(d), device_id_type=MESH,
        )

    def y_copy(g, rep, k, d):
        return pltpu.make_async_remote_copy(
            src_ref=end_y.at[rep, g, k], dst_ref=got_y.at[rep, g, gy],
            send_sem=sy.at[rep, d], recv_sem=ry_sem.at[rep, g],
            device_id=(gx, least + k), device_id_type=MESH,
        )

    def b_copy(g, rep, d):
        return pltpu.make_async_remote_copy(
            src_ref=back_y.at[rep, g, lax.rem(gy + d, ny)], dst_ref=come_y.at[rep, g, mine],
            send_sem=sb.at[rep, d - 1], recv_sem=rb.at[rep, g],
            device_id=y_peer(d), device_id_type=MESH,
        )

    def taken(ref, sem):
        pltpu.make_async_copy(ref, ref, sem).wait()

    def blocks(value):
        return jnp.concatenate([value[b * SIDE:(b + 1) * SIDE] for b in range(nb)], 1)

    def unblock(wide):
        return jnp.concatenate([wide[:, b * cols:(b + 1) * cols] for b in range(nb)], 0)

    def stack(value):
        return jnp.concatenate(split(value), 0)

    def across(wide):
        high, low = split(wide)
        return jnp.concatenate([unblock(high), unblock(low)], 1)

    def of(gs):
        return [(n, PAIR * g + i) for n, g in enumerate(gs) for i in range(PAIR)]

    def x_mask(l):
        return blocks(wet[l])

    def y_mask(l):
        return wet_t[l]

    def firsts(gs, rhs, dim, weights, mask_of):
        closing, opening = [None] * len(gs), [None] * len(gs)
        masked = []
        for (n, l), side in zip(of(gs), rhs):
            both = dot(weights[l, pl.ds(0, 2 * SIDE + 16), :], side, 1, dim)
            held = both[:SIDE] + both[SIDE:2 * SIDE]
            inside[l] = held
            closing[n] = plus(closing[n], halves(both[2 * SIDE:]))
            masked.append(stack(held * mask_of(l)))
        for (n, l), side in zip(of(gs), masked):
            opening[n] = plus(opening[n], halves(dot(weights[l, pl.ds(2 * SIDE + 16, 16), :], side)))
        return [tiles(value) for value in closing], [tiles(value) for value in opening]

    def seconds(gs, starts, lasts, weights, answers, mask_of):
        ahead = [three(jnp.concatenate(tile, 1)) for tile in starts]
        behind = [three(jnp.concatenate(tile, 1)) for tile in lasts]
        sides = []
        for n, l in of(gs):
            field = (inside[l] + dot(answers[l], ahead[n])) * mask_of(l)
            high, low = split(field)
            sides.append(jnp.concatenate([high, low, high, behind[n]], 0))
        return [dot(weights[l], side) * mask_of(l) for (n, l), side in zip(of(gs), sides)]

    def halves(both):
        return both[:8] + both[8:16]

    def tiles(wide):
        return [wide[:, t * 128:(t + 1) * 128] for t in range(wide.shape[1] // 128)]

    def plus(total, piece):
        return piece if total is None else total + piece

    def folded(mix):
        def one(m0, m1, m2, m3):
            both = jnp.where(place < 2, m0, jnp.where(place == 2, pltpu.roll(m2, 2, 0), pltpu.roll(m2, 1, 0)))
            return both, jnp.where(place < 3, m1, m3), jnp.where(row < 2, m3, pltpu.roll(m3, 6, 0))

        found = [one(*each_tile) for each_tile in zip(*[tiles(part) for part in mix])]
        return [jnp.concatenate(part, 1) for part in zip(*found)]

    def unfolded(t0, t1, t2):
        m0 = jnp.where(place == 2, pltpu.roll(t0, 1, 0), jnp.where(place == 3, pltpu.roll(t0, 3, 0), t0))
        m1 = jnp.where(place == 3, pltpu.roll(t1, 2, 0), t1)
        m2 = jnp.where(place == 0, pltpu.roll(t0, 6, 0), jnp.where(place < 3, pltpu.roll(t0, 7, 0), t0))
        m3 = jnp.where(row < 2, t2, jnp.where(row < 6, pltpu.roll(t2, 2, 0), pltpu.roll(t2, 4, 0)))
        return [m0, m1, m2, jnp.where(place == 3, t1, m3)]

    def packed(parts, k):
        t, off = (k * share) // 128, (k * share) % 128
        return jnp.concatenate([slide(part[t], -off) for part in parts], 0)

    def x_first(gs, rhs, dim, rep):
        closings, openings = firsts(gs, rhs, dim, wx, x_mask)
        for g, closing, opening in zip(gs, closings, openings):
            carry = closing[0]
            chain = [opening[0]]
            ends_x[g, 0] = opening[0]
            for n in range(1, nb):
                turns = turned(carry)
                before[g, n - 1] = carry
                ends_x[g, n] = opening[n]
                chain.append(opening[n] + mixed([block_x[g, j, :, pl.ds(n * 128, 128)] for j in range(4)], turns))
                carry = advance(turns, coef_x, g, 0) + closing[n]
            end = chain[-1]
            for n in range(nb - 2, -1, -1):
                end = advance(turned(end), coef_x, g, 0) + chain[n]
            message = jnp.concatenate([carry, end], 0)
            end_x[rep, g] = message
            got_x[rep, g, gx] = message
        for g in gs:
            for d in range(1, nx):
                x_copy(g, rep, d).start()

    def x_entries(g, rep):
        carry = got_x[rep, g, 0, pl.ds(0, 8)]
        zero = jnp.zeros_like(carry)
        come = zero
        ending = [None] * nx
        for j in range(1, nx):
            turns = turned(carry)
            come = jnp.where(gx == j, carry, come)
            ending[j] = got_x[rep, g, j, pl.ds(8, 8)] + mixed(
                [mix_x[g, j, pl.ds(8 * k, 8)] for k in range(4)], turns
            )
            if j < nx - 1:
                carry = advance(turns, coef_x, g, nb - 1) + got_x[rep, g, j, pl.ds(0, 8)]
        carry = ending[nx - 1]
        leave = jnp.where(gx == nx - 2, carry, zero)
        for j in range(nx - 2, 0, -1):
            carry = advance(turned(carry), coef_x, g, nb - 1) + ending[j]
            leave = jnp.where(gx == j - 1, carry, leave)
        turns = turned(come)
        starts = [come] + [advance(turns, coef_x, g, n - 1) + before[g, n - 1] for n in range(1, nb)]
        lasts = [None] * nb
        lasts[nb - 1] = leave
        for n in range(nb - 1, 0, -1):
            ending_n = ends_x[g, n] + mixed(
                [block_x[g, j, :, pl.ds(n * 128, 128)] for j in range(4)], turned(starts[n])
            )
            lasts[n - 1] = advance(turned(lasts[n]), coef_x, g, 0) + ending_n
        return starts, lasts

    def x_second(gs, rep):
        for g in gs:
            @pl.when(rep == 0)
            def _():
                taken(mix_x.at[g, pl.ds(0, nx - 1)], rmx.at[g])

            taken(got_x.at[rep, g, pl.ds(0, nx - 1)], rx_sem.at[rep, g])
        starts, lasts = zip(*[x_entries(g, rep) for g in gs])
        return seconds(gs, starts, lasts, bx, rx, x_mask)

    def y_first(gs, fields, rep):
        closings, openings = firsts(gs, [across(field) for field in fields], 1, wy, y_mask)
        for g, closing, opening in zip(gs, closings, openings):
            for k in range(owners):
                end_y[rep, g, k] = packed([closing, opening], k)
            got_y[rep, g, gy] = end_y[rep, g, mine]
        for d in range(owners):
            k, other = to_owner(d)

            @pl.when(other)
            def _():
                for g in gs:
                    y_copy(g, rep, k, d).start()

    def y_owner(gs, rep):
        for g in gs:
            @pl.when(rep == 0)
            def _():
                taken(got_m.at[g, pl.ds(0, ny - 1), pl.ds(0, UNIQUE)], rmy.at[g])
                for j in range(1, ny):
                    parts = unfolded(*[got_m[g, j, pl.ds(8 * m, 8)] for m in range(3)])
                    full_y[g, j] = jnp.concatenate(parts, 0)

        for g in gs:
            taken(got_y.at[rep, g, pl.ds(0, ny - 1)], ry_sem.at[rep, g])
        for g in gs:
            starts, ending = [None] * ny, [None] * ny
            carry = got_y[rep, g, 0, pl.ds(0, 8)]
            starts[0] = jnp.zeros_like(carry)
            for j in range(1, ny):
                turns = turned(carry)
                starts[j] = carry
                ending[j] = got_y[rep, g, j, pl.ds(8, 8)] + mixed(
                    [full_y[g, j, pl.ds(8 * m, 8)] for m in range(4)], turns
                )
                if j < ny - 1:
                    carry = advance(turns, coef_y, g, 0) + got_y[rep, g, j, pl.ds(0, 8)]
            last = jnp.zeros_like(carry)
            for j in range(ny - 1, -1, -1):
                back_y[rep, g, j] = jnp.concatenate([starts[j], last], 0)
                if j:
                    last = ending[j] if j == ny - 1 else advance(turned(last), coef_y, g, 0) + ending[j]
            come_y[rep, g, mine] = back_y[rep, g, gy]
        for g in gs:
            for d in range(1, ny):
                b_copy(g, rep, d).start()

    def y_entries(g, rep):
        starts, lasts = [None] * (rows // 128), [None] * (rows // 128)
        for k in range(owners):
            t, off = (k * share) // 128, (k * share) % 128
            start = slide(come_y[rep, g, k, pl.ds(0, 8)], off)
            last = slide(come_y[rep, g, k, pl.ds(8, 8)], off)
            if off == 0:
                starts[t], lasts[t] = start, last
            else:
                starts[t] = jnp.where(lane >= off, start, starts[t])
                lasts[t] = jnp.where(lane >= off, last, lasts[t])
        return starts, lasts

    def y_second(gs, rep):
        for count, role in ((owners - 1, is_owner), (owners, jnp.logical_not(is_owner))):
            @pl.when(role)
            def _():
                for g in gs:
                    taken(come_y.at[rep, g, pl.ds(0, count)], rb.at[rep, g])

        starts, lasts = zip(*[y_entries(g, rep) for g in gs])
        return seconds(gs, starts, lasts, by, ry, y_mask)

    def each(body, team=1):
        def step(s, c):
            body([team * s + n for n in range(team)])
            return c

        lax.fori_loop(0, groups // team, step, 0)

    sources = ((sea_hbm, sea), (inc_hbm, inc), (dev_hbm, dev))

    def incoming(l, n):
        src, dst = sources[n]
        return pltpu.make_async_copy(src.at[l], dst.at[l], in_sem.at[n, l])

    few = [
        pltpu.make_async_copy(src, dst, few_sem.at[n])
        for n, (src, dst) in enumerate(((steps_hbm, steps), (rate_x_hbm, rate_x), (rate_y_hbm, rate_y)))
    ]
    for copy in few:
        copy.start()
    for l in range(levels):
        for n in range(3):
            incoming(l, n).start()

    lags = (
        lax.broadcasted_iota(jnp.int32, (SIDE, SIDE), 0) - lax.broadcasted_iota(jnp.int32, (SIDE, SIDE), 1)
    ).astype(f32)

    def shape_of(lag):
        span = jnp.maximum(lag, 0.0)
        return span, jnp.where(lag > -0.5, (span + 1.0) * (span + 2.0) * (span + 3.0) / 6.0, 0.0)

    near = (shape_of(lags), shape_of(-lags))

    def tile(shape, rate, weight):
        weight4 = weight * weight * weight * weight
        weight4 = jnp.concatenate([weight4] * (SIDE // 8), 0)
        return split(weight4 * shape[1] * jnp.exp(-rate * shape[0]))

    def by_row(values, i):
        total = jnp.zeros(row.shape, f32)
        for k, value in enumerate(values):
            total = jnp.where(row == k + 4 * i, value, total)
        return total

    def powers(weight):
        return [jnp.ones_like(weight), weight, weight * weight, weight * weight * weight]

    def final_of(i, places, rate, weight):
        pw, leave = powers(weight), binomials(places + 1.0)
        return by_row([weight * pw[k] * leave[k] for k in range(4)], i) * jnp.exp(-rate * places)

    def answer_of(i, places, rate, weight):
        pw, ahead = powers(weight), places + 1.0
        come = binomials(ahead)
        return by_row([pw[3 - k] * come[3 - k] for k in range(4)], i) * jnp.exp(-rate * ahead)

    def high_low(value):
        high = value.astype(bf16).astype(f32)
        return high, value - high

    def finals(i, back, rate, weight):
        over = lane.astype(f32)
        high, low = high_low(final_of(i, over if back else SIDE - 1.0 - over, rate, weight))
        return jnp.concatenate([high, low], 0).astype(bf16)

    def answers(i, back, rate, weight):
        over = lane.astype(f32)
        high, low = high_low(answer_of(i, SIDE - 1.0 - over if back else over, rate, weight))
        return [high, high, low, jnp.zeros_like(high)]

    def filters(first, second, reply, g, rates, weights):
        zero = jnp.zeros((SIDE, SIDE), bf16)
        lower, upper = pl.ds(0, SIDE), pl.ds(SIDE, SIDE)
        replies = []
        for i in range(PAIR):
            l = PAIR * g + i
            rate, weight = rates[i], weights[i]
            high, low = tile(near[0], rate, weight)
            first[l, lower, lower] = high
            first[l, lower, upper] = high
            first[l, upper, lower] = low
            first[l, upper, upper] = zero
            high, low = tile(near[1], rate, weight)
            second[l, :, lower] = high
            second[l, :, upper] = high
            second[l, :, pl.ds(2 * SIDE, SIDE)] = low
            for back in (0, 1):
                final = finals(i, back, rate, weight)
                first[l, pl.ds(2 * SIDE + 16 * back, 16), lower] = final
                first[l, pl.ds(2 * SIDE + 16 * back, 16), upper] = final
                replies += answers(i, back, rate, weight)
        turn = jnp.concatenate(replies, 0).T
        for i in range(PAIR):
            l = PAIR * g + i
            for back in (0, 1):
                part = slide(turn, -32 * (2 * i + back))[:, :32].astype(bf16)
                if back:
                    second[l, :, pl.ds(3 * SIDE, 32)] = part
                else:
                    reply[l] = part

    def products(i, places, rate, weight):
        final = final_of(i, places, rate, weight)
        turns = turned(answer_of(i, places, rate, weight))
        parts = []
        for j in range(4):
            turn = turns[0] if j == 0 else jnp.where(place >= j, turns[j], pltpu.roll(turns[0], j + 4, 0))
            parts += list(high_low(final * turn))
        return jnp.concatenate(parts, 0).astype(bf16)

    def coefs(coef, g, spans, rates, weights):
        low = row < 4
        rate = jnp.where(low, rates[0], rates[1])
        weight = jnp.where(low, weights[0], weights[1])
        power = (jnp.ones_like(weight), weight, weight * weight, weight * weight * weight)
        for n, span in enumerate(spans):
            fall = jnp.exp(-rate * span)
            count = (1.0, span, span * (span + 1.0) / 2.0, span * (span + 1.0) * (span + 2.0) / 6.0)
            for j in range(4):
                coef[g, 4 * n + j] = jnp.where(place >= j, fall * (power[j] * count[j]), 0.0)

    def build_x(g):
        two = [PAIR * g + i for i in range(PAIR)]
        rates = [rate_x[l] for l in two]
        weights = [section_gain(rate_x[l], steps[l]) for l in two]
        filters(wx, bx, rx, g, rates, weights)
        for i, l in enumerate(two):
            for b in range(nb):
                places = lane.astype(f32) + float(b * SIDE)
                tx[l, :, pl.ds(b * SIDE, SIDE)] = products(i, places, rates[i], weights[i])
        spans = [float(SIDE * n) for n in range(1, nb)] + [float(rows)]
        coefs(coef_x, g, spans, rates, weights)

    def build_y(g):
        two = [PAIR * g + i for i in range(PAIR)]
        rates = [rate_y[l] for l in two]
        weights = [section_gain(rate_y[l], steps[l]) for l in two]
        filters(wy, by, ry, g, rates, weights)
        for i, l in enumerate(two):
            ty[l, pl.ds(0, SIDE)] = jnp.where(lags == 0.0, 1.0, 0.0).astype(bf16)
            ty[l, pl.ds(SIDE, 64)] = products(i, lane.astype(f32), rates[i], weights[i])
        coefs(coef_y, g, [float(cols)], rates, weights)

    barrier = pltpu.get_barrier_semaphore()
    for d in range(1, nx):
        pl.semaphore_signal(barrier, inc=1, device_id=x_peer(d), device_id_type=MESH)
    for d in range(1, ny):
        pl.semaphore_signal(barrier, inc=1, device_id=y_peer(d), device_id_type=MESH)

    for copy in few:
        copy.wait()
    each(lambda gs: build_x(gs[0]))

    def four(wide):
        return [halves(wide[16 * j:16 * j + 16]) for j in range(4)]

    def begin_x(gs):
        device, block = [None] * len(gs), [None] * len(gs)
        for n, l in of(gs):
            incoming(l, 0).wait()
        for n, l in of(gs):
            mask = sea[l].astype(f32)
            wet[l] = mask
            mask = mask.astype(bf16)
            device[n] = plus(device[n], dot(tx[l], mask))
            block[n] = plus(block[n], dot(tx[l, :, pl.ds(0, SIDE)], blocks(mask)))
        for n, g in enumerate(gs):
            mix_x[g, gx] = jnp.concatenate(four(device[n]), 0)
            for j, part in enumerate(four(block[n])):
                block_x[g, j] = part

        @pl.when(gs[0] == 0)
        def _():
            pl.semaphore_wait(barrier, nx + ny - 2)

        for g in gs:
            for d in range(1, nx):
                mx_copy(g, d).start()
        for n, l in of(gs):
            for m in (1, 2):
                incoming(l, m).wait()
        x_first(gs, [stack(blocks(dev[l] * wet[l] * inc[l])) for n, l in of(gs)], 0, 0)

    def begin_y(gs):
        for g in gs:
            build_y(g)
        mixes = [None] * len(gs)
        for n, l in of(gs):
            both = dot(ty[l], wet[l].astype(bf16), 1, 1)
            wet_t[l] = both[:SIDE]
            mixes[n] = plus(mixes[n], both[SIDE:])
        for n, g in enumerate(gs):
            parts = [tiles(part) for part in folded(four(mixes[n]))]
            for k in range(owners):
                mix_y[g, k] = packed(parts, k)
            got_m[g, gy] = mix_y[g, mine]
        for d in range(owners):
            k, other = to_owner(d)

            @pl.when(other)
            def _():
                for g in gs:
                    my_copy(g, k, d).start()

    def begin(gs):
        begin_x(gs)
        begin_y(gs)

    each(begin, TEAM)

    def repetition(rep, c):
        each(lambda gs: y_first(gs, x_second(gs, rep), rep), TEAM)
        @pl.when(is_owner)
        def _():
            each(lambda gs: y_owner(gs, rep), TEAM)


        @pl.when(rep < MAXSTEPS - 1)
        def _():
            def more(gs):
                fields = y_second(gs, rep)
                for (n, l), field in zip(of(gs), fields):
                    kept[l] = field
                x_first(gs, [across(field) for field in fields], 1, rep + 1)

            each(more, TEAM)

        @pl.when(rep == MAXSTEPS - 1)
        def _():
            def last(gs):
                fields = y_second(gs, rep)
                for (n, l), field in zip(of(gs), fields):
                    field = jnp.where(steps[l] > rep, field, kept[l])
                    for b in range(nb):
                        own = pl.ds(b * SIDE, SIDE)
                        out[l, own] = dev[l, own] * field[:, b * SIDE:(b + 1) * SIDE].T

            each(last, TEAM)

        return c

    lax.fori_loop(0, MAXSTEPS, repetition, 0)

    for d in range(1, nx):
        taken(mix_x.at[:, 0], smx.at[d - 1])
        for rep in range(MAXSTEPS):
            taken(end_x.at[rep], sx.at[rep, d - 1])
    for d in range(owners):
        k, other = to_owner(d)

        @pl.when(other)
        def _():
            taken(mix_y.at[:, 0, pl.ds(0, UNIQUE)], smy.at[d])
            for rep in range(MAXSTEPS):
                taken(end_y.at[rep, :, 0], sy.at[rep, d])

    @pl.when(is_owner)
    def _():
        for d in range(1, ny):
            for rep in range(MAXSTEPS):
                taken(back_y.at[rep, :, 0], sb.at[rep, d - 1])


def on_device(nx, ny, increment, deviation, land_sea, filter_steps, zonal_rate, meridional_rate):
    levels, rows, cols = increment.shape
    nb = rows // SIDE
    groups = levels // PAIR
    hbm = pl.BlockSpec(memory_space=pltpu.HBM)
    vmem = pl.BlockSpec(memory_space=pltpu.VMEM)
    reps = MAXSTEPS
    dma = pltpu.SemaphoreType.DMA
    return pl.pallas_call(
        functools.partial(kernel, nx, ny, levels, rows, cols),
        out_shape=jax.ShapeDtypeStruct(increment.shape, f32),
        in_specs=[hbm] * 6,
        out_specs=vmem,
        scratch_shapes=[
            pltpu.SMEM((levels,), jnp.int32),
            pltpu.SMEM((levels,), f32),
            pltpu.SMEM((levels,), f32),
            pltpu.VMEM((levels, 2 * SIDE + 32, 2 * SIDE), bf16),
            pltpu.VMEM((levels, SIDE, 3 * SIDE + 32), bf16),
            pltpu.VMEM((levels, SIDE, 32), bf16),
            pltpu.VMEM((levels, 2 * SIDE + 32, 2 * SIDE), bf16),
            pltpu.VMEM((levels, SIDE, 3 * SIDE + 32), bf16),
            pltpu.VMEM((levels, SIDE, 32), bf16),
            pltpu.VMEM((levels, 64, rows), bf16),
            pltpu.VMEM((levels, SIDE + 64, cols), bf16),
            pltpu.VMEM((groups, 4 * nb, 8, 128), f32),
            pltpu.VMEM((groups, 4, 8, 128), f32),
            pltpu.VMEM((levels, SIDE, nb * cols), f32),
            pltpu.VMEM((groups, nb - 1, 8, cols), f32),
            pltpu.VMEM((groups, nb, 8, cols), f32),
            pltpu.VMEM((groups, 4, 8, nb * cols), f32),
            pltpu.VMEM((groups, nx, 32, cols), f32),
            pltpu.VMEM((groups, ny // 2, 24, 128), f32),
            pltpu.VMEM((groups, ny, 24, 128), f32),
            pltpu.VMEM((groups, ny, 32, 128), f32),
            pltpu.VMEM((reps, groups, 16, cols), f32),
            pltpu.VMEM((reps, groups, nx, 16, cols), f32),
            pltpu.VMEM((reps, groups, ny // 2, 16, 128), f32),
            pltpu.VMEM((reps, groups, ny, 16, 128), f32),
            pltpu.VMEM((reps, groups, ny, 16, 128), f32),
            pltpu.VMEM((reps, groups, ny // 2, 16, 128), f32),
            pltpu.VMEM((levels, rows, cols), f32),
            pltpu.VMEM((levels, rows, cols), f32),
            pltpu.VMEM((levels, rows, cols), jnp.int32),
            pltpu.VMEM((levels, rows, cols), f32),
            pltpu.VMEM((levels, cols, rows), f32),
            pltpu.VMEM((levels, cols, rows), f32),
            dma((nx - 1,)),
            dma((groups,)),
            dma((ny // 2,)),
            dma((groups,)),
            dma((reps, nx - 1)),
            dma((reps, groups)),
            dma((reps, ny // 2)),
            dma((reps, groups)),
            dma((reps, ny - 1)),
            dma((reps, groups)),
            dma((3, levels)),
            dma((3,)),
        ],
        compiler_params=pltpu.CompilerParams(
            collective_id=0, has_side_effects=True, vmem_limit_bytes=40 * 1024 * 1024
        ),
    )(
        *(
            pltpu.with_memory_space_constraint(a, pltpu.HBM)
            for a in (filter_steps, zonal_rate, meridional_rate, increment, deviation, land_sea)
        )
    )


def solution(mesh):
    placed = (P(None, "gx", "gy"), P(None, "gx", "gy"), P(None, "gx", "gy"), P(), P(), P())
    body = functools.partial(on_device, mesh.shape["gx"], mesh.shape["gy"])
    return jax.shard_map(
        body, mesh=mesh, in_specs=placed, out_specs=P(None, "gx", "gy"), check_vma=False
    )
```

```python
import functools

import jax
import jax.numpy as jnp
from jax import lax
from jax.experimental import pallas as pl
from jax.experimental.pallas import tpu as pltpu
from jax.sharding import PartitionSpec as P

SIDE = 128
PAIR = 2
TEAM = 2
UNIQUE = 20
MAXSTEPS = 2
gain_base = 3.0**0.125
MESH = pl.DeviceIdType.MESH
f32, bf16 = jnp.float32, jnp.bfloat16


def section_gain(decay_rate, filter_steps):
    rate = jnp.full((8, 128), decay_rate)
    count = jnp.full((8, 128), filter_steps.astype(f32))
    series = jnp.ones_like(rate)
    for n in range(9, 1, -1):
        series = 1.0 - series * rate * (1.0 / n)
    fading = jnp.where(rate < 0.5, rate * series, 1.0 - jnp.exp(-rate))
    return gain_base * jnp.exp((1.0 - 1.0 / (16.0 * count)) * jnp.log(fading))


def binomials(count):
    return (
        jnp.ones_like(count),
        count,
        count * (count + 1.0) / 2.0,
        count * (count + 1.0) * (count + 2.0) / 6.0,
    )


def split(value):
    high = value.astype(bf16)
    return high, (value - high.astype(f32)).astype(bf16)


def three(state):
    high = state.astype(bf16).astype(f32)
    return jnp.concatenate([high, state - high, high, jnp.zeros_like(high)], 0).astype(bf16)


def dot(a, b, ca=1, cb=0):
    return lax.dot_general(a, b, (((ca,), (cb,)), ((), ())), preferred_element_type=f32)


def kernel(
    nx, ny, levels, rows, cols,
    steps_hbm, rate_x_hbm, rate_y_hbm,
    inc_hbm, dev_hbm, sea_hbm,
    out,
    steps, rate_x, rate_y,
    wx, bx, rx, wy, by, ry, tx, ty, coef_x, coef_y,
    inside, before, ends_x, block_x, mix_x, mix_y, got_m, full_y,
    end_x, got_x, end_y, got_y, back_y, come_y, inc, dev, sea, wet, wet_t, kept,
    smx, rmx, smy, rmy, sx, rx_sem, sy, ry_sem, sb, rb, in_sem, few_sem,
):
    gx, gy = lax.axis_index("gx"), lax.axis_index("gy")
    nb = rows // SIDE
    groups = levels // PAIR
    owners = ny // 2
    least = ny // 4
    share = rows // owners
    mine = jnp.clip(gy - least, 0, owners - 1)
    is_owner = (gy >= least) & (gy < least + owners)
    row = lax.broadcasted_iota(jnp.int32, (8, 128), 0)
    lane = lax.broadcasted_iota(jnp.int32, (8, 128), 1)
    place = jnp.where(row < 4, row, row - 4)

    def turned(state):
        return [state] + [pltpu.roll(state, j, 0) for j in range(1, 4)]

    def advance(turns, coef, g, index):
        total = None
        for j in range(4):
            term = coef[g, 4 * index + j] * turns[j]
            total = term if total is None else total + term
        return total

    def mixed(mix, turns):
        total = mix[0] * turns[0]
        for j in range(1, 4):
            total += mix[j] * jnp.where(place >= j, turns[j], pltpu.roll(turns[0], j + 4, 0))
        return total

    def slide(tile, count):
        count = count % 128
        return pltpu.roll(tile, count, 1) if count else tile

    def x_peer(d):
        return (lax.rem(gx + d, nx), gy)

    def y_peer(d):
        return (gx, lax.rem(gy + d, ny))

    def mx_copy(g, d):
        return pltpu.make_async_remote_copy(
            src_ref=mix_x.at[g, gx], dst_ref=mix_x.at[g, gx],
            send_sem=smx.at[d - 1], recv_sem=rmx.at[g],
            device_id=x_peer(d), device_id_type=MESH,
        )

    def to_owner(d):
        k = jnp.where(gy < ny // 2, owners - 1 - d, d)
        return k, least + k != gy

    def my_copy(g, k, d):
        return pltpu.make_async_remote_copy(
            src_ref=mix_y.at[g, k, pl.ds(0, UNIQUE)], dst_ref=got_m.at[g, gy, pl.ds(0, UNIQUE)],
            send_sem=smy.at[d], recv_sem=rmy.at[g],
            device_id=(gx, least + k), device_id_type=MESH,
        )

    def x_copy(g, rep, d):
        return pltpu.make_async_remote_copy(
            src_ref=end_x.at[rep, g], dst_ref=got_x.at[rep, g, gx],
            send_sem=sx.at[rep, d - 1], recv_sem=rx_sem.at[rep, g],
            device_id=x_peer(d), device_id_type=MESH,
        )

    def y_copy(g, rep, k, d):
        return pltpu.make_async_remote_copy(
            src_ref=end_y.at[rep, g, k], dst_ref=got_y.at[rep, g, gy],
            send_sem=sy.at[rep, d], recv_sem=ry_sem.at[rep, g],
            device_id=(gx, least + k), device_id_type=MESH,
        )

    def b_copy(g, rep, d):
        far = ny - d - (d >= ny - gy).astype(jnp.int32)
        near = d - 1 + (d > gy).astype(jnp.int32)
        target = jnp.where(gy < ny // 2, far, near)
        return pltpu.make_async_remote_copy(
            src_ref=back_y.at[rep, g, target], dst_ref=come_y.at[rep, g, mine],
            send_sem=sb.at[rep, d - 1], recv_sem=rb.at[rep, g],
            device_id=(gx, target), device_id_type=MESH,
        )

    def taken(ref, sem):
        pltpu.make_async_copy(ref, ref, sem).wait()

    def blocks(value):
        return jnp.concatenate([value[b * SIDE:(b + 1) * SIDE] for b in range(nb)], 1)

    def unblock(wide):
        return jnp.concatenate([wide[:, b * cols:(b + 1) * cols] for b in range(nb)], 0)

    def stack(value):
        return jnp.concatenate(split(value), 0)

    def across(wide):
        high, low = split(wide)
        return jnp.concatenate([unblock(high), unblock(low)], 1)

    def of(gs):
        return [(n, PAIR * g + i) for n, g in enumerate(gs) for i in range(PAIR)]

    def x_mask(l):
        return blocks(wet[l])

    def y_mask(l):
        return wet_t[l]

    def firsts(gs, rhs, dim, weights, mask_of):
        closing, opening = [None] * len(gs), [None] * len(gs)
        masked = []
        for (n, l), side in zip(of(gs), rhs):
            both = dot(weights[l, pl.ds(0, 2 * SIDE + 16), :], side, 1, dim)
            held = both[:SIDE] + both[SIDE:2 * SIDE]
            inside[l] = held
            closing[n] = plus(closing[n], halves(both[2 * SIDE:]))
            masked.append(stack(held * mask_of(l)))
        for (n, l), side in zip(of(gs), masked):
            opening[n] = plus(opening[n], halves(dot(weights[l, pl.ds(2 * SIDE + 16, 16), :], side)))
        return [tiles(value) for value in closing], [tiles(value) for value in opening]

    def seconds(gs, starts, lasts, weights, answers, mask_of):
        ahead = [three(jnp.concatenate(tile, 1)) for tile in starts]
        behind = [three(jnp.concatenate(tile, 1)) for tile in lasts]
        sides = []
        for n, l in of(gs):
            field = (inside[l] + dot(answers[l], ahead[n])) * mask_of(l)
            high, low = split(field)
            sides.append(jnp.concatenate([high, low, high, behind[n]], 0))
        return [dot(weights[l], side) * mask_of(l) for (n, l), side in zip(of(gs), sides)]

    def halves(both):
        return both[:8] + both[8:16]

    def tiles(wide):
        return [wide[:, t * 128:(t + 1) * 128] for t in range(wide.shape[1] // 128)]

    def plus(total, piece):
        return piece if total is None else total + piece

    def folded(mix):
        def one(m0, m1, m2, m3):
            both = jnp.where(place < 2, m0, jnp.where(place == 2, pltpu.roll(m2, 2, 0), pltpu.roll(m2, 1, 0)))
            return both, jnp.where(place < 3, m1, m3), jnp.where(row < 2, m3, pltpu.roll(m3, 6, 0))

        found = [one(*each_tile) for each_tile in zip(*[tiles(part) for part in mix])]
        return [jnp.concatenate(part, 1) for part in zip(*found)]

    def unfolded(t0, t1, t2):
        m0 = jnp.where(place == 2, pltpu.roll(t0, 1, 0), jnp.where(place == 3, pltpu.roll(t0, 3, 0), t0))
        m1 = jnp.where(place == 3, pltpu.roll(t1, 2, 0), t1)
        m2 = jnp.where(place == 0, pltpu.roll(t0, 6, 0), jnp.where(place < 3, pltpu.roll(t0, 7, 0), t0))
        m3 = jnp.where(row < 2, t2, jnp.where(row < 6, pltpu.roll(t2, 2, 0), pltpu.roll(t2, 4, 0)))
        return [m0, m1, m2, jnp.where(place == 3, t1, m3)]

    def packed(parts, k):
        t, off = (k * share) // 128, (k * share) % 128
        return jnp.concatenate([slide(part[t], -off) for part in parts], 0)

    def x_first(gs, rhs, dim, rep):
        closings, openings = firsts(gs, rhs, dim, wx, x_mask)
        for g, closing, opening in zip(gs, closings, openings):
            carry = closing[0]
            chain = [opening[0]]
            ends_x[g, 0] = opening[0]
            for n in range(1, nb):
                turns = turned(carry)
                before[g, n - 1] = carry
                ends_x[g, n] = opening[n]
                chain.append(opening[n] + mixed([block_x[g, j, :, pl.ds(n * 128, 128)] for j in range(4)], turns))
                carry = advance(turns, coef_x, g, 0) + closing[n]
            end = chain[-1]
            for n in range(nb - 2, -1, -1):
                end = advance(turned(end), coef_x, g, 0) + chain[n]
            message = jnp.concatenate([carry, end], 0)
            end_x[rep, g] = message
            got_x[rep, g, gx] = message
        for g in gs:
            for d in range(1, nx):
                x_copy(g, rep, d).start()

    def x_entries(g, rep):
        carry = got_x[rep, g, 0, pl.ds(0, 8)]
        zero = jnp.zeros_like(carry)
        come = zero
        ending = [None] * nx
        for j in range(1, nx):
            turns = turned(carry)
            come = jnp.where(gx == j, carry, come)
            ending[j] = got_x[rep, g, j, pl.ds(8, 8)] + mixed(
                [mix_x[g, j, pl.ds(8 * k, 8)] for k in range(4)], turns
            )
            if j < nx - 1:
                carry = advance(turns, coef_x, g, nb - 1) + got_x[rep, g, j, pl.ds(0, 8)]
        carry = ending[nx - 1]
        leave = jnp.where(gx == nx - 2, carry, zero)
        for j in range(nx - 2, 0, -1):
            carry = advance(turned(carry), coef_x, g, nb - 1) + ending[j]
            leave = jnp.where(gx == j - 1, carry, leave)
        turns = turned(come)
        starts = [come] + [advance(turns, coef_x, g, n - 1) + before[g, n - 1] for n in range(1, nb)]
        lasts = [None] * nb
        lasts[nb - 1] = leave
        for n in range(nb - 1, 0, -1):
            ending_n = ends_x[g, n] + mixed(
                [block_x[g, j, :, pl.ds(n * 128, 128)] for j in range(4)], turned(starts[n])
            )
            lasts[n - 1] = advance(turned(lasts[n]), coef_x, g, 0) + ending_n
        return starts, lasts

    def x_second(gs, rep):
        for g in gs:
            @pl.when(rep == 0)
            def _():
                taken(mix_x.at[g, pl.ds(0, nx - 1)], rmx.at[g])

            taken(got_x.at[rep, g, pl.ds(0, nx - 1)], rx_sem.at[rep, g])
        starts, lasts = zip(*[x_entries(g, rep) for g in gs])
        return seconds(gs, starts, lasts, bx, rx, x_mask)

    def y_first(gs, fields, rep):
        closings, openings = firsts(gs, [across(field) for field in fields], 1, wy, y_mask)
        for g, closing, opening in zip(gs, closings, openings):
            for k in range(owners):
                end_y[rep, g, k] = packed([closing, opening], k)
            got_y[rep, g, gy] = end_y[rep, g, mine]
        for d in range(owners):
            k, other = to_owner(d)

            @pl.when(other)
            def _():
                for g in gs:
                    y_copy(g, rep, k, d).start()

    def y_owner(gs, rep):
        for g in gs:
            @pl.when(rep == 0)
            def _():
                taken(got_m.at[g, pl.ds(0, ny - 1), pl.ds(0, UNIQUE)], rmy.at[g])
                for j in range(1, ny):
                    parts = unfolded(*[got_m[g, j, pl.ds(8 * m, 8)] for m in range(3)])
                    full_y[g, j] = jnp.concatenate(parts, 0)

        for g in gs:
            taken(got_y.at[rep, g, pl.ds(0, ny - 1)], ry_sem.at[rep, g])
        for g in gs:
            starts, ending = [None] * ny, [None] * ny
            carry = got_y[rep, g, 0, pl.ds(0, 8)]
            starts[0] = jnp.zeros_like(carry)
            for j in range(1, ny):
                turns = turned(carry)
                starts[j] = carry
                ending[j] = got_y[rep, g, j, pl.ds(8, 8)] + mixed(
                    [full_y[g, j, pl.ds(8 * m, 8)] for m in range(4)], turns
                )
                if j < ny - 1:
                    carry = advance(turns, coef_y, g, 0) + got_y[rep, g, j, pl.ds(0, 8)]
            last = jnp.zeros_like(carry)
            for j in range(ny - 1, -1, -1):
                back_y[rep, g, j] = jnp.concatenate([starts[j], last], 0)
                if j:
                    last = ending[j] if j == ny - 1 else advance(turned(last), coef_y, g, 0) + ending[j]
            come_y[rep, g, mine] = back_y[rep, g, gy]
        for g in gs:
            for d in range(1, ny):
                b_copy(g, rep, d).start()

    def y_entries(g, rep):
        starts, lasts = [None] * (rows // 128), [None] * (rows // 128)
        for k in range(owners):
            t, off = (k * share) // 128, (k * share) % 128
            start = slide(come_y[rep, g, k, pl.ds(0, 8)], off)
            last = slide(come_y[rep, g, k, pl.ds(8, 8)], off)
            if off == 0:
                starts[t], lasts[t] = start, last
            else:
                starts[t] = jnp.where(lane >= off, start, starts[t])
                lasts[t] = jnp.where(lane >= off, last, lasts[t])
        return starts, lasts

    def y_second(gs, rep):
        for count, role in ((owners - 1, is_owner), (owners, jnp.logical_not(is_owner))):
            @pl.when(role)
            def _():
                for g in gs:
                    taken(come_y.at[rep, g, pl.ds(0, count)], rb.at[rep, g])

        starts, lasts = zip(*[y_entries(g, rep) for g in gs])
        return seconds(gs, starts, lasts, by, ry, y_mask)

    def each(body, team=1):
        def step(s, c):
            body([team * s + n for n in range(team)])
            return c

        lax.fori_loop(0, groups // team, step, 0)

    sources = ((sea_hbm, sea), (inc_hbm, inc), (dev_hbm, dev))

    def incoming(l, n):
        src, dst = sources[n]
        return pltpu.make_async_copy(src.at[l], dst.at[l], in_sem.at[n, l])

    few = [
        pltpu.make_async_copy(src, dst, few_sem.at[n])
        for n, (src, dst) in enumerate(((steps_hbm, steps), (rate_x_hbm, rate_x), (rate_y_hbm, rate_y)))
    ]
    for copy in few:
        copy.start()
    for l in range(levels):
        for n in range(3):
            incoming(l, n).start()

    lags = (
        lax.broadcasted_iota(jnp.int32, (SIDE, SIDE), 0) - lax.broadcasted_iota(jnp.int32, (SIDE, SIDE), 1)
    ).astype(f32)

    def shape_of(lag):
        span = jnp.maximum(lag, 0.0)
        return span, jnp.where(lag > -0.5, (span + 1.0) * (span + 2.0) * (span + 3.0) / 6.0, 0.0)

    near = (shape_of(lags), shape_of(-lags))

    def tile(shape, rate, weight):
        weight4 = weight * weight * weight * weight
        weight4 = jnp.concatenate([weight4] * (SIDE // 8), 0)
        return split(weight4 * shape[1] * jnp.exp(-rate * shape[0]))

    def by_row(values, i):
        total = jnp.zeros(row.shape, f32)
        for k, value in enumerate(values):
            total = jnp.where(row == k + 4 * i, value, total)
        return total

    def powers(weight):
        return [jnp.ones_like(weight), weight, weight * weight, weight * weight * weight]

    def final_of(i, places, rate, weight):
        pw, leave = powers(weight), binomials(places + 1.0)
        return by_row([weight * pw[k] * leave[k] for k in range(4)], i) * jnp.exp(-rate * places)

    def answer_of(i, places, rate, weight):
        pw, ahead = powers(weight), places + 1.0
        come = binomials(ahead)
        return by_row([pw[3 - k] * come[3 - k] for k in range(4)], i) * jnp.exp(-rate * ahead)

    def high_low(value):
        high = value.astype(bf16).astype(f32)
        return high, value - high

    def finals(i, back, rate, weight):
        over = lane.astype(f32)
        high, low = high_low(final_of(i, over if back else SIDE - 1.0 - over, rate, weight))
        return jnp.concatenate([high, low], 0).astype(bf16)

    def answers(i, back, rate, weight):
        over = lane.astype(f32)
        high, low = high_low(answer_of(i, SIDE - 1.0 - over if back else over, rate, weight))
        return [high, high, low, jnp.zeros_like(high)]

    def filters(first, second, reply, g, rates, weights):
        zero = jnp.zeros((SIDE, SIDE), bf16)
        lower, upper = pl.ds(0, SIDE), pl.ds(SIDE, SIDE)
        replies = []
        for i in range(PAIR):
            l = PAIR * g + i
            rate, weight = rates[i], weights[i]
            high, low = tile(near[0], rate, weight)
            first[l, lower, lower] = high
            first[l, lower, upper] = high
            first[l, upper, lower] = low
            first[l, upper, upper] = zero
            high, low = tile(near[1], rate, weight)
            second[l, :, lower] = high
            second[l, :, upper] = high
            second[l, :, pl.ds(2 * SIDE, SIDE)] = low
            for back in (0, 1):
                final = finals(i, back, rate, weight)
                first[l, pl.ds(2 * SIDE + 16 * back, 16), lower] = final
                first[l, pl.ds(2 * SIDE + 16 * back, 16), upper] = final
                replies += answers(i, back, rate, weight)
        turn = jnp.concatenate(replies, 0).T
        for i in range(PAIR):
            l = PAIR * g + i
            for back in (0, 1):
                part = slide(turn, -32 * (2 * i + back))[:, :32].astype(bf16)
                if back:
                    second[l, :, pl.ds(3 * SIDE, 32)] = part
                else:
                    reply[l] = part

    def products(i, places, rate, weight):
        final = final_of(i, places, rate, weight)
        turns = turned(answer_of(i, places, rate, weight))
        parts = []
        for j in range(4):
            turn = turns[0] if j == 0 else jnp.where(place >= j, turns[j], pltpu.roll(turns[0], j + 4, 0))
            parts += list(high_low(final * turn))
        return jnp.concatenate(parts, 0).astype(bf16)

    def coefs(coef, g, spans, rates, weights):
        low = row < 4
        rate = jnp.where(low, rates[0], rates[1])
        weight = jnp.where(low, weights[0], weights[1])
        power = (jnp.ones_like(weight), weight, weight * weight, weight * weight * weight)
        for n, span in enumerate(spans):
            fall = jnp.exp(-rate * span)
            count = (1.0, span, span * (span + 1.0) / 2.0, span * (span + 1.0) * (span + 2.0) / 6.0)
            for j in range(4):
                coef[g, 4 * n + j] = jnp.where(place >= j, fall * (power[j] * count[j]), 0.0)

    def build_x(g):
        two = [PAIR * g + i for i in range(PAIR)]
        rates = [rate_x[l] for l in two]
        weights = [section_gain(rate_x[l], steps[l]) for l in two]
        filters(wx, bx, rx, g, rates, weights)
        for i, l in enumerate(two):
            for b in range(nb):
                places = lane.astype(f32) + float(b * SIDE)
                tx[l, :, pl.ds(b * SIDE, SIDE)] = products(i, places, rates[i], weights[i])
        spans = [float(SIDE * n) for n in range(1, nb)] + [float(rows)]
        coefs(coef_x, g, spans, rates, weights)

    def build_y(g):
        two = [PAIR * g + i for i in range(PAIR)]
        rates = [rate_y[l] for l in two]
        weights = [section_gain(rate_y[l], steps[l]) for l in two]
        filters(wy, by, ry, g, rates, weights)
        for i, l in enumerate(two):
            ty[l, pl.ds(0, SIDE)] = jnp.where(lags == 0.0, 1.0, 0.0).astype(bf16)
            ty[l, pl.ds(SIDE, 64)] = products(i, lane.astype(f32), rates[i], weights[i])
        coefs(coef_y, g, [float(cols)], rates, weights)

    barrier = pltpu.get_barrier_semaphore()
    for d in range(1, nx):
        pl.semaphore_signal(barrier, inc=1, device_id=x_peer(d), device_id_type=MESH)
    for d in range(1, ny):
        pl.semaphore_signal(barrier, inc=1, device_id=y_peer(d), device_id_type=MESH)

    for copy in few:
        copy.wait()
    each(lambda gs: [build_x(g) for g in gs], 2)

    def four(wide):
        return [halves(wide[16 * j:16 * j + 16]) for j in range(4)]

    def begin_x(gs):
        device, block = [None] * len(gs), [None] * len(gs)
        for n, l in of(gs):
            incoming(l, 0).wait()
        for n, l in of(gs):
            mask = sea[l].astype(f32)
            wet[l] = mask
            mask = mask.astype(bf16)
            device[n] = plus(device[n], dot(tx[l], mask))
            block[n] = plus(block[n], dot(tx[l, :, pl.ds(0, SIDE)], blocks(mask)))
        for n, g in enumerate(gs):
            mix_x[g, gx] = jnp.concatenate(four(device[n]), 0)
            for j, part in enumerate(four(block[n])):
                block_x[g, j] = part

        @pl.when(gs[0] == 0)
        def _():
            pl.semaphore_wait(barrier, nx + ny - 2)

        for g in gs:
            for d in range(1, nx):
                mx_copy(g, d).start()
        for n, l in of(gs):
            for m in (1, 2):
                incoming(l, m).wait()
        x_first(gs, [stack(blocks(dev[l] * wet[l] * inc[l])) for n, l in of(gs)], 0, 0)

    def begin_y(gs):
        for g in gs:
            build_y(g)
        mixes = [None] * len(gs)
        for n, l in of(gs):
            both = dot(ty[l], wet[l].astype(bf16), 1, 1)
            wet_t[l] = both[:SIDE]
            mixes[n] = plus(mixes[n], both[SIDE:])
        for n, g in enumerate(gs):
            parts = [tiles(part) for part in folded(four(mixes[n]))]
            for k in range(owners):
                mix_y[g, k] = packed(parts, k)
            got_m[g, gy] = mix_y[g, mine]
        for d in range(owners):
            k, other = to_owner(d)

            @pl.when(other)
            def _():
                for g in gs:
                    my_copy(g, k, d).start()

    def begin(gs):
        begin_x(gs)
        begin_y(gs)

    each(begin, 2)

    def repetition(rep, c):
        each(lambda gs: y_first(gs, x_second(gs, rep), rep), 1)
        @pl.when(is_owner)
        def _():
            each(lambda gs: y_owner(gs, rep), 1)


        @pl.when(rep < MAXSTEPS - 1)
        def _():
            def more(gs):
                fields = y_second(gs, rep)
                for (n, l), field in zip(of(gs), fields):
                    kept[l] = field
                x_first(gs, [across(field) for field in fields], 1, rep + 1)

            each(more, 1)

        @pl.when(rep == MAXSTEPS - 1)
        def _():
            def last(gs):
                fields = y_second(gs, rep)
                for (n, l), field in zip(of(gs), fields):
                    field = jnp.where(steps[l] > rep, field, kept[l])
                    for b in range(nb):
                        own = pl.ds(b * SIDE, SIDE)
                        out[l, own] = dev[l, own] * field[:, b * SIDE:(b + 1) * SIDE].T

            each(last, 1)

        return c

    lax.fori_loop(0, MAXSTEPS, repetition, 0)

    for d in range(1, nx):
        taken(mix_x.at[:, 0], smx.at[d - 1])
        for rep in range(MAXSTEPS):
            taken(end_x.at[rep], sx.at[rep, d - 1])
    for d in range(owners):
        k, other = to_owner(d)

        @pl.when(other)
        def _():
            taken(mix_y.at[:, 0, pl.ds(0, UNIQUE)], smy.at[d])
            for rep in range(MAXSTEPS):
                taken(end_y.at[rep, :, 0], sy.at[rep, d])

    @pl.when(is_owner)
    def _():
        for d in range(1, ny):
            for rep in range(MAXSTEPS):
                taken(back_y.at[rep, :, 0], sb.at[rep, d - 1])


def on_device(nx, ny, increment, deviation, land_sea, filter_steps, zonal_rate, meridional_rate):
    levels, rows, cols = increment.shape
    nb = rows // SIDE
    groups = levels // PAIR
    hbm = pl.BlockSpec(memory_space=pltpu.HBM)
    vmem = pl.BlockSpec(memory_space=pltpu.VMEM)
    reps = MAXSTEPS
    dma = pltpu.SemaphoreType.DMA
    return pl.pallas_call(
        functools.partial(kernel, nx, ny, levels, rows, cols),
        out_shape=jax.ShapeDtypeStruct(increment.shape, f32),
        in_specs=[hbm] * 6,
        out_specs=vmem,
        scratch_shapes=[
            pltpu.SMEM((levels,), jnp.int32),
            pltpu.SMEM((levels,), f32),
            pltpu.SMEM((levels,), f32),
            pltpu.VMEM((levels, 2 * SIDE + 32, 2 * SIDE), bf16),
            pltpu.VMEM((levels, SIDE, 3 * SIDE + 32), bf16),
            pltpu.VMEM((levels, SIDE, 32), bf16),
            pltpu.VMEM((levels, 2 * SIDE + 32, 2 * SIDE), bf16),
            pltpu.VMEM((levels, SIDE, 3 * SIDE + 32), bf16),
            pltpu.VMEM((levels, SIDE, 32), bf16),
            pltpu.VMEM((levels, 64, rows), bf16),
            pltpu.VMEM((levels, SIDE + 64, cols), bf16),
            pltpu.VMEM((groups, 4 * nb, 8, 128), f32),
            pltpu.VMEM((groups, 4, 8, 128), f32),
            pltpu.VMEM((levels, SIDE, nb * cols), f32),
            pltpu.VMEM((groups, nb - 1, 8, cols), f32),
            pltpu.VMEM((groups, nb, 8, cols), f32),
            pltpu.VMEM((groups, 4, 8, nb * cols), f32),
            pltpu.VMEM((groups, nx, 32, cols), f32),
            pltpu.VMEM((groups, ny // 2, 24, 128), f32),
            pltpu.VMEM((groups, ny, 24, 128), f32),
            pltpu.VMEM((groups, ny, 32, 128), f32),
            pltpu.VMEM((reps, groups, 16, cols), f32),
            pltpu.VMEM((reps, groups, nx, 16, cols), f32),
            pltpu.VMEM((reps, groups, ny // 2, 16, 128), f32),
            pltpu.VMEM((reps, groups, ny, 16, 128), f32),
            pltpu.VMEM((reps, groups, ny, 16, 128), f32),
            pltpu.VMEM((reps, groups, ny // 2, 16, 128), f32),
            pltpu.VMEM((levels, rows, cols), f32),
            pltpu.VMEM((levels, rows, cols), f32),
            pltpu.VMEM((levels, rows, cols), jnp.int32),
            pltpu.VMEM((levels, rows, cols), f32),
            pltpu.VMEM((levels, cols, rows), f32),
            pltpu.VMEM((levels, cols, rows), f32),
            dma((nx - 1,)),
            dma((groups,)),
            dma((ny // 2,)),
            dma((groups,)),
            dma((reps, nx - 1)),
            dma((reps, groups)),
            dma((reps, ny // 2)),
            dma((reps, groups)),
            dma((reps, ny - 1)),
            dma((reps, groups)),
            dma((3, levels)),
            dma((3,)),
        ],
        compiler_params=pltpu.CompilerParams(
            collective_id=0, has_side_effects=True, vmem_limit_bytes=40 * 1024 * 1024
        ),
    )(
        *(
            pltpu.with_memory_space_constraint(a, pltpu.HBM)
            for a in (filter_steps, zonal_rate, meridional_rate, increment, deviation, land_sea)
        )
    )


def solution(mesh):
    placed = (P(None, "gx", "gy"), P(None, "gx", "gy"), P(None, "gx", "gy"), P(), P(), P())
    body = functools.partial(on_device, mesh.shape["gx"], mesh.shape["gy"])
    return jax.shard_map(
        body, mesh=mesh, in_specs=placed, out_specs=P(None, "gx", "gy"), check_vma=False
    )
```

```python
import functools

import jax
import jax.numpy as jnp
from jax import lax
from jax.experimental import pallas as pl
from jax.experimental.pallas import tpu as pltpu
from jax.sharding import PartitionSpec as P

SIDE = 128
PAIR = 2
TEAM = 2
UNIQUE = 20
MAXSTEPS = 2
gain_base = 3.0**0.125
MESH = pl.DeviceIdType.MESH
f32, bf16 = jnp.float32, jnp.bfloat16


def section_gain(decay_rate, filter_steps):
    rate = jnp.full((8, 128), decay_rate)
    count = jnp.full((8, 128), filter_steps.astype(f32))
    series = jnp.ones_like(rate)
    for n in range(9, 1, -1):
        series = 1.0 - series * rate * (1.0 / n)
    fading = jnp.where(rate < 0.5, rate * series, 1.0 - jnp.exp(-rate))
    return gain_base * jnp.exp((1.0 - 1.0 / (16.0 * count)) * jnp.log(fading))


def binomials(count):
    return (
        jnp.ones_like(count),
        count,
        count * (count + 1.0) / 2.0,
        count * (count + 1.0) * (count + 2.0) / 6.0,
    )


def split(value):
    high = value.astype(bf16)
    return high, (value - high.astype(f32)).astype(bf16)


def three(state):
    high = state.astype(bf16).astype(f32)
    return jnp.concatenate([high, state - high, high, jnp.zeros_like(high)], 0).astype(bf16)


def dot(a, b, ca=1, cb=0):
    return lax.dot_general(a, b, (((ca,), (cb,)), ((), ())), preferred_element_type=f32)


def kernel(
    nx, ny, levels, rows, cols,
    steps_hbm, rate_x_hbm, rate_y_hbm,
    inc_hbm, dev_hbm, sea_hbm,
    out,
    steps, rate_x, rate_y,
    wx, bx, rx, wy, by, ry, tx, ty, coef_x, coef_y,
    inside, before, ends_x, block_x, mix_x, mix_y, got_m, full_y,
    end_x, got_x, end_y, got_y, back_y, come_y, inc, dev, sea, wet, wet_t, kept,
    smx, rmx, smy, rmy, sx, rx_sem, sy, ry_sem, sb, rb, in_sem, few_sem,
):
    gx, gy = lax.axis_index("gx"), lax.axis_index("gy")
    nb = rows // SIDE
    groups = levels // PAIR
    owners = ny // 2
    least = ny // 4
    share = rows // owners
    mine = jnp.clip(gy - least, 0, owners - 1)
    is_owner = (gy >= least) & (gy < least + owners)
    row = lax.broadcasted_iota(jnp.int32, (8, 128), 0)
    lane = lax.broadcasted_iota(jnp.int32, (8, 128), 1)
    place = jnp.where(row < 4, row, row - 4)

    def turned(state):
        return [state] + [pltpu.roll(state, j, 0) for j in range(1, 4)]

    def advance(turns, coef, g, index):
        total = None
        for j in range(4):
            term = coef[g, 4 * index + j] * turns[j]
            total = term if total is None else total + term
        return total

    def mixed(mix, turns):
        total = mix[0] * turns[0]
        for j in range(1, 4):
            total += mix[j] * jnp.where(place >= j, turns[j], pltpu.roll(turns[0], j + 4, 0))
        return total

    def slide(tile, count):
        count = count % 128
        return pltpu.roll(tile, count, 1) if count else tile

    def x_peer(d):
        return (lax.rem(gx + d, nx), gy)

    def y_peer(d):
        return (gx, lax.rem(gy + d, ny))

    def mx_copy(g, d):
        return pltpu.make_async_remote_copy(
            src_ref=mix_x.at[g, gx], dst_ref=mix_x.at[g, gx],
            send_sem=smx.at[d - 1], recv_sem=rmx.at[g],
            device_id=x_peer(d), device_id_type=MESH,
        )

    def to_owner(d):
        k = jnp.where(gy < ny // 2, owners - 1 - d, d)
        return k, least + k != gy

    def my_copy(g, k, d):
        return pltpu.make_async_remote_copy(
            src_ref=mix_y.at[g, k, pl.ds(0, UNIQUE)], dst_ref=got_m.at[g, gy, pl.ds(0, UNIQUE)],
            send_sem=smy.at[d], recv_sem=rmy.at[g],
            device_id=(gx, least + k), device_id_type=MESH,
        )

    def x_copy(g, rep, d):
        return pltpu.make_async_remote_copy(
            src_ref=end_x.at[rep, g], dst_ref=got_x.at[rep, g, gx],
            send_sem=sx.at[rep, d - 1], recv_sem=rx_sem.at[rep, g],
            device_id=x_peer(d), device_id_type=MESH,
        )

    def y_copy(g, rep, k, d):
        return pltpu.make_async_remote_copy(
            src_ref=end_y.at[rep, g, k], dst_ref=got_y.at[rep, g, gy],
            send_sem=sy.at[rep, d], recv_sem=ry_sem.at[rep, g],
            device_id=(gx, least + k), device_id_type=MESH,
        )

    def b_copy(g, rep, d):
        far = ny - d - (d >= ny - gy).astype(jnp.int32)
        near = d - 1 + (d > gy).astype(jnp.int32)
        target = jnp.where(gy < ny // 2, far, near)
        return pltpu.make_async_remote_copy(
            src_ref=back_y.at[rep, g, target], dst_ref=come_y.at[rep, g, mine],
            send_sem=sb.at[rep, d - 1], recv_sem=rb.at[rep, g],
            device_id=(gx, target), device_id_type=MESH,
        )

    def taken(ref, sem):
        pltpu.make_async_copy(ref, ref, sem).wait()

    def blocks(value):
        return jnp.concatenate([value[b * SIDE:(b + 1) * SIDE] for b in range(nb)], 1)

    def unblock(wide):
        return jnp.concatenate([wide[:, b * cols:(b + 1) * cols] for b in range(nb)], 0)

    def stack(value):
        return jnp.concatenate(split(value), 0)

    def across(wide):
        high, low = split(wide)
        return jnp.concatenate([unblock(high), unblock(low)], 1)

    def of(gs):
        return [(n, PAIR * g + i) for n, g in enumerate(gs) for i in range(PAIR)]

    def x_mask(l):
        return blocks(wet[l])

    def y_mask(l):
        return wet_t[l]

    def firsts(gs, rhs, dim, weights, mask_of):
        closing, opening = [None] * len(gs), [None] * len(gs)
        masked = []
        wides = [dot(weights[l, pl.ds(0, 2 * SIDE + 16), :], side, 1, dim) for (n, l), side in zip(of(gs), rhs)]
        for (n, l), both in zip(of(gs), wides):
            held = both[:SIDE] + both[SIDE:2 * SIDE]
            inside[l] = held
            closing[n] = plus(closing[n], halves(both[2 * SIDE:]))
            masked.append(stack(held * mask_of(l)))
        for (n, l), side in zip(of(gs), masked):
            opening[n] = plus(opening[n], halves(dot(weights[l, pl.ds(2 * SIDE + 16, 16), :], side)))
        return [tiles(value) for value in closing], [tiles(value) for value in opening]

    def seconds(gs, starts, lasts, weights, answers, mask_of):
        ahead = [three(jnp.concatenate(tile, 1)) for tile in starts]
        behind = [three(jnp.concatenate(tile, 1)) for tile in lasts]
        sides = []
        for n, l in of(gs):
            field = (inside[l] + dot(answers[l], ahead[n])) * mask_of(l)
            high, low = split(field)
            sides.append(jnp.concatenate([high, low, high, behind[n]], 0))
        return [dot(weights[l], side) * mask_of(l) for (n, l), side in zip(of(gs), sides)]

    def halves(both):
        return both[:8] + both[8:16]

    def tiles(wide):
        return [wide[:, t * 128:(t + 1) * 128] for t in range(wide.shape[1] // 128)]

    def plus(total, piece):
        return piece if total is None else total + piece

    def folded(mix):
        def one(m0, m1, m2, m3):
            both = jnp.where(place < 2, m0, jnp.where(place == 2, pltpu.roll(m2, 2, 0), pltpu.roll(m2, 1, 0)))
            return both, jnp.where(place < 3, m1, m3), jnp.where(row < 2, m3, pltpu.roll(m3, 6, 0))

        found = [one(*each_tile) for each_tile in zip(*[tiles(part) for part in mix])]
        return [jnp.concatenate(part, 1) for part in zip(*found)]

    def unfolded(t0, t1, t2):
        m0 = jnp.where(place == 2, pltpu.roll(t0, 1, 0), jnp.where(place == 3, pltpu.roll(t0, 3, 0), t0))
        m1 = jnp.where(place == 3, pltpu.roll(t1, 2, 0), t1)
        m2 = jnp.where(place == 0, pltpu.roll(t0, 6, 0), jnp.where(place < 3, pltpu.roll(t0, 7, 0), t0))
        m3 = jnp.where(row < 2, t2, jnp.where(row < 6, pltpu.roll(t2, 2, 0), pltpu.roll(t2, 4, 0)))
        return [m0, m1, m2, jnp.where(place == 3, t1, m3)]

    def packed(parts, k):
        t, off = (k * share) // 128, (k * share) % 128
        return jnp.concatenate([slide(part[t], -off) for part in parts], 0)

    def x_first(gs, rhs, dim, rep):
        closings, openings = firsts(gs, rhs, dim, wx, x_mask)
        for g, closing, opening in zip(gs, closings, openings):
            carry = closing[0]
            chain = [opening[0]]
            ends_x[g, 0] = opening[0]
            for n in range(1, nb):
                turns = turned(carry)
                before[g, n - 1] = carry
                ends_x[g, n] = opening[n]
                chain.append(opening[n] + mixed([block_x[g, j, :, pl.ds(n * 128, 128)] for j in range(4)], turns))
                carry = advance(turns, coef_x, g, 0) + closing[n]
            end = chain[-1]
            for n in range(nb - 2, -1, -1):
                end = advance(turned(end), coef_x, g, 0) + chain[n]
            message = jnp.concatenate([carry, end], 0)
            end_x[rep, g] = message
            got_x[rep, g, gx] = message
        for g in gs:
            for d in range(1, nx):
                x_copy(g, rep, d).start()

    def x_entries(g, rep):
        carry = got_x[rep, g, 0, pl.ds(0, 8)]
        zero = jnp.zeros_like(carry)
        come = zero
        ending = [None] * nx
        for j in range(1, nx):
            turns = turned(carry)
            come = jnp.where(gx == j, carry, come)
            ending[j] = got_x[rep, g, j, pl.ds(8, 8)] + mixed(
                [mix_x[g, j, pl.ds(8 * k, 8)] for k in range(4)], turns
            )
            if j < nx - 1:
                carry = advance(turns, coef_x, g, nb - 1) + got_x[rep, g, j, pl.ds(0, 8)]
        carry = ending[nx - 1]
        leave = jnp.where(gx == nx - 2, carry, zero)
        for j in range(nx - 2, 0, -1):
            carry = advance(turned(carry), coef_x, g, nb - 1) + ending[j]
            leave = jnp.where(gx == j - 1, carry, leave)
        turns = turned(come)
        starts = [come] + [advance(turns, coef_x, g, n - 1) + before[g, n - 1] for n in range(1, nb)]
        lasts = [None] * nb
        lasts[nb - 1] = leave
        for n in range(nb - 1, 0, -1):
            ending_n = ends_x[g, n] + mixed(
                [block_x[g, j, :, pl.ds(n * 128, 128)] for j in range(4)], turned(starts[n])
            )
            lasts[n - 1] = advance(turned(lasts[n]), coef_x, g, 0) + ending_n
        return starts, lasts

    def x_second(gs, rep):
        for g in gs:
            @pl.when(rep == 0)
            def _():
                taken(mix_x.at[g, pl.ds(0, nx - 1)], rmx.at[g])

            taken(got_x.at[rep, g, pl.ds(0, nx - 1)], rx_sem.at[rep, g])
        starts, lasts = zip(*[x_entries(g, rep) for g in gs])
        return seconds(gs, starts, lasts, bx, rx, x_mask)

    def y_first(gs, fields, rep):
        closings, openings = firsts(gs, [across(field) for field in fields], 1, wy, y_mask)
        for g, closing, opening in zip(gs, closings, openings):
            for k in range(owners):
                end_y[rep, g, k] = packed([closing, opening], k)
            got_y[rep, g, gy] = end_y[rep, g, mine]
        for d in range(owners):
            k, other = to_owner(d)

            @pl.when(other)
            def _():
                for g in gs:
                    y_copy(g, rep, k, d).start()

    def y_owner(gs, rep):
        for g in gs:
            @pl.when(rep == 0)
            def _():
                taken(got_m.at[g, pl.ds(0, ny - 1), pl.ds(0, UNIQUE)], rmy.at[g])
                for j in range(1, ny):
                    parts = unfolded(*[got_m[g, j, pl.ds(8 * m, 8)] for m in range(3)])
                    full_y[g, j] = jnp.concatenate(parts, 0)

        for g in gs:
            taken(got_y.at[rep, g, pl.ds(0, ny - 1)], ry_sem.at[rep, g])
        for g in gs:
            starts, ending = [None] * ny, [None] * ny
            carry = got_y[rep, g, 0, pl.ds(0, 8)]
            starts[0] = jnp.zeros_like(carry)
            for j in range(1, ny):
                turns = turned(carry)
                starts[j] = carry
                ending[j] = got_y[rep, g, j, pl.ds(8, 8)] + mixed(
                    [full_y[g, j, pl.ds(8 * m, 8)] for m in range(4)], turns
                )
                if j < ny - 1:
                    carry = advance(turns, coef_y, g, 0) + got_y[rep, g, j, pl.ds(0, 8)]
            last = jnp.zeros_like(carry)
            for j in range(ny - 1, -1, -1):
                back_y[rep, g, j] = jnp.concatenate([starts[j], last], 0)
                if j:
                    last = ending[j] if j == ny - 1 else advance(turned(last), coef_y, g, 0) + ending[j]
            come_y[rep, g, mine] = back_y[rep, g, gy]
        for g in gs:
            for d in range(1, ny):
                b_copy(g, rep, d).start()

    def y_entries(g, rep):
        starts, lasts = [None] * (rows // 128), [None] * (rows // 128)
        for k in range(owners):
            t, off = (k * share) // 128, (k * share) % 128
            start = slide(come_y[rep, g, k, pl.ds(0, 8)], off)
            last = slide(come_y[rep, g, k, pl.ds(8, 8)], off)
            if off == 0:
                starts[t], lasts[t] = start, last
            else:
                starts[t] = jnp.where(lane >= off, start, starts[t])
                lasts[t] = jnp.where(lane >= off, last, lasts[t])
        return starts, lasts

    def y_second(gs, rep):
        for count, role in ((owners - 1, is_owner), (owners, jnp.logical_not(is_owner))):
            @pl.when(role)
            def _():
                for g in gs:
                    taken(come_y.at[rep, g, pl.ds(0, count)], rb.at[rep, g])

        starts, lasts = zip(*[y_entries(g, rep) for g in gs])
        return seconds(gs, starts, lasts, by, ry, y_mask)

    def each(body, team=1):
        def step(s, c):
            body([team * s + n for n in range(team)])
            return c

        lax.fori_loop(0, groups // team, step, 0)

    sources = ((sea_hbm, sea), (inc_hbm, inc), (dev_hbm, dev))

    def incoming(s, n):
        src, dst = sources[n]
        own = pl.ds(s * PAIR * TEAM, PAIR * TEAM)
        return pltpu.make_async_copy(src.at[own], dst.at[own], in_sem.at[n, s])

    few = [
        pltpu.make_async_copy(src, dst, few_sem.at[n])
        for n, (src, dst) in enumerate(((steps_hbm, steps), (rate_x_hbm, rate_x), (rate_y_hbm, rate_y)))
    ]
    for copy in few:
        copy.start()
    for s in range(groups // TEAM):
        for n in range(3):
            incoming(s, n).start()

    lags = (
        lax.broadcasted_iota(jnp.int32, (SIDE, SIDE), 0) - lax.broadcasted_iota(jnp.int32, (SIDE, SIDE), 1)
    ).astype(f32)

    def shape_of(lag):
        span = jnp.maximum(lag, 0.0)
        return span, jnp.where(lag > -0.5, (span + 1.0) * (span + 2.0) * (span + 3.0) / 6.0, 0.0)

    near = (shape_of(lags), shape_of(-lags))

    def tile(shape, rate, weight):
        weight4 = weight * weight * weight * weight
        weight4 = jnp.concatenate([weight4] * (SIDE // 8), 0)
        return split(weight4 * shape[1] * jnp.exp(-rate * shape[0]))

    def by_row(values, i):
        total = jnp.zeros(row.shape, f32)
        for k, value in enumerate(values):
            total = jnp.where(row == k + 4 * i, value, total)
        return total

    def powers(weight):
        return [jnp.ones_like(weight), weight, weight * weight, weight * weight * weight]

    def final_of(i, places, rate, weight):
        pw, leave = powers(weight), binomials(places + 1.0)
        return by_row([weight * pw[k] * leave[k] for k in range(4)], i) * jnp.exp(-rate * places)

    def answer_of(i, places, rate, weight):
        pw, ahead = powers(weight), places + 1.0
        come = binomials(ahead)
        return by_row([pw[3 - k] * come[3 - k] for k in range(4)], i) * jnp.exp(-rate * ahead)

    def high_low(value):
        high = value.astype(bf16).astype(f32)
        return high, value - high

    def finals(i, back, rate, weight):
        over = lane.astype(f32)
        high, low = high_low(final_of(i, over if back else SIDE - 1.0 - over, rate, weight))
        return jnp.concatenate([high, low], 0).astype(bf16)

    def answers(i, back, rate, weight):
        over = lane.astype(f32)
        high, low = high_low(answer_of(i, SIDE - 1.0 - over if back else over, rate, weight))
        return [high, high, low, jnp.zeros_like(high)]

    def filters_first(first, g, rates, weights):
        zero = jnp.zeros((SIDE, SIDE), bf16)
        lower, upper = pl.ds(0, SIDE), pl.ds(SIDE, SIDE)
        for i in range(PAIR):
            l = PAIR * g + i
            high, low = tile(near[0], rates[i], weights[i])
            first[l, lower, lower] = high
            first[l, lower, upper] = high
            first[l, upper, lower] = low
            first[l, upper, upper] = zero
            for back in (0, 1):
                final = finals(i, back, rates[i], weights[i])
                first[l, pl.ds(2 * SIDE + 16 * back, 16), lower] = final
                first[l, pl.ds(2 * SIDE + 16 * back, 16), upper] = final

    def filters_second(second, reply, g, rates, weights):
        replies = []
        for i in range(PAIR):
            l = PAIR * g + i
            high, low = tile(near[1], rates[i], weights[i])
            second[l, :, pl.ds(0, SIDE)] = high
            second[l, :, pl.ds(SIDE, SIDE)] = high
            second[l, :, pl.ds(2 * SIDE, SIDE)] = low
            for back in (0, 1):
                replies += answers(i, back, rates[i], weights[i])
        turn = jnp.concatenate(replies, 0).T
        for i in range(PAIR):
            l = PAIR * g + i
            for back in (0, 1):
                part = slide(turn, -32 * (2 * i + back))[:, :32].astype(bf16)
                if back:
                    second[l, :, pl.ds(3 * SIDE, 32)] = part
                else:
                    reply[l] = part

    def products(i, places, rate, weight):
        final = final_of(i, places, rate, weight)
        turns = turned(answer_of(i, places, rate, weight))
        parts = []
        for j in range(4):
            turn = turns[0] if j == 0 else jnp.where(place >= j, turns[j], pltpu.roll(turns[0], j + 4, 0))
            parts += list(high_low(final * turn))
        return jnp.concatenate(parts, 0).astype(bf16)

    def coefs(coef, g, spans, rates, weights):
        low = row < 4
        rate = jnp.where(low, rates[0], rates[1])
        weight = jnp.where(low, weights[0], weights[1])
        power = (jnp.ones_like(weight), weight, weight * weight, weight * weight * weight)
        for n, span in enumerate(spans):
            fall = jnp.exp(-rate * span)
            count = (1.0, span, span * (span + 1.0) / 2.0, span * (span + 1.0) * (span + 2.0) / 6.0)
            for j in range(4):
                coef[g, 4 * n + j] = jnp.where(place >= j, fall * (power[j] * count[j]), 0.0)

    def build_x(g):
        two = [PAIR * g + i for i in range(PAIR)]
        rates = [rate_x[l] for l in two]
        weights = [section_gain(rate_x[l], steps[l]) for l in two]
        filters_first(wx, g, rates, weights)
        filters_second(bx, rx, g, rates, weights)
        for i, l in enumerate(two):
            for b in range(nb):
                places = lane.astype(f32) + float(b * SIDE)
                tx[l, :, pl.ds(b * SIDE, SIDE)] = products(i, places, rates[i], weights[i])
        spans = [float(SIDE * n) for n in range(1, nb)] + [float(rows)]
        coefs(coef_x, g, spans, rates, weights)

    def build_y(g):
        two = [PAIR * g + i for i in range(PAIR)]
        rates = [rate_y[l] for l in two]
        weights = [section_gain(rate_y[l], steps[l]) for l in two]
        filters_first(wy, g, rates, weights)
        for i, l in enumerate(two):
            ty[l, pl.ds(0, SIDE)] = jnp.where(lags == 0.0, 1.0, 0.0).astype(bf16)
            ty[l, pl.ds(SIDE, 64)] = products(i, lane.astype(f32), rates[i], weights[i])
        coefs(coef_y, g, [float(cols)], rates, weights)

    def build_later(g):
        two = [PAIR * g + i for i in range(PAIR)]
        weights = [section_gain(rate_y[l], steps[l]) for l in two]
        filters_second(by, ry, g, [rate_y[l] for l in two], weights)

    barrier = pltpu.get_barrier_semaphore()
    for d in range(1, nx):
        pl.semaphore_signal(barrier, inc=1, device_id=x_peer(d), device_id_type=MESH)
    for d in range(1, ny):
        pl.semaphore_signal(barrier, inc=1, device_id=y_peer(d), device_id_type=MESH)

    for copy in few:
        copy.wait()
    each(lambda gs: [build_x(g) for g in gs], 2)

    def four(wide):
        return [halves(wide[16 * j:16 * j + 16]) for j in range(4)]

    def begin_x(gs):
        device, block = [None] * len(gs), [None] * len(gs)
        incoming(gs[0] // TEAM, 0).wait()
        for n, l in of(gs):
            mask = sea[l].astype(f32)
            wet[l] = mask
            mask = mask.astype(bf16)
            device[n] = plus(device[n], dot(tx[l], mask))
            block[n] = plus(block[n], dot(tx[l, :, pl.ds(0, SIDE)], blocks(mask)))
        for n, g in enumerate(gs):
            mix_x[g, gx] = jnp.concatenate(four(device[n]), 0)
            for j, part in enumerate(four(block[n])):
                block_x[g, j] = part

        @pl.when(gs[0] == 0)
        def _():
            pl.semaphore_wait(barrier, nx + ny - 2)

        for g in gs:
            for d in range(1, nx):
                mx_copy(g, d).start()
        for m in (1, 2):
            incoming(gs[0] // TEAM, m).wait()
        x_first(gs, [stack(blocks(dev[l] * wet[l] * inc[l])) for n, l in of(gs)], 0, 0)

    def begin_y(gs):
        for g in gs:
            build_y(g)
        mixes = [None] * len(gs)
        for n, l in of(gs):
            both = dot(ty[l], wet[l].astype(bf16), 1, 1)
            wet_t[l] = both[:SIDE]
            mixes[n] = plus(mixes[n], both[SIDE:])
        for n, g in enumerate(gs):
            parts = [tiles(part) for part in folded(four(mixes[n]))]
            for k in range(owners):
                mix_y[g, k] = packed(parts, k)
            got_m[g, gy] = mix_y[g, mine]
        for d in range(owners):
            k, other = to_owner(d)

            @pl.when(other)
            def _():
                for g in gs:
                    my_copy(g, k, d).start()

    def begin(gs):
        begin_x(gs)
        begin_y(gs)

    each(begin, TEAM)

    def repetition(rep, c):
        each(lambda gs: y_first(gs, x_second(gs, rep), rep), 1)
        @pl.when(rep == 0)
        def _():
            each(lambda gs: [build_later(g) for g in gs], TEAM)

        @pl.when(is_owner)
        def _():
            each(lambda gs: y_owner(gs, rep), 1)


        @pl.when(rep < MAXSTEPS - 1)
        def _():
            def more(gs):
                fields = y_second(gs, rep)
                for (n, l), field in zip(of(gs), fields):
                    kept[l] = field
                x_first(gs, [across(field) for field in fields], 1, rep + 1)

            each(more, 1)

        @pl.when(rep == MAXSTEPS - 1)
        def _():
            def last(gs):
                fields = y_second(gs, rep)
                for (n, l), field in zip(of(gs), fields):
                    field = jnp.where(steps[l] > rep, field, kept[l])
                    for b in range(nb):
                        own = pl.ds(b * SIDE, SIDE)
                        out[l, own] = dev[l, own] * field[:, b * SIDE:(b + 1) * SIDE].T

            each(last, 1)

        return c

    lax.fori_loop(0, MAXSTEPS, repetition, 0)

    for d in range(1, nx):
        taken(mix_x.at[:, 0], smx.at[d - 1])
        for rep in range(MAXSTEPS):
            taken(end_x.at[rep], sx.at[rep, d - 1])
    for d in range(owners):
        k, other = to_owner(d)

        @pl.when(other)
        def _():
            taken(mix_y.at[:, 0, pl.ds(0, UNIQUE)], smy.at[d])
            for rep in range(MAXSTEPS):
                taken(end_y.at[rep, :, 0], sy.at[rep, d])

    @pl.when(is_owner)
    def _():
        for d in range(1, ny):
            for rep in range(MAXSTEPS):
                taken(back_y.at[rep, :, 0], sb.at[rep, d - 1])


def on_device(nx, ny, increment, deviation, land_sea, filter_steps, zonal_rate, meridional_rate):
    levels, rows, cols = increment.shape
    nb = rows // SIDE
    groups = levels // PAIR
    hbm = pl.BlockSpec(memory_space=pltpu.HBM)
    vmem = pl.BlockSpec(memory_space=pltpu.VMEM)
    reps = MAXSTEPS
    dma = pltpu.SemaphoreType.DMA
    return pl.pallas_call(
        functools.partial(kernel, nx, ny, levels, rows, cols),
        out_shape=jax.ShapeDtypeStruct(increment.shape, f32),
        in_specs=[hbm] * 6,
        out_specs=vmem,
        scratch_shapes=[
            pltpu.SMEM((levels,), jnp.int32),
            pltpu.SMEM((levels,), f32),
            pltpu.SMEM((levels,), f32),
            pltpu.VMEM((levels, 2 * SIDE + 32, 2 * SIDE), bf16),
            pltpu.VMEM((levels, SIDE, 3 * SIDE + 32), bf16),
            pltpu.VMEM((levels, SIDE, 32), bf16),
            pltpu.VMEM((levels, 2 * SIDE + 32, 2 * SIDE), bf16),
            pltpu.VMEM((levels, SIDE, 3 * SIDE + 32), bf16),
            pltpu.VMEM((levels, SIDE, 32), bf16),
            pltpu.VMEM((levels, 64, rows), bf16),
            pltpu.VMEM((levels, SIDE + 64, cols), bf16),
            pltpu.VMEM((groups, 4 * nb, 8, 128), f32),
            pltpu.VMEM((groups, 4, 8, 128), f32),
            pltpu.VMEM((levels, SIDE, nb * cols), f32),
            pltpu.VMEM((groups, nb - 1, 8, cols), f32),
            pltpu.VMEM((groups, nb, 8, cols), f32),
            pltpu.VMEM((groups, 4, 8, nb * cols), f32),
            pltpu.VMEM((groups, nx, 32, cols), f32),
            pltpu.VMEM((groups, ny // 2, 24, 128), f32),
            pltpu.VMEM((groups, ny, 24, 128), f32),
            pltpu.VMEM((groups, ny, 32, 128), f32),
            pltpu.VMEM((reps, groups, 16, cols), f32),
            pltpu.VMEM((reps, groups, nx, 16, cols), f32),
            pltpu.VMEM((reps, groups, ny // 2, 16, 128), f32),
            pltpu.VMEM((reps, groups, ny, 16, 128), f32),
            pltpu.VMEM((reps, groups, ny, 16, 128), f32),
            pltpu.VMEM((reps, groups, ny // 2, 16, 128), f32),
            pltpu.VMEM((levels, rows, cols), f32),
            pltpu.VMEM((levels, rows, cols), f32),
            pltpu.VMEM((levels, rows, cols), jnp.int32),
            pltpu.VMEM((levels, rows, cols), f32),
            pltpu.VMEM((levels, cols, rows), f32),
            pltpu.VMEM((levels, cols, rows), f32),
            dma((nx - 1,)),
            dma((groups,)),
            dma((ny // 2,)),
            dma((groups,)),
            dma((reps, nx - 1)),
            dma((reps, groups)),
            dma((reps, ny // 2)),
            dma((reps, groups)),
            dma((reps, ny - 1)),
            dma((reps, groups)),
            dma((3, groups // TEAM)),
            dma((3,)),
        ],
        compiler_params=pltpu.CompilerParams(
            collective_id=0, has_side_effects=True, vmem_limit_bytes=40 * 1024 * 1024
        ),
    )(
        *(
            pltpu.with_memory_space_constraint(a, pltpu.HBM)
            for a in (filter_steps, zonal_rate, meridional_rate, increment, deviation, land_sea)
        )
    )


def solution(mesh):
    placed = (P(None, "gx", "gy"), P(None, "gx", "gy"), P(None, "gx", "gy"), P(), P(), P())
    body = functools.partial(on_device, mesh.shape["gx"], mesh.shape["gy"])
    return jax.shard_map(
        body, mesh=mesh, in_specs=placed, out_specs=P(None, "gx", "gy"), check_vma=False
    )
```

```python
import functools

import jax
import jax.numpy as jnp
from jax import lax
from jax.experimental import pallas as pl
from jax.experimental.pallas import tpu as pltpu
from jax.sharding import PartitionSpec as P

SIDE = 128
PAIR = 2
TEAM = 2
UNIQUE = 20
MAXSTEPS = 2
gain_base = 3.0**0.125
MESH = pl.DeviceIdType.MESH
f32, bf16 = jnp.float32, jnp.bfloat16


def section_gain(decay_rate, filter_steps):
    rate = jnp.full((8, 128), decay_rate)
    count = jnp.full((8, 128), filter_steps.astype(f32))
    series = jnp.ones_like(rate)
    for n in range(9, 1, -1):
        series = 1.0 - series * rate * (1.0 / n)
    fading = jnp.where(rate < 0.5, rate * series, 1.0 - jnp.exp(-rate))
    return gain_base * jnp.exp((1.0 - 1.0 / (16.0 * count)) * jnp.log(fading))


def binomials(count):
    return (
        jnp.ones_like(count),
        count,
        count * (count + 1.0) / 2.0,
        count * (count + 1.0) * (count + 2.0) / 6.0,
    )


def split(value):
    high = value.astype(bf16)
    return high, (value - high.astype(f32)).astype(bf16)


def three(state):
    high = state.astype(bf16).astype(f32)
    return jnp.concatenate([high, state - high, high, jnp.zeros_like(high)], 0).astype(bf16)


def dot(a, b, ca=1, cb=0):
    return lax.dot_general(a, b, (((ca,), (cb,)), ((), ())), preferred_element_type=f32)


def kernel(
    nx, ny, levels, rows, cols,
    steps_hbm, rate_x_hbm, rate_y_hbm,
    inc_hbm, dev_hbm, sea_hbm,
    out,
    steps, rate_x, rate_y,
    wx, bx, rx, wy, by, ry, tx, ty, coef_x, coef_y,
    inside, before, ends_x, block_x, mix_x, mix_y, got_m, full_y,
    end_x, got_x, end_y, got_y, back_y, come_y, inc, dev, sea, wet, wet_t, kept,
    smx, rmx, smy, rmy, sx, rx_sem, sy, ry_sem, sb, rb, in_sem, few_sem,
):
    gx, gy = lax.axis_index("gx"), lax.axis_index("gy")
    nb = rows // SIDE
    groups = levels // PAIR
    owners = ny // 2
    least = ny // 4
    share = rows // owners
    mine = jnp.clip(gy - least, 0, owners - 1)
    is_owner = (gy >= least) & (gy < least + owners)
    row = lax.broadcasted_iota(jnp.int32, (8, 128), 0)
    lane = lax.broadcasted_iota(jnp.int32, (8, 128), 1)
    place = jnp.where(row < 4, row, row - 4)

    def turned(state):
        return [state] + [pltpu.roll(state, j, 0) for j in range(1, 4)]

    def advance(turns, coef, g, index):
        total = None
        for j in range(4):
            term = coef[g, 4 * index + j] * turns[j]
            total = term if total is None else total + term
        return total

    def mixed(mix, turns):
        total = mix[0] * turns[0]
        for j in range(1, 4):
            total += mix[j] * jnp.where(place >= j, turns[j], pltpu.roll(turns[0], j + 4, 0))
        return total

    def slide(tile, count):
        count = count % 128
        return pltpu.roll(tile, count, 1) if count else tile

    def x_peer(d):
        return (lax.rem(gx + d, nx), gy)

    def y_peer(d):
        return (gx, lax.rem(gy + d, ny))

    def mx_copy(g, d):
        return pltpu.make_async_remote_copy(
            src_ref=mix_x.at[g, gx], dst_ref=mix_x.at[g, gx],
            send_sem=smx.at[d - 1], recv_sem=rmx.at[g],
            device_id=x_peer(d), device_id_type=MESH,
        )

    def to_owner(d):
        k = jnp.where(gy < ny // 2, owners - 1 - d, d)
        return k, least + k != gy

    def my_copy(g, k, d):
        return pltpu.make_async_remote_copy(
            src_ref=mix_y.at[g, k, pl.ds(0, UNIQUE)], dst_ref=got_m.at[g, gy, pl.ds(0, UNIQUE)],
            send_sem=smy.at[d], recv_sem=rmy.at[g],
            device_id=(gx, least + k), device_id_type=MESH,
        )

    def x_copy(g, rep, d):
        return pltpu.make_async_remote_copy(
            src_ref=end_x.at[rep, g], dst_ref=got_x.at[rep, g, gx],
            send_sem=sx.at[rep, d - 1], recv_sem=rx_sem.at[rep, g],
            device_id=x_peer(d), device_id_type=MESH,
        )

    def y_copy(g, rep, k, d):
        return pltpu.make_async_remote_copy(
            src_ref=end_y.at[rep, g, k], dst_ref=got_y.at[rep, g, gy],
            send_sem=sy.at[rep, d], recv_sem=ry_sem.at[rep, g],
            device_id=(gx, least + k), device_id_type=MESH,
        )

    def b_copy(g, rep, d):
        far = ny - d - (d >= ny - gy).astype(jnp.int32)
        near = d - 1 + (d > gy).astype(jnp.int32)
        target = jnp.where(gy < ny // 2, far, near)
        return pltpu.make_async_remote_copy(
            src_ref=back_y.at[rep, g, target], dst_ref=come_y.at[rep, g, mine],
            send_sem=sb.at[rep, d - 1], recv_sem=rb.at[rep, g],
            device_id=(gx, target), device_id_type=MESH,
        )

    def taken(ref, sem):
        pltpu.make_async_copy(ref, ref, sem).wait()

    def blocks(value):
        return jnp.concatenate([value[b * SIDE:(b + 1) * SIDE] for b in range(nb)], 1)

    def unblock(wide):
        return jnp.concatenate([wide[:, b * cols:(b + 1) * cols] for b in range(nb)], 0)

    def stack(value):
        return jnp.concatenate(split(value), 0)

    def across(wide):
        high, low = split(wide)
        return jnp.concatenate([unblock(high), unblock(low)], 1)

    def of(gs):
        return [(n, PAIR * g + i) for n, g in enumerate(gs) for i in range(PAIR)]

    def x_mask(l):
        return blocks(wet[l])

    def y_mask(l):
        return wet_t[l]

    def firsts(gs, rhs, dim, weights, mask_of):
        closing, opening = [None] * len(gs), [None] * len(gs)
        masked = []
        wides = [dot(weights[l, pl.ds(0, 2 * SIDE + 16), :], side, 1, dim) for (n, l), side in zip(of(gs), rhs)]
        for (n, l), both in zip(of(gs), wides):
            held = both[:SIDE] + both[SIDE:2 * SIDE]
            inside[l] = held
            closing[n] = plus(closing[n], halves(both[2 * SIDE:]))
            masked.append(stack(held * mask_of(l)))
        for (n, l), side in zip(of(gs), masked):
            opening[n] = plus(opening[n], halves(dot(weights[l, pl.ds(2 * SIDE + 16, 16), :], side)))
        return [tiles(value) for value in closing], [tiles(value) for value in opening]

    def seconds(gs, starts, lasts, weights, answers, mask_of):
        ahead = [three(jnp.concatenate(tile, 1)) for tile in starts]
        behind = [three(jnp.concatenate(tile, 1)) for tile in lasts]
        sides = []
        for n, l in of(gs):
            field = (inside[l] + dot(answers[l], ahead[n])) * mask_of(l)
            high, low = split(field)
            sides.append(jnp.concatenate([high, low, high, behind[n]], 0))
        return [dot(weights[l], side) * mask_of(l) for (n, l), side in zip(of(gs), sides)]

    def halves(both):
        return both[:8] + both[8:16]

    def tiles(wide):
        return [wide[:, t * 128:(t + 1) * 128] for t in range(wide.shape[1] // 128)]

    def plus(total, piece):
        return piece if total is None else total + piece

    def folded(mix):
        def one(m0, m1, m2, m3):
            both = jnp.where(place < 2, m0, jnp.where(place == 2, pltpu.roll(m2, 2, 0), pltpu.roll(m2, 1, 0)))
            return both, jnp.where(place < 3, m1, m3), jnp.where(row < 2, m3, pltpu.roll(m3, 6, 0))

        found = [one(*each_tile) for each_tile in zip(*[tiles(part) for part in mix])]
        return [jnp.concatenate(part, 1) for part in zip(*found)]

    def unfolded(t0, t1, t2):
        m0 = jnp.where(place == 2, pltpu.roll(t0, 1, 0), jnp.where(place == 3, pltpu.roll(t0, 3, 0), t0))
        m1 = jnp.where(place == 3, pltpu.roll(t1, 2, 0), t1)
        m2 = jnp.where(place == 0, pltpu.roll(t0, 6, 0), jnp.where(place < 3, pltpu.roll(t0, 7, 0), t0))
        m3 = jnp.where(row < 2, t2, jnp.where(row < 6, pltpu.roll(t2, 2, 0), pltpu.roll(t2, 4, 0)))
        return [m0, m1, m2, jnp.where(place == 3, t1, m3)]

    def packed(parts, k):
        t, off = (k * share) // 128, (k * share) % 128
        return jnp.concatenate([slide(part[t], -off) for part in parts], 0)

    def x_first(gs, rhs, dim, rep):
        closings, openings = firsts(gs, rhs, dim, wx, x_mask)
        for g, closing, opening in zip(gs, closings, openings):
            carry = closing[0]
            chain = [opening[0]]
            ends_x[g, 0] = opening[0]
            for n in range(1, nb):
                turns = turned(carry)
                before[g, n - 1] = carry
                ends_x[g, n] = opening[n]
                chain.append(opening[n] + mixed([block_x[g, j, :, pl.ds(n * 128, 128)] for j in range(4)], turns))
                carry = advance(turns, coef_x, g, 0) + closing[n]
            end = chain[-1]
            for n in range(nb - 2, -1, -1):
                end = advance(turned(end), coef_x, g, 0) + chain[n]
            message = jnp.concatenate([carry, end], 0)
            end_x[rep, g] = message
            got_x[rep, g, gx] = message
        for g in gs:
            for d in range(1, nx):
                x_copy(g, rep, d).start()

    def x_entries(g, rep):
        carry = got_x[rep, g, 0, pl.ds(0, 8)]
        zero = jnp.zeros_like(carry)
        come = zero
        ending = [None] * nx
        for j in range(1, nx):
            turns = turned(carry)
            come = jnp.where(gx == j, carry, come)
            ending[j] = got_x[rep, g, j, pl.ds(8, 8)] + mixed(
                [mix_x[g, j, pl.ds(8 * k, 8)] for k in range(4)], turns
            )
            if j < nx - 1:
                carry = advance(turns, coef_x, g, nb - 1) + got_x[rep, g, j, pl.ds(0, 8)]
        carry = ending[nx - 1]
        leave = jnp.where(gx == nx - 2, carry, zero)
        for j in range(nx - 2, 0, -1):
            carry = advance(turned(carry), coef_x, g, nb - 1) + ending[j]
            leave = jnp.where(gx == j - 1, carry, leave)
        turns = turned(come)
        starts = [come] + [advance(turns, coef_x, g, n - 1) + before[g, n - 1] for n in range(1, nb)]
        lasts = [None] * nb
        lasts[nb - 1] = leave
        for n in range(nb - 1, 0, -1):
            ending_n = ends_x[g, n] + mixed(
                [block_x[g, j, :, pl.ds(n * 128, 128)] for j in range(4)], turned(starts[n])
            )
            lasts[n - 1] = advance(turned(lasts[n]), coef_x, g, 0) + ending_n
        return starts, lasts

    def x_second(gs, rep):
        for g in gs:
            @pl.when(rep == 0)
            def _():
                taken(mix_x.at[g, pl.ds(0, nx - 1)], rmx.at[g])

            taken(got_x.at[rep, g, pl.ds(0, nx - 1)], rx_sem.at[rep, g])
        starts, lasts = zip(*[x_entries(g, rep) for g in gs])
        return seconds(gs, starts, lasts, bx, rx, x_mask)

    def y_first(gs, fields, rep):
        closings, openings = firsts(gs, [across(field) for field in fields], 1, wy, y_mask)
        for g, closing, opening in zip(gs, closings, openings):
            for k in range(owners):
                end_y[rep, g, k] = packed([closing, opening], k)
            got_y[rep, g, gy] = end_y[rep, g, mine]
        for d in range(owners):
            k, other = to_owner(d)

            @pl.when(other)
            def _():
                for g in gs:
                    y_copy(g, rep, k, d).start()

    def y_owner(gs, rep):
        for g in gs:
            @pl.when(rep == 0)
            def _():
                taken(got_m.at[g, pl.ds(0, ny - 1), pl.ds(0, UNIQUE)], rmy.at[g])
                for j in range(1, ny):
                    parts = unfolded(*[got_m[g, j, pl.ds(8 * m, 8)] for m in range(3)])
                    full_y[g, j] = jnp.concatenate(parts, 0)

        for g in gs:
            taken(got_y.at[rep, g, pl.ds(0, ny - 1)], ry_sem.at[rep, g])
        for g in gs:
            starts, ending = [None] * ny, [None] * ny
            carry = got_y[rep, g, 0, pl.ds(0, 8)]
            starts[0] = jnp.zeros_like(carry)
            for j in range(1, ny):
                turns = turned(carry)
                starts[j] = carry
                ending[j] = got_y[rep, g, j, pl.ds(8, 8)] + mixed(
                    [full_y[g, j, pl.ds(8 * m, 8)] for m in range(4)], turns
                )
                if j < ny - 1:
                    carry = advance(turns, coef_y, g, 0) + got_y[rep, g, j, pl.ds(0, 8)]
            last = jnp.zeros_like(carry)
            for j in range(ny - 1, -1, -1):
                back_y[rep, g, j] = jnp.concatenate([starts[j], last], 0)
                if j:
                    last = ending[j] if j == ny - 1 else advance(turned(last), coef_y, g, 0) + ending[j]
            come_y[rep, g, mine] = back_y[rep, g, gy]
        for g in gs:
            for d in range(1, ny):
                b_copy(g, rep, d).start()

    def y_entries(g, rep):
        starts, lasts = [None] * (rows // 128), [None] * (rows // 128)
        for k in range(owners):
            t, off = (k * share) // 128, (k * share) % 128
            start = slide(come_y[rep, g, k, pl.ds(0, 8)], off)
            last = slide(come_y[rep, g, k, pl.ds(8, 8)], off)
            if off == 0:
                starts[t], lasts[t] = start, last
            else:
                starts[t] = jnp.where(lane >= off, start, starts[t])
                lasts[t] = jnp.where(lane >= off, last, lasts[t])
        return starts, lasts

    def y_second(gs, rep):
        for count, role in ((owners - 1, is_owner), (owners, jnp.logical_not(is_owner))):
            @pl.when(role)
            def _():
                for g in gs:
                    taken(come_y.at[rep, g, pl.ds(0, count)], rb.at[rep, g])

        starts, lasts = zip(*[y_entries(g, rep) for g in gs])
        return seconds(gs, starts, lasts, by, ry, y_mask)

    def each(body, team=1):
        def step(s, c):
            body([team * s + n for n in range(team)])
            return c

        lax.fori_loop(0, groups // team, step, 0)

    sources = ((sea_hbm, sea), (inc_hbm, inc), (dev_hbm, dev))

    def incoming(s, n):
        src, dst = sources[n]
        own = pl.ds(s * PAIR * TEAM, PAIR * TEAM)
        return pltpu.make_async_copy(src.at[own], dst.at[own], in_sem.at[n, s])

    few = [
        pltpu.make_async_copy(src, dst, few_sem.at[n])
        for n, (src, dst) in enumerate(((steps_hbm, steps), (rate_x_hbm, rate_x), (rate_y_hbm, rate_y)))
    ]
    for copy in few:
        copy.start()
    for s in range(groups // TEAM):
        for n in range(3):
            incoming(s, n).start()

    lags = (
        lax.broadcasted_iota(jnp.int32, (SIDE, SIDE), 0) - lax.broadcasted_iota(jnp.int32, (SIDE, SIDE), 1)
    ).astype(f32)

    def shape_of(lag):
        span = jnp.maximum(lag, 0.0)
        return span, jnp.where(lag > -0.5, (span + 1.0) * (span + 2.0) * (span + 3.0) / 6.0, 0.0)

    near = (shape_of(lags), shape_of(-lags))

    def tile(shape, rate, weight):
        weight4 = weight * weight * weight * weight
        weight4 = jnp.concatenate([weight4] * (SIDE // 8), 0)
        return split(weight4 * shape[1] * jnp.exp(-rate * shape[0]))

    def by_row(values, i):
        total = jnp.zeros(row.shape, f32)
        for k, value in enumerate(values):
            total = jnp.where(row == k + 4 * i, value, total)
        return total

    def powers(weight):
        return [jnp.ones_like(weight), weight, weight * weight, weight * weight * weight]

    def final_of(i, places, rate, weight):
        pw, leave = powers(weight), binomials(places + 1.0)
        return by_row([weight * pw[k] * leave[k] for k in range(4)], i) * jnp.exp(-rate * places)

    def answer_of(i, places, rate, weight):
        pw, ahead = powers(weight), places + 1.0
        come = binomials(ahead)
        return by_row([pw[3 - k] * come[3 - k] for k in range(4)], i) * jnp.exp(-rate * ahead)

    def high_low(value):
        high = value.astype(bf16).astype(f32)
        return high, value - high

    def finals(i, back, rate, weight):
        over = lane.astype(f32)
        high, low = high_low(final_of(i, over if back else SIDE - 1.0 - over, rate, weight))
        return jnp.concatenate([high, low], 0).astype(bf16)

    def answers(i, back, rate, weight):
        over = lane.astype(f32)
        high, low = high_low(answer_of(i, SIDE - 1.0 - over if back else over, rate, weight))
        return [high, high, low, jnp.zeros_like(high)]

    def filters(first, second, reply, g, rates, weights):
        zero = jnp.zeros((SIDE, SIDE), bf16)
        lower, upper = pl.ds(0, SIDE), pl.ds(SIDE, SIDE)
        replies = []
        for i in range(PAIR):
            l = PAIR * g + i
            rate, weight = rates[i], weights[i]
            high, low = tile(near[0], rate, weight)
            first[l, lower, lower] = high
            first[l, lower, upper] = high
            first[l, upper, lower] = low
            first[l, upper, upper] = zero
            high, low = tile(near[1], rate, weight)
            second[l, :, lower] = high
            second[l, :, upper] = high
            second[l, :, pl.ds(2 * SIDE, SIDE)] = low
            for back in (0, 1):
                final = finals(i, back, rate, weight)
                first[l, pl.ds(2 * SIDE + 16 * back, 16), lower] = final
                first[l, pl.ds(2 * SIDE + 16 * back, 16), upper] = final
                replies += answers(i, back, rate, weight)
        turn = jnp.concatenate(replies, 0).T
        for i in range(PAIR):
            l = PAIR * g + i
            for back in (0, 1):
                part = slide(turn, -32 * (2 * i + back))[:, :32].astype(bf16)
                if back:
                    second[l, :, pl.ds(3 * SIDE, 32)] = part
                else:
                    reply[l] = part

    def products(i, places, rate, weight):
        final = final_of(i, places, rate, weight)
        turns = turned(answer_of(i, places, rate, weight))
        parts = []
        for j in range(4):
            turn = turns[0] if j == 0 else jnp.where(place >= j, turns[j], pltpu.roll(turns[0], j + 4, 0))
            parts += list(high_low(final * turn))
        return jnp.concatenate(parts, 0).astype(bf16)

    def coefs(coef, g, spans, rates, weights):
        low = row < 4
        rate = jnp.where(low, rates[0], rates[1])
        weight = jnp.where(low, weights[0], weights[1])
        power = (jnp.ones_like(weight), weight, weight * weight, weight * weight * weight)
        for n, span in enumerate(spans):
            fall = jnp.exp(-rate * span)
            count = (1.0, span, span * (span + 1.0) / 2.0, span * (span + 1.0) * (span + 2.0) / 6.0)
            for j in range(4):
                coef[g, 4 * n + j] = jnp.where(place >= j, fall * (power[j] * count[j]), 0.0)

    def build_x(g):
        two = [PAIR * g + i for i in range(PAIR)]
        rates = [rate_x[l] for l in two]
        weights = [section_gain(rate_x[l], steps[l]) for l in two]
        filters(wx, bx, rx, g, rates, weights)
        for i, l in enumerate(two):
            for b in range(nb):
                places = lane.astype(f32) + float(b * SIDE)
                tx[l, :, pl.ds(b * SIDE, SIDE)] = products(i, places, rates[i], weights[i])
        spans = [float(SIDE * n) for n in range(1, nb)] + [float(rows)]
        coefs(coef_x, g, spans, rates, weights)

    def build_y(g):
        two = [PAIR * g + i for i in range(PAIR)]
        rates = [rate_y[l] for l in two]
        weights = [section_gain(rate_y[l], steps[l]) for l in two]
        filters(wy, by, ry, g, rates, weights)
        for i, l in enumerate(two):
            ty[l, pl.ds(0, SIDE)] = jnp.where(lags == 0.0, 1.0, 0.0).astype(bf16)
            ty[l, pl.ds(SIDE, 64)] = products(i, lane.astype(f32), rates[i], weights[i])
        coefs(coef_y, g, [float(cols)], rates, weights)

    barrier = pltpu.get_barrier_semaphore()
    for d in range(1, nx):
        pl.semaphore_signal(barrier, inc=1, device_id=x_peer(d), device_id_type=MESH)
    for d in range(1, ny):
        pl.semaphore_signal(barrier, inc=1, device_id=y_peer(d), device_id_type=MESH)

    for copy in few:
        copy.wait()
    each(lambda gs: [build_x(g) for g in gs], 2)

    def four(wide):
        return [halves(wide[16 * j:16 * j + 16]) for j in range(4)]

    def begin_x(gs):
        device, block = [None] * len(gs), [None] * len(gs)
        incoming(gs[0] // TEAM, 0).wait()
        for n, l in of(gs):
            mask = sea[l].astype(f32)
            wet[l] = mask
            mask = mask.astype(bf16)
            device[n] = plus(device[n], dot(tx[l], mask))
            block[n] = plus(block[n], dot(tx[l, :, pl.ds(0, SIDE)], blocks(mask)))
        for n, g in enumerate(gs):
            mix_x[g, gx] = jnp.concatenate(four(device[n]), 0)
            for j, part in enumerate(four(block[n])):
                block_x[g, j] = part

        @pl.when(gs[0] == 0)
        def _():
            pl.semaphore_wait(barrier, nx + ny - 2)

        for g in gs:
            for d in range(1, nx):
                mx_copy(g, d).start()
        for m in (1, 2):
            incoming(gs[0] // TEAM, m).wait()
        x_first(gs, [stack(blocks(dev[l] * wet[l] * inc[l])) for n, l in of(gs)], 0, 0)

    def begin_y(gs):
        for g in gs:
            build_y(g)
        mixes = [None] * len(gs)
        for n, l in of(gs):
            both = dot(ty[l], wet[l].astype(bf16), 1, 1)
            wet_t[l] = both[:SIDE]
            mixes[n] = plus(mixes[n], both[SIDE:])
        for n, g in enumerate(gs):
            parts = [tiles(part) for part in folded(four(mixes[n]))]
            for k in range(owners):
                mix_y[g, k] = packed(parts, k)
            got_m[g, gy] = mix_y[g, mine]
        for d in range(owners):
            k, other = to_owner(d)

            @pl.when(other)
            def _():
                for g in gs:
                    my_copy(g, k, d).start()

    def begin(gs):
        begin_x(gs)
        begin_y(gs)

    each(begin, TEAM)

    def repetition(rep, c):
        each(lambda gs: y_first(gs, x_second(gs, rep), rep), 1)
        @pl.when(is_owner)
        def _():
            each(lambda gs: y_owner(gs, rep), 1)


        @pl.when(rep < MAXSTEPS - 1)
        def _():
            def more(gs):
                fields = y_second(gs, rep)
                for (n, l), field in zip(of(gs), fields):
                    kept[l] = field
                x_first(gs, [across(field) for field in fields], 1, rep + 1)

            each(more, 1)

        @pl.when(rep == MAXSTEPS - 1)
        def _():
            def last(gs):
                fields = y_second(gs, rep)
                for (n, l), field in zip(of(gs), fields):
                    field = jnp.where(steps[l] > rep, field, kept[l])
                    for b in range(nb):
                        own = pl.ds(b * SIDE, SIDE)
                        out[l, own] = dev[l, own] * field[:, b * SIDE:(b + 1) * SIDE].T

            each(last, 1)

        return c

    lax.fori_loop(0, MAXSTEPS, repetition, 0)

    for d in range(1, nx):
        taken(mix_x.at[:, 0], smx.at[d - 1])
        for rep in range(MAXSTEPS):
            taken(end_x.at[rep], sx.at[rep, d - 1])
    for d in range(owners):
        k, other = to_owner(d)

        @pl.when(other)
        def _():
            taken(mix_y.at[:, 0, pl.ds(0, UNIQUE)], smy.at[d])
            for rep in range(MAXSTEPS):
                taken(end_y.at[rep, :, 0], sy.at[rep, d])

    @pl.when(is_owner)
    def _():
        for d in range(1, ny):
            for rep in range(MAXSTEPS):
                taken(back_y.at[rep, :, 0], sb.at[rep, d - 1])


def on_device(nx, ny, increment, deviation, land_sea, filter_steps, zonal_rate, meridional_rate):
    levels, rows, cols = increment.shape
    nb = rows // SIDE
    groups = levels // PAIR
    hbm = pl.BlockSpec(memory_space=pltpu.HBM)
    vmem = pl.BlockSpec(memory_space=pltpu.VMEM)
    reps = MAXSTEPS
    dma = pltpu.SemaphoreType.DMA
    return pl.pallas_call(
        functools.partial(kernel, nx, ny, levels, rows, cols),
        out_shape=jax.ShapeDtypeStruct(increment.shape, f32),
        in_specs=[hbm] * 6,
        out_specs=vmem,
        scratch_shapes=[
            pltpu.SMEM((levels,), jnp.int32),
            pltpu.SMEM((levels,), f32),
            pltpu.SMEM((levels,), f32),
            pltpu.VMEM((levels, 2 * SIDE + 32, 2 * SIDE), bf16),
            pltpu.VMEM((levels, SIDE, 3 * SIDE + 32), bf16),
            pltpu.VMEM((levels, SIDE, 32), bf16),
            pltpu.VMEM((levels, 2 * SIDE + 32, 2 * SIDE), bf16),
            pltpu.VMEM((levels, SIDE, 3 * SIDE + 32), bf16),
            pltpu.VMEM((levels, SIDE, 32), bf16),
            pltpu.VMEM((levels, 64, rows), bf16),
            pltpu.VMEM((levels, SIDE + 64, cols), bf16),
            pltpu.VMEM((groups, 4 * nb, 8, 128), f32),
            pltpu.VMEM((groups, 4, 8, 128), f32),
            pltpu.VMEM((levels, SIDE, nb * cols), f32),
            pltpu.VMEM((groups, nb - 1, 8, cols), f32),
            pltpu.VMEM((groups, nb, 8, cols), f32),
            pltpu.VMEM((groups, 4, 8, nb * cols), f32),
            pltpu.VMEM((groups, nx, 32, cols), f32),
            pltpu.VMEM((groups, ny // 2, 24, 128), f32),
            pltpu.VMEM((groups, ny, 24, 128), f32),
            pltpu.VMEM((groups, ny, 32, 128), f32),
            pltpu.VMEM((reps, groups, 16, cols), f32),
            pltpu.VMEM((reps, groups, nx, 16, cols), f32),
            pltpu.VMEM((reps, groups, ny // 2, 16, 128), f32),
            pltpu.VMEM((reps, groups, ny, 16, 128), f32),
            pltpu.VMEM((reps, groups, ny, 16, 128), f32),
            pltpu.VMEM((reps, groups, ny // 2, 16, 128), f32),
            pltpu.VMEM((levels, rows, cols), f32),
            pltpu.VMEM((levels, rows, cols), f32),
            pltpu.VMEM((levels, rows, cols), jnp.int32),
            pltpu.VMEM((levels, rows, cols), f32),
            pltpu.VMEM((levels, cols, rows), f32),
            pltpu.VMEM((levels, cols, rows), f32),
            dma((nx - 1,)),
            dma((groups,)),
            dma((ny // 2,)),
            dma((groups,)),
            dma((reps, nx - 1)),
            dma((reps, groups)),
            dma((reps, ny // 2)),
            dma((reps, groups)),
            dma((reps, ny - 1)),
            dma((reps, groups)),
            dma((3, groups // TEAM)),
            dma((3,)),
        ],
        compiler_params=pltpu.CompilerParams(
            collective_id=0, has_side_effects=True, vmem_limit_bytes=40 * 1024 * 1024
        ),
    )(
        *(
            pltpu.with_memory_space_constraint(a, pltpu.HBM)
            for a in (filter_steps, zonal_rate, meridional_rate, increment, deviation, land_sea)
        )
    )


def solution(mesh):
    placed = (P(None, "gx", "gy"), P(None, "gx", "gy"), P(None, "gx", "gy"), P(), P(), P())
    body = functools.partial(on_device, mesh.shape["gx"], mesh.shape["gy"])
    return jax.shard_map(
        body, mesh=mesh, in_specs=placed, out_specs=P(None, "gx", "gy"), check_vma=False
    )
```

```python
import functools

import jax
import jax.numpy as jnp
from jax import lax
from jax.experimental import pallas as pl
from jax.experimental.pallas import tpu as pltpu
from jax.sharding import PartitionSpec as P

SIDE = 128
PAIR = 2
TEAM = 2
UNIQUE = 20
MAXSTEPS = 2
gain_base = 3.0**0.125
MESH = pl.DeviceIdType.MESH
f32, bf16 = jnp.float32, jnp.bfloat16


def section_gain(decay_rate, filter_steps):
    rate = jnp.full((8, 128), decay_rate)
    count = jnp.full((8, 128), filter_steps.astype(f32))
    series = jnp.ones_like(rate)
    for n in range(9, 1, -1):
        series = 1.0 - series * rate * (1.0 / n)
    fading = jnp.where(rate < 0.5, rate * series, 1.0 - jnp.exp(-rate))
    return gain_base * jnp.exp((1.0 - 1.0 / (16.0 * count)) * jnp.log(fading))


def binomials(count):
    return (
        jnp.ones_like(count),
        count,
        count * (count + 1.0) / 2.0,
        count * (count + 1.0) * (count + 2.0) / 6.0,
    )


def split(value):
    high = value.astype(bf16)
    return high, (value - high.astype(f32)).astype(bf16)


def three(state):
    high = state.astype(bf16).astype(f32)
    return jnp.concatenate([high, state - high, high, jnp.zeros_like(high)], 0).astype(bf16)


def dot(a, b, ca=1, cb=0):
    return lax.dot_general(a, b, (((ca,), (cb,)), ((), ())), preferred_element_type=f32)


def kernel(
    nx, ny, levels, rows, cols,
    steps_hbm, rate_x_hbm, rate_y_hbm,
    inc_hbm, dev_hbm, sea_hbm,
    out,
    steps, rate_x, rate_y,
    wx, bx, rx, wy, by, ry, tx, ty, coef_x, coef_y,
    inside, before, ends_x, block_x, mix_x, mix_y, got_m, full_y,
    end_x, got_x, end_y, got_y, back_y, come_y, inc, dev, sea, wet, wet_t, kept,
    smx, rmx, smy, rmy, sx, rx_sem, sy, ry_sem, sb, rb, in_sem, few_sem,
):
    gx, gy = lax.axis_index("gx"), lax.axis_index("gy")
    nb = rows // SIDE
    groups = levels // PAIR
    owners = ny // 2
    least = ny // 4
    share = rows // owners
    mine = jnp.clip(gy - least, 0, owners - 1)
    is_owner = (gy >= least) & (gy < least + owners)
    row = lax.broadcasted_iota(jnp.int32, (8, 128), 0)
    lane = lax.broadcasted_iota(jnp.int32, (8, 128), 1)
    place = jnp.where(row < 4, row, row - 4)

    def turned(state):
        return [state] + [pltpu.roll(state, j, 0) for j in range(1, 4)]

    def advance(turns, coef, g, index):
        total = None
        for j in range(4):
            term = coef[g, 4 * index + j] * turns[j]
            total = term if total is None else total + term
        return total

    def mixed(mix, turns):
        total = mix[0] * turns[0]
        for j in range(1, 4):
            total += mix[j] * jnp.where(place >= j, turns[j], pltpu.roll(turns[0], j + 4, 0))
        return total

    def slide(tile, count):
        count = count % 128
        return pltpu.roll(tile, count, 1) if count else tile

    def x_peer(d):
        return (lax.rem(gx + d, nx), gy)

    def y_peer(d):
        return (gx, lax.rem(gy + d, ny))

    def mx_copy(g, d):
        return pltpu.make_async_remote_copy(
            src_ref=mix_x.at[g, gx], dst_ref=mix_x.at[g, gx],
            send_sem=smx.at[d - 1], recv_sem=rmx.at[g],
            device_id=x_peer(d), device_id_type=MESH,
        )

    def to_owner(d):
        k = jnp.where(gy < ny // 2, owners - 1 - d, d)
        return k, least + k != gy

    def my_copy(g, k, d):
        return pltpu.make_async_remote_copy(
            src_ref=mix_y.at[g, k, pl.ds(0, UNIQUE)], dst_ref=got_m.at[g, gy, pl.ds(0, UNIQUE)],
            send_sem=smy.at[d], recv_sem=rmy.at[g],
            device_id=(gx, least + k), device_id_type=MESH,
        )

    def x_copy(g, rep, d):
        return pltpu.make_async_remote_copy(
            src_ref=end_x.at[rep, g], dst_ref=got_x.at[rep, g, gx],
            send_sem=sx.at[rep, d - 1], recv_sem=rx_sem.at[rep, g],
            device_id=x_peer(d), device_id_type=MESH,
        )

    def y_copy(g, rep, k, d):
        return pltpu.make_async_remote_copy(
            src_ref=end_y.at[rep, g, k], dst_ref=got_y.at[rep, g, gy],
            send_sem=sy.at[rep, d], recv_sem=ry_sem.at[rep, g],
            device_id=(gx, least + k), device_id_type=MESH,
        )

    def b_copy(g, rep, d):
        far = ny - d - (d >= ny - gy).astype(jnp.int32)
        near = d - 1 + (d > gy).astype(jnp.int32)
        target = jnp.where(gy < ny // 2, far, near)
        return pltpu.make_async_remote_copy(
            src_ref=back_y.at[rep, g, target], dst_ref=come_y.at[rep, g, mine],
            send_sem=sb.at[rep, d - 1], recv_sem=rb.at[rep, g],
            device_id=(gx, target), device_id_type=MESH,
        )

    def taken(ref, sem):
        pltpu.make_async_copy(ref, ref, sem).wait()

    def blocks(value):
        return jnp.concatenate([value[b * SIDE:(b + 1) * SIDE] for b in range(nb)], 1)

    def unblock(wide):
        return jnp.concatenate([wide[:, b * cols:(b + 1) * cols] for b in range(nb)], 0)

    def stack(value):
        return jnp.concatenate(split(value), 0)

    def across(wide):
        high, low = split(wide)
        return jnp.concatenate([unblock(high), unblock(low)], 1)

    def of(gs):
        return [(n, PAIR * g + i) for n, g in enumerate(gs) for i in range(PAIR)]

    def x_mask(l):
        return blocks(wet[l])

    def y_mask(l):
        return wet_t[l]

    def firsts(gs, rhs, dim, weights, mask_of):
        closing, opening = [None] * len(gs), [None] * len(gs)
        masked = []
        wides = [dot(weights[l, pl.ds(0, 2 * SIDE + 16), :], side, 1, dim) for (n, l), side in zip(of(gs), rhs)]
        for (n, l), both in zip(of(gs), wides):
            held = both[:SIDE] + both[SIDE:2 * SIDE]
            inside[l] = held
            closing[n] = plus(closing[n], halves(both[2 * SIDE:]))
            masked.append(stack(held * mask_of(l)))
        for (n, l), side in zip(of(gs), masked):
            opening[n] = plus(opening[n], halves(dot(weights[l, pl.ds(2 * SIDE + 16, 16), :], side)))
        return [tiles(value) for value in closing], [tiles(value) for value in opening]

    def seconds(gs, starts, lasts, weights, answers, mask_of):
        ahead = [three(jnp.concatenate(tile, 1)) for tile in starts]
        behind = [three(jnp.concatenate(tile, 1)) for tile in lasts]
        sides = []
        for n, l in of(gs):
            field = (inside[l] + dot(answers[l], ahead[n])) * mask_of(l)
            high, low = split(field)
            sides.append(jnp.concatenate([high, low, high, behind[n]], 0))
        return [dot(weights[l], side) * mask_of(l) for (n, l), side in zip(of(gs), sides)]

    def halves(both):
        return both[:8] + both[8:16]

    def tiles(wide):
        return [wide[:, t * 128:(t + 1) * 128] for t in range(wide.shape[1] // 128)]

    def plus(total, piece):
        return piece if total is None else total + piece

    def folded(mix):
        def one(m0, m1, m2, m3):
            both = jnp.where(place < 2, m0, jnp.where(place == 2, pltpu.roll(m2, 2, 0), pltpu.roll(m2, 1, 0)))
            return both, jnp.where(place < 3, m1, m3), jnp.where(row < 2, m3, pltpu.roll(m3, 6, 0))

        found = [one(*each_tile) for each_tile in zip(*[tiles(part) for part in mix])]
        return [jnp.concatenate(part, 1) for part in zip(*found)]

    def unfolded(t0, t1, t2):
        m0 = jnp.where(place == 2, pltpu.roll(t0, 1, 0), jnp.where(place == 3, pltpu.roll(t0, 3, 0), t0))
        m1 = jnp.where(place == 3, pltpu.roll(t1, 2, 0), t1)
        m2 = jnp.where(place == 0, pltpu.roll(t0, 6, 0), jnp.where(place < 3, pltpu.roll(t0, 7, 0), t0))
        m3 = jnp.where(row < 2, t2, jnp.where(row < 6, pltpu.roll(t2, 2, 0), pltpu.roll(t2, 4, 0)))
        return [m0, m1, m2, jnp.where(place == 3, t1, m3)]

    def packed(parts, k):
        t, off = (k * share) // 128, (k * share) % 128
        return jnp.concatenate([slide(part[t], -off) for part in parts], 0)

    def x_first(gs, rhs, dim, rep):
        closings, openings = firsts(gs, rhs, dim, wx, x_mask)
        for g, closing, opening in zip(gs, closings, openings):
            carry = closing[0]
            chain = [opening[0]]
            ends_x[g, 0] = opening[0]
            for n in range(1, nb):
                turns = turned(carry)
                before[g, n - 1] = carry
                ends_x[g, n] = opening[n]
                chain.append(opening[n] + mixed([block_x[g, j, :, pl.ds(n * 128, 128)] for j in range(4)], turns))
                carry = advance(turns, coef_x, g, 0) + closing[n]
            end = chain[-1]
            for n in range(nb - 2, -1, -1):
                end = advance(turned(end), coef_x, g, 0) + chain[n]
            message = jnp.concatenate([carry, end], 0)
            end_x[rep, g] = message
            got_x[rep, g, gx] = message
        for g in gs:
            for d in range(1, nx):
                x_copy(g, rep, d).start()

    def x_entries(g, rep):
        carry = got_x[rep, g, 0, pl.ds(0, 8)]
        zero = jnp.zeros_like(carry)
        come = zero
        ending = [None] * nx
        for j in range(1, nx):
            turns = turned(carry)
            come = jnp.where(gx == j, carry, come)
            ending[j] = got_x[rep, g, j, pl.ds(8, 8)] + mixed(
                [mix_x[g, j, pl.ds(8 * k, 8)] for k in range(4)], turns
            )
            if j < nx - 1:
                carry = advance(turns, coef_x, g, nb - 1) + got_x[rep, g, j, pl.ds(0, 8)]
        carry = ending[nx - 1]
        leave = jnp.where(gx == nx - 2, carry, zero)
        for j in range(nx - 2, 0, -1):
            carry = advance(turned(carry), coef_x, g, nb - 1) + ending[j]
            leave = jnp.where(gx == j - 1, carry, leave)
        turns = turned(come)
        starts = [come] + [advance(turns, coef_x, g, n - 1) + before[g, n - 1] for n in range(1, nb)]
        lasts = [None] * nb
        lasts[nb - 1] = leave
        for n in range(nb - 1, 0, -1):
            ending_n = ends_x[g, n] + mixed(
                [block_x[g, j, :, pl.ds(n * 128, 128)] for j in range(4)], turned(starts[n])
            )
            lasts[n - 1] = advance(turned(lasts[n]), coef_x, g, 0) + ending_n
        return starts, lasts

    def x_second(gs, rep):
        for g in gs:
            @pl.when(rep == 0)
            def _():
                taken(mix_x.at[g, pl.ds(0, nx - 1)], rmx.at[g])

            taken(got_x.at[rep, g, pl.ds(0, nx - 1)], rx_sem.at[rep, g])
        starts, lasts = zip(*[x_entries(g, rep) for g in gs])
        return seconds(gs, starts, lasts, bx, rx, x_mask)

    def y_first(gs, fields, rep):
        closings, openings = firsts(gs, [across(field) for field in fields], 1, wy, y_mask)
        for g, closing, opening in zip(gs, closings, openings):
            for k in range(owners):
                end_y[rep, g, k] = packed([closing, opening], k)
            got_y[rep, g, gy] = end_y[rep, g, mine]
        for d in range(owners):
            k, other = to_owner(d)

            @pl.when(other)
            def _():
                for g in gs:
                    y_copy(g, rep, k, d).start()

    def y_owner(gs, rep):
        for g in gs:
            @pl.when(rep == 0)
            def _():
                taken(got_m.at[g, pl.ds(0, ny - 2), pl.ds(0, UNIQUE)], rmy.at[g])
                for j in range(1, ny):
                    parts = unfolded(*[got_m[g, j, pl.ds(8 * m, 8)] for m in range(3)])
                    full_y[g, j] = jnp.concatenate(parts, 0)

        for g in gs:
            taken(got_y.at[rep, g, pl.ds(0, ny - 1)], ry_sem.at[rep, g])
        for g in gs:
            starts, ending = [None] * ny, [None] * ny
            carry = got_y[rep, g, 0, pl.ds(0, 8)]
            starts[0] = jnp.zeros_like(carry)
            for j in range(1, ny):
                turns = turned(carry)
                starts[j] = carry
                ending[j] = got_y[rep, g, j, pl.ds(8, 8)] + mixed(
                    [full_y[g, j, pl.ds(8 * m, 8)] for m in range(4)], turns
                )
                if j < ny - 1:
                    carry = advance(turns, coef_y, g, 0) + got_y[rep, g, j, pl.ds(0, 8)]
            last = jnp.zeros_like(carry)
            for j in range(ny - 1, -1, -1):
                back_y[rep, g, j] = jnp.concatenate([starts[j], last], 0)
                if j:
                    last = ending[j] if j == ny - 1 else advance(turned(last), coef_y, g, 0) + ending[j]
            come_y[rep, g, mine] = back_y[rep, g, gy]
        for g in gs:
            for d in range(1, ny):
                b_copy(g, rep, d).start()

    def y_entries(g, rep):
        starts, lasts = [None] * (rows // 128), [None] * (rows // 128)
        for k in range(owners):
            t, off = (k * share) // 128, (k * share) % 128
            start = slide(come_y[rep, g, k, pl.ds(0, 8)], off)
            last = slide(come_y[rep, g, k, pl.ds(8, 8)], off)
            if off == 0:
                starts[t], lasts[t] = start, last
            else:
                starts[t] = jnp.where(lane >= off, start, starts[t])
                lasts[t] = jnp.where(lane >= off, last, lasts[t])
        return starts, lasts

    def y_second(gs, rep):
        for count, role in ((owners - 1, is_owner), (owners, jnp.logical_not(is_owner))):
            @pl.when(role)
            def _():
                for g in gs:
                    taken(come_y.at[rep, g, pl.ds(0, count)], rb.at[rep, g])

        starts, lasts = zip(*[y_entries(g, rep) for g in gs])
        return seconds(gs, starts, lasts, by, ry, y_mask)

    def each(body, team=1):
        def step(s, c):
            body([team * s + n for n in range(team)])
            return c

        lax.fori_loop(0, groups // team, step, 0)

    sources = ((sea_hbm, sea), (inc_hbm, inc), (dev_hbm, dev))

    def incoming(s, n):
        src, dst = sources[n]
        own = pl.ds(s * PAIR * TEAM, PAIR * TEAM)
        return pltpu.make_async_copy(src.at[own], dst.at[own], in_sem.at[n, s])

    few = [
        pltpu.make_async_copy(src, dst, few_sem.at[n])
        for n, (src, dst) in enumerate(((steps_hbm, steps), (rate_x_hbm, rate_x), (rate_y_hbm, rate_y)))
    ]
    for copy in few:
        copy.start()
    for s in range(groups // TEAM):
        for n in range(3):
            incoming(s, n).start()

    lags = (
        lax.broadcasted_iota(jnp.int32, (SIDE, SIDE), 0) - lax.broadcasted_iota(jnp.int32, (SIDE, SIDE), 1)
    ).astype(f32)

    def shape_of(lag):
        span = jnp.maximum(lag, 0.0)
        return span, jnp.where(lag > -0.5, (span + 1.0) * (span + 2.0) * (span + 3.0) / 6.0, 0.0)

    near = (shape_of(lags), shape_of(-lags))

    def tile(shape, rate, weight):
        weight4 = weight * weight * weight * weight
        weight4 = jnp.concatenate([weight4] * (SIDE // 8), 0)
        return split(weight4 * shape[1] * jnp.exp(-rate * shape[0]))

    def by_row(values, i):
        total = jnp.zeros(row.shape, f32)
        for k, value in enumerate(values):
            total = jnp.where(row == k + 4 * i, value, total)
        return total

    def powers(weight):
        return [jnp.ones_like(weight), weight, weight * weight, weight * weight * weight]

    def final_of(i, places, rate, weight):
        pw, leave = powers(weight), binomials(places + 1.0)
        return by_row([weight * pw[k] * leave[k] for k in range(4)], i) * jnp.exp(-rate * places)

    def answer_of(i, places, rate, weight):
        pw, ahead = powers(weight), places + 1.0
        come = binomials(ahead)
        return by_row([pw[3 - k] * come[3 - k] for k in range(4)], i) * jnp.exp(-rate * ahead)

    def high_low(value):
        high = value.astype(bf16).astype(f32)
        return high, value - high

    def finals(i, back, rate, weight):
        over = lane.astype(f32)
        high, low = high_low(final_of(i, over if back else SIDE - 1.0 - over, rate, weight))
        return jnp.concatenate([high, low], 0).astype(bf16)

    def answers(i, back, rate, weight):
        over = lane.astype(f32)
        high, low = high_low(answer_of(i, SIDE - 1.0 - over if back else over, rate, weight))
        return [high, high, low, jnp.zeros_like(high)]

    def filters(first, second, reply, g, rates, weights):
        zero = jnp.zeros((SIDE, SIDE), bf16)
        lower, upper = pl.ds(0, SIDE), pl.ds(SIDE, SIDE)
        replies = []
        for i in range(PAIR):
            l = PAIR * g + i
            rate, weight = rates[i], weights[i]
            high, low = tile(near[0], rate, weight)
            first[l, lower, lower] = high
            first[l, lower, upper] = high
            first[l, upper, lower] = low
            first[l, upper, upper] = zero
            high, low = tile(near[1], rate, weight)
            second[l, :, lower] = high
            second[l, :, upper] = high
            second[l, :, pl.ds(2 * SIDE, SIDE)] = low
            for back in (0, 1):
                final = finals(i, back, rate, weight)
                first[l, pl.ds(2 * SIDE + 16 * back, 16), lower] = final
                first[l, pl.ds(2 * SIDE + 16 * back, 16), upper] = final
                replies += answers(i, back, rate, weight)
        turn = jnp.concatenate(replies, 0).T
        for i in range(PAIR):
            l = PAIR * g + i
            for back in (0, 1):
                part = slide(turn, -32 * (2 * i + back))[:, :32].astype(bf16)
                if back:
                    second[l, :, pl.ds(3 * SIDE, 32)] = part
                else:
                    reply[l] = part

    def products(i, places, rate, weight):
        final = final_of(i, places, rate, weight)
        turns = turned(answer_of(i, places, rate, weight))
        parts = []
        for j in range(4):
            turn = turns[0] if j == 0 else jnp.where(place >= j, turns[j], pltpu.roll(turns[0], j + 4, 0))
            parts += list(high_low(final * turn))
        return jnp.concatenate(parts, 0).astype(bf16)

    def coefs(coef, g, spans, rates, weights):
        low = row < 4
        rate = jnp.where(low, rates[0], rates[1])
        weight = jnp.where(low, weights[0], weights[1])
        power = (jnp.ones_like(weight), weight, weight * weight, weight * weight * weight)
        for n, span in enumerate(spans):
            fall = jnp.exp(-rate * span)
            count = (1.0, span, span * (span + 1.0) / 2.0, span * (span + 1.0) * (span + 2.0) / 6.0)
            for j in range(4):
                coef[g, 4 * n + j] = jnp.where(place >= j, fall * (power[j] * count[j]), 0.0)

    def build_x(g):
        two = [PAIR * g + i for i in range(PAIR)]
        rates = [rate_x[l] for l in two]
        weights = [section_gain(rate_x[l], steps[l]) for l in two]
        filters(wx, bx, rx, g, rates, weights)
        for i, l in enumerate(two):
            for b in range(nb):
                places = lane.astype(f32) + float(b * SIDE)
                tx[l, :, pl.ds(b * SIDE, SIDE)] = products(i, places, rates[i], weights[i])
        spans = [float(SIDE * n) for n in range(1, nb)] + [float(rows)]
        coefs(coef_x, g, spans, rates, weights)

    def build_y(g):
        two = [PAIR * g + i for i in range(PAIR)]
        rates = [rate_y[l] for l in two]
        weights = [section_gain(rate_y[l], steps[l]) for l in two]
        filters(wy, by, ry, g, rates, weights)
        for i, l in enumerate(two):
            ty[l, pl.ds(0, SIDE)] = jnp.where(lags == 0.0, 1.0, 0.0).astype(bf16)
            ty[l, pl.ds(SIDE, 64)] = products(i, lane.astype(f32), rates[i], weights[i])
        coefs(coef_y, g, [float(cols)], rates, weights)

    barrier = pltpu.get_barrier_semaphore()
    for d in range(1, nx):
        pl.semaphore_signal(barrier, inc=1, device_id=x_peer(d), device_id_type=MESH)
    for d in range(1, ny):
        pl.semaphore_signal(barrier, inc=1, device_id=y_peer(d), device_id_type=MESH)

    for copy in few:
        copy.wait()
    each(lambda gs: [build_x(g) for g in gs], 2)

    def four(wide):
        return [halves(wide[16 * j:16 * j + 16]) for j in range(4)]

    def begin_x(gs):
        device, block = [None] * len(gs), [None] * len(gs)
        incoming(gs[0] // TEAM, 0).wait()
        for n, l in of(gs):
            mask = sea[l].astype(f32)
            wet[l] = mask
            mask = mask.astype(bf16)
            device[n] = plus(device[n], dot(tx[l], mask))
            block[n] = plus(block[n], dot(tx[l, :, pl.ds(0, SIDE)], blocks(mask)))
        for n, g in enumerate(gs):
            mix_x[g, gx] = jnp.concatenate(four(device[n]), 0)
            for j, part in enumerate(four(block[n])):
                block_x[g, j] = part

        @pl.when(gs[0] == 0)
        def _():
            pl.semaphore_wait(barrier, nx + ny - 2)

        for g in gs:
            for d in range(1, nx):
                mx_copy(g, d).start()
        for m in (1, 2):
            incoming(gs[0] // TEAM, m).wait()
        x_first(gs, [stack(blocks(dev[l] * wet[l] * inc[l])) for n, l in of(gs)], 0, 0)

    def begin_y(gs):
        for g in gs:
            build_y(g)
        mixes = [None] * len(gs)
        for n, l in of(gs):
            both = dot(ty[l], wet[l].astype(bf16), 1, 1)
            wet_t[l] = both[:SIDE]
            mixes[n] = plus(mixes[n], both[SIDE:])
        for n, g in enumerate(gs):
            parts = [tiles(part) for part in folded(four(mixes[n]))]
            for k in range(owners):
                mix_y[g, k] = packed(parts, k)
            got_m[g, gy] = mix_y[g, mine]
        for d in range(owners):
            k, other = to_owner(d)

            @pl.when(other & (gy > 0))
            def _():
                for g in gs:
                    my_copy(g, k, d).start()

    def begin(gs):
        begin_x(gs)
        begin_y(gs)

    each(begin, TEAM)

    def repetition(rep, c):
        each(lambda gs: y_first(gs, x_second(gs, rep), rep), 1)
        @pl.when(is_owner)
        def _():
            each(lambda gs: y_owner(gs, rep), 1)


        @pl.when(rep < MAXSTEPS - 1)
        def _():
            def more(gs):
                fields = y_second(gs, rep)
                for (n, l), field in zip(of(gs), fields):
                    kept[l] = field
                x_first(gs, [across(field) for field in fields], 1, rep + 1)

            each(more, 1)

        @pl.when(rep == MAXSTEPS - 1)
        def _():
            def last(gs):
                fields = y_second(gs, rep)
                for (n, l), field in zip(of(gs), fields):
                    field = jnp.where(steps[l] > rep, field, kept[l])
                    for b in range(nb):
                        own = pl.ds(b * SIDE, SIDE)
                        out[l, own] = dev[l, own] * field[:, b * SIDE:(b + 1) * SIDE].T

            each(last, 1)

        return c

    lax.fori_loop(0, MAXSTEPS, repetition, 0)

    for d in range(1, nx):
        taken(mix_x.at[:, 0], smx.at[d - 1])
        for rep in range(MAXSTEPS):
            taken(end_x.at[rep], sx.at[rep, d - 1])
    for d in range(owners):
        k, other = to_owner(d)

        @pl.when(other)
        def _():
            @pl.when(gy > 0)
            def _():
                taken(mix_y.at[:, 0, pl.ds(0, UNIQUE)], smy.at[d])

            for rep in range(MAXSTEPS):
                taken(end_y.at[rep, :, 0], sy.at[rep, d])

    @pl.when(is_owner)
    def _():
        for d in range(1, ny):
            for rep in range(MAXSTEPS):
                taken(back_y.at[rep, :, 0], sb.at[rep, d - 1])


def on_device(nx, ny, increment, deviation, land_sea, filter_steps, zonal_rate, meridional_rate):
    levels, rows, cols = increment.shape
    nb = rows // SIDE
    groups = levels // PAIR
    hbm = pl.BlockSpec(memory_space=pltpu.HBM)
    vmem = pl.BlockSpec(memory_space=pltpu.VMEM)
    reps = MAXSTEPS
    dma = pltpu.SemaphoreType.DMA
    return pl.pallas_call(
        functools.partial(kernel, nx, ny, levels, rows, cols),
        out_shape=jax.ShapeDtypeStruct(increment.shape, f32),
        in_specs=[hbm] * 6,
        out_specs=vmem,
        scratch_shapes=[
            pltpu.SMEM((levels,), jnp.int32),
            pltpu.SMEM((levels,), f32),
            pltpu.SMEM((levels,), f32),
            pltpu.VMEM((levels, 2 * SIDE + 32, 2 * SIDE), bf16),
            pltpu.VMEM((levels, SIDE, 3 * SIDE + 32), bf16),
            pltpu.VMEM((levels, SIDE, 32), bf16),
            pltpu.VMEM((levels, 2 * SIDE + 32, 2 * SIDE), bf16),
            pltpu.VMEM((levels, SIDE, 3 * SIDE + 32), bf16),
            pltpu.VMEM((levels, SIDE, 32), bf16),
            pltpu.VMEM((levels, 64, rows), bf16),
            pltpu.VMEM((levels, SIDE + 64, cols), bf16),
            pltpu.VMEM((groups, 4 * nb, 8, 128), f32),
            pltpu.VMEM((groups, 4, 8, 128), f32),
            pltpu.VMEM((levels, SIDE, nb * cols), f32),
            pltpu.VMEM((groups, nb - 1, 8, cols), f32),
            pltpu.VMEM((groups, nb, 8, cols), f32),
            pltpu.VMEM((groups, 4, 8, nb * cols), f32),
            pltpu.VMEM((groups, nx, 32, cols), f32),
            pltpu.VMEM((groups, ny // 2, 24, 128), f32),
            pltpu.VMEM((groups, ny, 24, 128), f32),
            pltpu.VMEM((groups, ny, 32, 128), f32),
            pltpu.VMEM((reps, groups, 16, cols), f32),
            pltpu.VMEM((reps, groups, nx, 16, cols), f32),
            pltpu.VMEM((reps, groups, ny // 2, 16, 128), f32),
            pltpu.VMEM((reps, groups, ny, 16, 128), f32),
            pltpu.VMEM((reps, groups, ny, 16, 128), f32),
            pltpu.VMEM((reps, groups, ny // 2, 16, 128), f32),
            pltpu.VMEM((levels, rows, cols), f32),
            pltpu.VMEM((levels, rows, cols), f32),
            pltpu.VMEM((levels, rows, cols), jnp.int32),
            pltpu.VMEM((levels, rows, cols), f32),
            pltpu.VMEM((levels, cols, rows), f32),
            pltpu.VMEM((levels, cols, rows), f32),
            dma((nx - 1,)),
            dma((groups,)),
            dma((ny // 2,)),
            dma((groups,)),
            dma((reps, nx - 1)),
            dma((reps, groups)),
            dma((reps, ny // 2)),
            dma((reps, groups)),
            dma((reps, ny - 1)),
            dma((reps, groups)),
            dma((3, groups // TEAM)),
            dma((3,)),
        ],
        compiler_params=pltpu.CompilerParams(
            collective_id=0, has_side_effects=True, vmem_limit_bytes=40 * 1024 * 1024
        ),
    )(
        *(
            pltpu.with_memory_space_constraint(a, pltpu.HBM)
            for a in (filter_steps, zonal_rate, meridional_rate, increment, deviation, land_sea)
        )
    )


def solution(mesh):
    placed = (P(None, "gx", "gy"), P(None, "gx", "gy"), P(None, "gx", "gy"), P(), P(), P())
    body = functools.partial(on_device, mesh.shape["gx"], mesh.shape["gy"])
    return jax.shard_map(
        body, mesh=mesh, in_specs=placed, out_specs=P(None, "gx", "gy"), check_vma=False
    )
```
